32 devices in a mesh: lag: 4 (over y, x), row: 8 (over z, core).
Axes of the slice: x: 2, y: 2, z: 4, core: 2. Of those that a mesh axis runs over, the one named last changes fastest.
Arguments:
- lag_weights: float32 [16, 4096, 4096], P('lag', 'row'), may hold values from -0.0234375 to 0.0234375
- inverse_head: float32 [4096, 4096], P('row'), may hold values from -0.09375 to 0.09375
- excitation: float32 [3, 4096, 128], P(None, 'row'), may hold values from -6 to 6
- history: float32 [16, 4096, 128], P('lag', 'row'), may hold values from -6 to 6
Outputs:
- densities: float32 [3, 4096, 128], P(None, 'row')
The draws below stay inside these ranges and needn't reach their ends.
All inputs are finite; a program needn't handle non-finite values.
Results may differ from the reference program's by a relative error of at most 0.0001.
Values sent between devices are 32-bit elements; how exact they have to be, the bound alone decides.
No kernel may reach another device: no remote copies, remote signals or barrier semaphores. Data moves between devices by JAX's collectives and lax.ppermute only.
A program may use at most 128 MiB of HBM per device.

```python
import jax
import jax.numpy as jnp
from jax import lax

M = 4096
EXC = 128
STEPS = 3
LAGS = 16


def block_levels(stream_key, extent, cuts, smallest, largest):
    level = 1.0
    for axis_at, shards_of in cuts:
        draws = jax.random.uniform(jax.random.fold_in(jax.random.fold_in(stream_key, 6), axis_at), (shards_of,), jnp.float32, smallest / len(cuts), largest / len(cuts))
        level = level * jnp.repeat(jnp.exp(draws), extent[axis_at] // shards_of).reshape((-1,) + (1,) * (len(extent) - 1 - axis_at))
    return level


def centred(stream_key, dims, deviation, bound, shards=(), kind=jnp.bfloat16):
    result = jax.random.normal(stream_key, dims, jnp.float32) * deviation
    if len(shards) > 0:
        result = block_levels(stream_key, dims, shards, -0.22, 0.18) * result
    return jnp.clip(result, min=-bound, max=bound).astype(kind)


def setup_inputs(seed: int = 0) -> dict:
    arg_keys = jax.random.split(jax.random.key(seed), 5)
    lag_weights = centred(arg_keys[0], (LAGS, M, M), (M * LAGS) ** -0.5, 0.0234375, ((0, 4), (1, 8)), jnp.float32)
    inverse_head = centred(arg_keys[1], (M, M), M ** -0.5, 0.09375, ((0, 8),), jnp.float32)
    excitation = centred(arg_keys[2], (STEPS, M, EXC), 1.0, 6.0, ((1, 8),), jnp.float32)
    history = centred(arg_keys[3], (LAGS, M, EXC), 1.0, 6.0, ((0, 4), (1, 8)), jnp.float32)
    return {"lag_weights": lag_weights, "inverse_head": inverse_head, "excitation": excitation, "history": history}


def reference(lag_weights, inverse_head, excitation, history):
    past = history
    results = []
    for step in range(STEPS):
        carried = jnp.einsum("kmc,kcr->mr", lag_weights, past, precision=lax.Precision.HIGHEST)
        density = jnp.dot(inverse_head, excitation[step] - carried, precision=lax.Precision.HIGHEST, preferred_element_type=jnp.float32)
        results.append(density)
        past = jnp.concatenate([density[None], past[:-1]], axis=0)
    return jnp.stack(results, axis=0)
```

```python
import jax
import jax.numpy as jnp
from jax import lax
from jax.experimental import pallas as pl
from jax.experimental.pallas import tpu as pltpu
from jax.sharding import PartitionSpec as P


STEPS = 3
HIGHEST = lax.Precision.HIGHEST
F32 = jnp.float32
BF16 = jnp.bfloat16


def split(value):
    high = value.astype(BF16)
    return high, (value - high.astype(F32)).astype(BF16)


def dot(a, b):
    return jnp.dot(a, b, preferred_element_type=F32)


def product(weight, vectors):
    count, width = len(vectors), vectors[0].shape[1]
    wh, wl = split(weight)
    highs, lows = zip(*(split(v) for v in vectors))
    main = dot(wh, jnp.concatenate(highs + lows, axis=1))
    rest = dot(wl, jnp.concatenate(highs, axis=1) if count > 1 else highs[0])
    return main[:, : count * width] + main[:, count * width :] + rest


def halves(core, weights):
    rows = weights.shape[1]
    for side in (core, 1 - core):
        yield weights[0, :, pl.ds(pl.multiple_of(side * rows, rows), rows)]


def chip_kernel(where, weights, near, far, *refs):
    outs, high, low = refs[-STEPS - 2 : -2], *refs[-2:]
    totals = refs[:-STEPS - 2]
    at = pl.program_id(0)
    lags, rows, width = near.shape
    core = where[0]

    @pl.when(at == 0)
    def _():
        for n, out in enumerate(outs):
            out[...] = totals[n][...] if totals else jnp.zeros_like(out)
        for k in range(lags):
            columns = slice((lags - 1 - k) * width, (lags - k) * width)
            for piece, side in ((near, core), (far, 1 - core)):
                here = pl.ds(pl.multiple_of(side * rows, rows), rows)
                high[here, columns], low[here, columns] = split(piece[k])

    for k in range(lags):

        @pl.when(at == k)
        def _():
            size = min(k + 1, STEPS) * width
            columns = slice((lags - 1 - k) * width, (lags - 1 - k) * width + size)
            wh, wl = split(weights[0])
            h = high[:, columns]
            main = dot(wh, jnp.concatenate([h, low[:, columns]], axis=1))
            result = main[:, :size] + main[:, size:] + dot(wl, h)
            for n in range(size // width):
                outs[n][...] += result[:, n * width : (n + 1) * width]


def first_kernel(where, weights, near, far, total, out):
    @pl.when(pl.program_id(0) == 0)
    def _():
        out[...] = total[...]

    for weight, piece in zip(halves(where[0], weights), (near, far)):
        out[...] += product(weight, [piece[0]])


def rest_kernel(where, weights, near, near_before, far, far_before, one, two, one_out, two_out):
    at = pl.program_id(0)
    width = near.shape[-1]

    @pl.when(at == 0)
    def _():
        one_out[...] = one[...]
        two_out[...] = two[...]
        for weight, piece in zip(halves(where[0], weights), (near, far)):
            one_out[...] += product(weight, [piece[0]])

    @pl.when(at > 0)
    def _():
        for weight, piece, before in zip(halves(where[0], weights), (near, far), (near_before, far_before)):
            result = product(weight, [piece[0], before[0]])
            one_out[...] += result[:, :width]
            two_out[...] += result[:, width:]


def entered_kernel(where, weights, *refs):
    pieces, total, out = refs[:-2], refs[-2], refs[-1]
    hop = pl.program_id(0)

    @pl.when(hop == 0)
    def _():
        out[...] = total[...]

    for h in range(len(pieces) // 2):

        @pl.when(jnp.logical_and(where[1] > 0, hop == h))
        def _():
            for weight, piece in zip(halves(where[0], weights), pieces[2 * h : 2 * h + 2]):
                out[...] += product(weight, [piece[0]])


def second_kernel(where, weights, *refs):
    nears, fars, total, out = refs[: len(refs) // 2 - 1], refs[len(refs) // 2 - 1 : -2], refs[-2], refs[-1]

    @pl.when(pl.program_id(0) == 0)
    def _():
        out[...] = total[...]

    @pl.when(where[1] == 0)
    def _():
        for weight, parts in zip(halves(where[0], weights), (nears, fars)):
            out[...] += product(weight, [jnp.concatenate([p[...] for p in parts], axis=0)])


def columns_kernel(where, *refs):
    fold, groups = where.shape[1] - 1, where.shape[2]
    sources, outs = refs[:fold], refs[fold:]
    part = sources[0].shape[2] // groups
    take = lambda j: jnp.concatenate([s[0, :, j * part : (j + 1) * part] for s in sources], axis=1)
    if len(outs) == 1:
        for j in range(groups):

            @pl.when(where[0, fold, 0] == j)
            def _():
                outs[0][...] = take(j)

        return
    for j in range(groups - 1):
        outs[j][...] = take(j)
    for side, out in enumerate(outs[groups - 1 :]):

        @pl.when(pl.program_id(0) == side)
        def _():
            out[...] = take(groups - 1)


def pick_kernel(which, *refs):
    sources, out = refs[:-1], refs[-1]
    groups = len(sources) - 1
    for j, source in enumerate(sources):
        chosen = which[0] == min(j, groups - 1)
        if j >= groups - 1:
            chosen = jnp.logical_and(chosen, pl.program_id(0) == j - groups + 1)

        @pl.when(chosen)
        def _():
            out[...] = source[...]


def call(kernel, where, grid, operands, specs, count, shape, cost, aliases={}, scratch=()):
    return pl.pallas_call(
        kernel,
        out_shape=[jax.ShapeDtypeStruct(shape, F32)] * count,
        grid_spec=pltpu.PrefetchScalarGridSpec(
            num_scalar_prefetch=1, grid=grid, in_specs=specs, out_specs=[all_of(shape)] * count, scratch_shapes=scratch
        ),
        input_output_aliases=aliases,
        cost_estimate=pl.CostEstimate(flops=cost[0], bytes_accessed=cost[1], transcendentals=0),
        compiler_params=pltpu.CompilerParams(dimension_semantics=("arbitrary",) * len(grid)),
    )(where, *operands)


def all_of(shape):
    return pl.BlockSpec(shape, lambda *_: (0,) * len(shape))


def on_device(lag_weights, inverse_head, excitation, history):
    groups, devices = lax.axis_size("lag"), lax.axis_size("row")
    group, at = lax.axis_index("lag"), lax.axis_index("row")
    chips = devices // 2
    chip, core = at // 2, at % 2
    lags, rows, order = lag_weights.shape
    width = history.shape[-1]
    part = rows // groups
    tile = rows * 2 * rows
    square = (rows, width)
    tie = lax.optimization_barrier

    def pairs(axis_size, mask):
        return [(i, i ^ mask) for i in range(axis_size)]

    def other_core(value):
        return lax.ppermute(value, "row", pairs(devices, 1))

    def along(value, step, sources):
        return lax.ppermute(value, "row", [(2 * i + c, 2 * (i + step) + c) for i in sources for c in (0, 1)])

    def go_up(value, hop):
        return along(value, 1, range(hop - 1, chips - 1))

    def go_down(value, hop):
        return along(value, -1, range(1, chips - hop + 1))

    def taken(z, stage):
        both = min(z, chips - 1 - z)
        if stage <= 2 * both:
            return (stage + 1) // 2, stage % 2 == 1
        return stage - both, z >= stage - both

    def by_chip(values):
        result = jnp.int32(values[0])
        for z in range(1, chips):
            result = jnp.where(chip == z, values[z], result)
        return result

    def source_of(stage):
        return by_chip([z + (-h if u else h) for z in range(chips) for h, u in [taken(z, stage)]])

    def choose(stage, ups, downs):
        found = sorted({taken(z, stage) for z in range(chips)})
        arrays = [(ups if u else downs)[h] for h, u in found]
        return lax.select_n(by_chip([found.index(taken(z, stage)) for z in range(chips)]), *arrays) if len(found) > 1 else arrays[0]

    stages = [chip] + [source_of(stage) for stage in range(1, chips)]
    ring = [(chip + chips - h) % chips for h in range(chips)]
    xored = [chip ^ k for k in range(chips)]
    where = jnp.stack([core, group, *stages, *ring, *xored]).astype(jnp.int32)

    def weight_spec(stage, first=0):
        return pl.BlockSpec((1, rows, 2 * rows), lambda k, w: (k + first, 0, w[2 + stage]))

    def lag_spec(shift):
        return pl.BlockSpec((1, rows, width), lambda k, w: (jnp.maximum(k + shift, 0), 0, 0))

    def add_chip(totals, near, far, stage):
        return call(
            chip_kernel, where, (lags,), (lag_weights, near, far, *totals),
            [weight_spec(stage)] + [all_of(v.shape) for v in (near, far, *totals)], STEPS, square,
            (18 * lags * tile * width, 4 * lags * tile), {4 + n: n for n in range(len(totals))},
            [pltpu.VMEM((2 * rows, lags * width), BF16)] * 2,
        )

    def add_first(total, near, far, stage):
        return call(
            first_kernel, where, (lags,), (lag_weights, near, far, total),
            [weight_spec(stage), lag_spec(0), lag_spec(0), all_of(square)], 1, square,
            (6 * lags * tile * width, 4 * lags * tile), {4: 0},
        )[0]

    def add_rest(one, two, near, far, stage):
        return call(
            rest_kernel, where, (lags - 1,), (lag_weights, near, near, far, far, one, two),
            [weight_spec(stage, 1), lag_spec(0), lag_spec(-1), lag_spec(0), lag_spec(-1), all_of(square), all_of(square)],
            2, square, (12 * lags * tile * width, 4 * lags * tile), {6: 0, 7: 1},
        )

    def add_entered(total, both, k, n):
        return call(
            entered_kernel, where, (chips,), (lag_weights, *both, total),
            [pl.BlockSpec((1, rows, 2 * rows), lambda h, w: (k, 0, jnp.where(w[1] > 0, w[2 + chips + h], 0)))]
            + [pl.BlockSpec((1, rows, width), lambda h, w: (STEPS - 1 + k - n, 0, 0))] * len(both) + [all_of(square)],
            1, square, (6 * chips * tile * width, 4 * chips * tile), {len(both) + 2: 0},
        )[0]

    def add_second(total, nears, fars):
        block = pl.BlockSpec((part, width), lambda k, w: (k, 0))
        return call(
            second_kernel, where, (chips,), (lag_weights, *nears, *fars, total),
            [pl.BlockSpec((1, rows, 2 * rows), lambda k, w: (1, 0, jnp.where(w[1] == 0, w[2 + 2 * chips + k], 0)))]
            + [block] * 2 * groups + [all_of(square)],
            1, square, (6 * rows * order * width, 4 * rows * order), {2 + 2 * groups: 0},
        )[0]

    slots = jnp.stack([(chip ^ k) * 2 + (core ^ h) for h in (0, 1) for k in range(chips)]).astype(jnp.int32)
    meet = devices * part

    def columns(matrix, every):
        fold = devices // 2
        numbers = jnp.tile(slots.reshape(2, fold, 1), (1, 1, groups))
        numbers = jnp.concatenate([numbers, jnp.full((2, 1, groups), group, jnp.int32)], axis=1)
        whole = pl.BlockSpec((rows, meet // 2), lambda s, w: (0, s))
        half = pl.BlockSpec((rows, meet // 2), lambda s, w: (0, 0))
        shape = lambda size: jax.ShapeDtypeStruct((rows, size), F32)
        return pl.pallas_call(
            columns_kernel,
            out_shape=[shape(meet)] * (groups - 1) + [shape(meet // 2)] * 2 if every else [shape(meet)],
            grid_spec=pltpu.PrefetchScalarGridSpec(
                num_scalar_prefetch=1,
                grid=(2,),
                in_specs=[pl.BlockSpec((1, rows, rows), lambda s, w, i=i: (0, 0, w[s, i, 0])) for i in range(fold)],
                out_specs=[whole] * (groups - 1) + [half] * 2 if every else [whole],
            ),
            cost_estimate=pl.CostEstimate(flops=0, bytes_accessed=8 * rows * order, transcendentals=0),
            compiler_params=pltpu.CompilerParams(dimension_semantics=("arbitrary",)),
            name="columns",
        )(numbers, *[matrix] * fold)

    def pick(matrices):
        spec = lambda j: pl.BlockSpec((rows, meet // 2), lambda s, w: (0, jnp.where(w[0] == j, s, 0)))
        return pl.pallas_call(
            pick_kernel,
            out_shape=jax.ShapeDtypeStruct((rows, meet), F32),
            grid_spec=pltpu.PrefetchScalarGridSpec(
                num_scalar_prefetch=1,
                grid=(2,),
                in_specs=[spec(j) for j in range(groups - 1)] + [all_of((rows, meet // 2))] * 2,
                out_specs=pl.BlockSpec((rows, meet // 2), lambda s, w: (0, s)),
            ),
            cost_estimate=pl.CostEstimate(flops=0, bytes_accessed=16 * rows * meet, transcendentals=0),
            compiler_params=pltpu.CompilerParams(dimension_semantics=("arbitrary",)),
            name="pick",
        )(group.astype(jnp.int32).reshape(1), *matrices)

    def gather_near(value):
        pieces = [value] + [lax.ppermute(value, "row", pairs(devices, 2 * k)) for k in range(1, chips)]
        return jnp.concatenate(pieces, axis=0)

    def gather_far(mine):
        return jnp.concatenate([mine, other_core(mine)], axis=0)

    def own_part(value):
        return lax.dynamic_slice(value, (group * part, 0), (part, value.shape[1]))

    def sum_parts(value):
        result = own_part(value)
        for mask in range(1, groups):
            sent = lax.dynamic_slice(value, ((group ^ mask) * part, 0), (part, width))
            result = result + lax.ppermute(sent, "lag", pairs(groups, mask))
        return result

    def whole_rows(value):
        pieces = [value] + [lax.ppermute(value, "lag", pairs(groups, mask)) for mask in range(1, groups)]
        return jnp.concatenate([lax.select_n(group ^ i, *pieces) for i in range(groups)], axis=0)

    def multiply(matrix, vector):
        return jnp.dot(matrix, vector, precision=HIGHEST)

    ups, downs = {1: go_up(history, 1)}, {1: go_down(history, 1)}
    entered = lax.ppermute(history[lags - (STEPS - 1) :], "lag", [(i, i + 1) for i in range(groups - 1)])
    far = other_core(history)
    *chunks, last_near, last_far = columns(lag_weights, True)
    relayed = lax.ppermute(last_far, "lag", [(0, groups // 2)])
    sent = [lax.ppermute(chunks[j], "lag", [(0, j)]) for j in range(1, groups - 1)]
    sent.append(lax.ppermute(last_near, "lag", [(0, groups - 1)]))
    totals = add_chip([], history, far, 0)
    ups[1], downs[1], entered, totals = tie((ups[1], downs[1], entered, totals))
    for stage in range(1, chips - 1):
        ups[stage + 1], downs[stage + 1] = go_up(ups[stage], stage + 1), go_down(downs[stage], stage + 1)
        near = choose(stage, ups, downs)
        if stage == chips - 2:
            relayed, near = tie((relayed, near))
            sent.append(lax.ppermute(relayed, "lag", [(groups // 2, groups - 1)]))
        totals = add_chip(totals, near, other_core(near), stage)
        if stage == chips - 2:
            (head_columns,) = columns(inverse_head[None], False)
            totals, head_columns = tie((totals, head_columns))
        ups[stage + 1], downs[stage + 1], totals = tie((ups[stage + 1], downs[stage + 1], totals))
    first, rest_one, rest_two = totals

    entered, ups[chips - 1] = tie((entered, ups[chips - 1]))
    near = choose(chips - 1, ups, downs)
    climbs, falls = {1: go_up(entered, 1)}, {1: go_down(entered, 1)}
    far = other_core(near)
    first = add_first(first, near, far, chips - 1)

    def next_hop(hop, value):
        climbs[hop], falls[hop], value = tie((climbs[hop], falls[hop], value))
        if hop + 1 < chips:
            climbs[hop + 1], falls[hop + 1] = go_up(climbs[hop], hop + 1), go_down(falls[hop], hop + 1)
        return value

    for hop in range(1, chips - 2):
        first = next_hop(hop, first)
    right_side = own_part(excitation[0]) - sum_parts(first)
    right_side, near, far, rest_one, rest_two = tie((right_side, near, far, rest_one, rest_two))
    mine = gather_near(right_side)
    rest_one, rest_two = add_rest(rest_one, rest_two, near, far, chips - 1)
    mine, rest_one, rest_two = tie((mine, rest_one, rest_two))
    mine = next_hop(chips - 2, mine)
    density = sum_parts(multiply(head_columns, gather_far(mine)))
    density = next_hop(chips - 1, density)
    results = [density]

    mine = gather_near(density)
    pieces = [entered] + [climbs[h] + falls[chips - h] for h in range(1, chips)]
    both = [v for piece in pieces for v in (piece, other_core(piece))]
    sent, rest_one, density = tie((sent, rest_one, density))
    first_columns = pick([chunks[0], *sent])
    rest_one = add_entered(rest_one, both, 0, 1)
    mine, both, rest_one, first_columns = tie((mine, both, rest_one, first_columns))
    spread = gather_far(mine)
    right_side = own_part(excitation[1]) - sum_parts(rest_one + multiply(first_columns, spread))

    right_side, rest_two, both, old = tie((right_side, rest_two, both, mine))
    mine = gather_near(right_side)
    nears = [old] + [lax.ppermute(old, "lag", [(j, 0)]) for j in range(1, groups)]
    rest_two = add_entered(rest_two, both, 1, 2)
    mine, rest_two, nears = tie((mine, rest_two, nears))
    density = sum_parts(multiply(head_columns, gather_far(mine)))
    results.append(density)

    density, nears, rest_two = tie((density, nears, rest_two))
    mine = gather_near(density)
    fars = other_core(jnp.stack(nears))
    later = add_entered(rest_two, both, 0, 2)
    later = add_second(later, nears, [fars[j] for j in range(groups)])
    mine, later = tie((mine, later))
    right_side = own_part(excitation[2]) - sum_parts(later + multiply(first_columns, gather_far(mine)))

    right_side, results = tie((right_side, results))
    mine = gather_near(right_side)
    early = [whole_rows(density) for density in results]
    mine, early = tie((mine, early))
    density = sum_parts(multiply(head_columns, gather_far(mine)))
    return jnp.stack([*early, whole_rows(density)], axis=0)


def solution(mesh):
    placed = (P("lag", "row", None), P("row", None), P(None, "row", None), P("lag", "row", None))

    return jax.shard_map(on_device, mesh=mesh, in_specs=placed, out_specs=P(None, "row", None), check_vma=False)
```

```python
import jax
import jax.numpy as jnp
from jax import lax
from jax.experimental import pallas as pl
from jax.experimental.pallas import tpu as pltpu
from jax.sharding import PartitionSpec as P


STEPS = 3
HIGHEST = lax.Precision.HIGHEST
F32 = jnp.float32
BF16 = jnp.bfloat16


def split(value):
    high = value.astype(BF16)
    return high, (value - high.astype(F32)).astype(BF16)


def dot(a, b):
    return jnp.dot(a, b, preferred_element_type=F32)


def product(weight, vectors):
    count, width = len(vectors), vectors[0].shape[1]
    wh, wl = split(weight)
    highs, lows = zip(*(split(v) for v in vectors))
    main = dot(wh, jnp.concatenate(highs + lows, axis=1))
    rest = dot(wl, jnp.concatenate(highs, axis=1) if count > 1 else highs[0])
    return main[:, : count * width] + main[:, count * width :] + rest


def ordered(core, near, far):
    return jnp.concatenate([jnp.where(core == 0, near, far), jnp.where(core == 0, far, near)], axis=0)


def chip_kernel(where, weights, near, far, *refs):
    outs, high, low = refs[-STEPS - 2 : -2], *refs[-2:]
    totals = refs[:-STEPS - 2]
    at = pl.program_id(0)
    lags, rows, width = near.shape
    core = where[0]

    @pl.when(at == 0)
    def _():
        for n, out in enumerate(outs):
            out[...] = totals[n][...] if totals else jnp.zeros_like(out)
        for k in range(lags):
            columns = slice((lags - 1 - k) * width, (lags - k) * width)
            for piece, side in ((near, core), (far, 1 - core)):
                here = pl.ds(pl.multiple_of(side * rows, rows), rows)
                high[here, columns], low[here, columns] = split(piece[k])

    for k in range(STEPS):

        @pl.when(at == k if k + 1 < STEPS else at >= k)
        def _():
            size = (k + 1) * width
            columns = pl.ds(pl.multiple_of((lags - 1 - at) * width, width), size)
            wh, wl = split(weights[0])
            h = high[:, columns]
            main = dot(wh, jnp.concatenate([h, low[:, columns]], axis=1))
            result = main[:, :size] + main[:, size:] + dot(wl, h)
            for n in range(k + 1):
                outs[n][...] += result[:, n * width : (n + 1) * width]


def first_kernel(where, weights, near, far, total, out):
    @pl.when(pl.program_id(0) == 0)
    def _():
        out[...] = total[...]

    out[...] += product(weights[0], [ordered(where[0], near[0], far[0])])


def rest_kernel(where, weights, near, near_before, far, far_before, one, two, one_out, two_out):
    at = pl.program_id(0)
    width = near.shape[-1]
    now = ordered(where[0], near[0], far[0])

    @pl.when(at == 0)
    def _():
        one_out[...] = one[...] + product(weights[0], [now])
        two_out[...] = two[...]

    @pl.when(at > 0)
    def _():
        result = product(weights[0], [now, ordered(where[0], near_before[0], far_before[0])])
        one_out[...] += result[:, :width]
        two_out[...] += result[:, width:]


def entered_kernel(where, weights, near, far, one, two, one_out, two_out):
    at = pl.program_id(0)
    width = near.shape[-1]
    last = ordered(where[0], near[1], far[1])

    @pl.when(at == 0)
    def _():
        one_out[...] = one[...]
        two_out[...] = two[...]

    @pl.when(jnp.logical_and(where[1] > 0, at == 0))
    def _():
        result = product(weights[0], [last, ordered(where[0], near[0], far[0])])
        one_out[...] += result[:, :width]
        two_out[...] += result[:, width:]

    @pl.when(jnp.logical_and(where[1] > 0, at == 1))
    def _():
        two_out[...] += product(weights[0], [last])


def second_kernel(where, weights, *refs):
    nears, fars, total, out = refs[: len(refs) // 2 - 1], refs[len(refs) // 2 - 1 : -2], refs[-2], refs[-1]

    @pl.when(pl.program_id(0) == 0)
    def _():
        out[...] = total[...]

    @pl.when(where[1] == 0)
    def _():
        near, far = (jnp.concatenate([p[...] for p in parts], axis=0) for parts in (nears, fars))
        out[...] += product(weights[0], [ordered(where[0], near, far)])


def columns_kernel(where, *refs):
    fold, groups = where.shape[1] - 1, where.shape[2]
    sources, outs = refs[:fold], refs[fold:]
    part = sources[0].shape[2] // groups
    take = lambda j: jnp.concatenate([s[0, :, j * part : (j + 1) * part] for s in sources], axis=1)
    if len(outs) == 1:
        for j in range(groups):

            @pl.when(where[0, fold, 0] == j)
            def _():
                outs[0][...] = take(j)

        return
    for j in range(groups - 1):
        outs[j][...] = take(j)
    for side, out in enumerate(outs[groups - 1 :]):

        @pl.when(pl.program_id(0) == side)
        def _():
            out[...] = take(groups - 1)


def pick_kernel(which, *refs):
    sources, out = refs[:-1], refs[-1]
    groups = len(sources) - 1
    for j, source in enumerate(sources):
        chosen = which[0] == min(j, groups - 1)
        if j >= groups - 1:
            chosen = jnp.logical_and(chosen, pl.program_id(0) == j - groups + 1)

        @pl.when(chosen)
        def _():
            out[...] = source[...]


def call(kernel, where, grid, operands, specs, count, shape, cost, aliases={}, scratch=()):
    return pl.pallas_call(
        kernel,
        out_shape=[jax.ShapeDtypeStruct(shape, F32)] * count,
        grid_spec=pltpu.PrefetchScalarGridSpec(
            num_scalar_prefetch=1, grid=grid, in_specs=specs, out_specs=[all_of(shape)] * count, scratch_shapes=scratch
        ),
        input_output_aliases=aliases,
        cost_estimate=pl.CostEstimate(flops=cost[0], bytes_accessed=cost[1], transcendentals=0),
        compiler_params=pltpu.CompilerParams(dimension_semantics=("arbitrary",) * len(grid)),
    )(where, *operands)


def all_of(shape):
    return pl.BlockSpec(shape, lambda *_: (0,) * len(shape))


def on_device(lag_weights, inverse_head, excitation, history):
    groups, devices = lax.axis_size("lag"), lax.axis_size("row")
    group, at = lax.axis_index("lag"), lax.axis_index("row")
    chips = devices // 2
    chip, core = at // 2, at % 2
    lags, rows, order = lag_weights.shape
    width = history.shape[-1]
    part = rows // groups
    tile = rows * 2 * rows
    square = (rows, width)
    tie = lax.optimization_barrier

    def pairs(axis_size, mask):
        return [(i, i ^ mask) for i in range(axis_size)]

    def other_core(value):
        return lax.ppermute(value, "row", pairs(devices, 1))

    def along(value, step, sources):
        return lax.ppermute(value, "row", [(2 * i + c, 2 * (i + step) + c) for i in sources for c in (0, 1)])

    def go_up(value, hop):
        return along(value, 1, range(hop - 1, chips - 1))

    def go_down(value, hop):
        return along(value, -1, range(1, chips - hop + 1))

    def taken(z, stage):
        both = min(z, chips - 1 - z)
        if stage <= 2 * both:
            return (stage + 1) // 2, stage % 2 == 1
        return stage - both, z >= stage - both

    def by_chip(values):
        result = jnp.int32(values[0])
        for z in range(1, chips):
            result = jnp.where(chip == z, values[z], result)
        return result

    def source_of(stage):
        return by_chip([z + (-h if u else h) for z in range(chips) for h, u in [taken(z, stage)]])

    def choose(stage, ups, downs):
        found = sorted({taken(z, stage) for z in range(chips)})
        arrays = [(ups if u else downs)[h] for h, u in found]
        return lax.select_n(by_chip([found.index(taken(z, stage)) for z in range(chips)]), *arrays) if len(found) > 1 else arrays[0]

    stages = [chip] + [source_of(stage) for stage in range(1, chips)]
    xored = [chip ^ k for k in range(chips)]
    where = jnp.stack([core, group, *stages, *xored]).astype(jnp.int32)

    def weight_spec(stage, first=0):
        return pl.BlockSpec((1, rows, 2 * rows), lambda k, w: (k + first, 0, w[2 + stage]))

    def lag_spec(shift):
        return pl.BlockSpec((1, rows, width), lambda k, w: (jnp.maximum(k + shift, 0), 0, 0))

    def add_chip(totals, near, far, stage):
        return call(
            chip_kernel, where, (lags,), (lag_weights, near, far, *totals),
            [weight_spec(stage)] + [all_of(v.shape) for v in (near, far, *totals)], STEPS, square,
            (18 * lags * tile * width, 4 * lags * tile), {4 + n: n for n in range(len(totals))},
            [pltpu.VMEM((2 * rows, lags * width), BF16)] * 2,
        )

    def add_first(total, near, far, stage):
        return call(
            first_kernel, where, (lags,), (lag_weights, near, far, total),
            [weight_spec(stage), lag_spec(0), lag_spec(0), all_of(square)], 1, square,
            (6 * lags * tile * width, 4 * lags * tile), {4: 0},
        )[0]

    def add_rest(one, two, near, far, stage):
        return call(
            rest_kernel, where, (lags - 1,), (lag_weights, near, near, far, far, one, two),
            [weight_spec(stage, 1), lag_spec(0), lag_spec(-1), lag_spec(0), lag_spec(-1), all_of(square), all_of(square)],
            2, square, (12 * lags * tile * width, 4 * lags * tile), {6: 0, 7: 1},
        )

    def add_entered(one, two, near, stage):
        far = other_core(near)
        spec = pl.BlockSpec((1, rows, 2 * rows), lambda k, w: (jnp.where(w[1] > 0, k, 0), 0, w[2 + stage]))
        return call(
            entered_kernel, where, (STEPS - 1,), (lag_weights, near, far, one, two),
            [spec, all_of(near.shape), all_of(near.shape), all_of(square), all_of(square)],
            2, square, (18 * tile * width, 8 * tile), {4: 0, 5: 1},
        )

    def add_second(total, nears, fars):
        block = pl.BlockSpec((part, width), lambda k, w: (k, 0))
        return call(
            second_kernel, where, (chips,), (lag_weights, *nears, *fars, total),
            [pl.BlockSpec((1, rows, 2 * rows), lambda k, w: (1, 0, jnp.where(w[1] == 0, w[2 + chips + k], 0)))]
            + [block] * 2 * groups + [all_of(square)],
            1, square, (6 * rows * order * width, 4 * rows * order), {2 + 2 * groups: 0},
        )[0]

    slots = jnp.stack([(chip ^ k) * 2 + (core ^ h) for h in (0, 1) for k in range(chips)]).astype(jnp.int32)
    meet = devices * part

    def columns(matrix, every):
        fold = devices // 2
        numbers = jnp.tile(slots.reshape(2, fold, 1), (1, 1, groups))
        numbers = jnp.concatenate([numbers, jnp.full((2, 1, groups), group, jnp.int32)], axis=1)
        whole = pl.BlockSpec((rows, meet // 2), lambda s, w: (0, s))
        half = pl.BlockSpec((rows, meet // 2), lambda s, w: (0, 0))
        shape = lambda size: jax.ShapeDtypeStruct((rows, size), F32)
        return pl.pallas_call(
            columns_kernel,
            out_shape=[shape(meet)] * (groups - 1) + [shape(meet // 2)] * 2 if every else [shape(meet)],
            grid_spec=pltpu.PrefetchScalarGridSpec(
                num_scalar_prefetch=1,
                grid=(2,),
                in_specs=[pl.BlockSpec((1, rows, rows), lambda s, w, i=i: (0, 0, w[s, i, 0])) for i in range(fold)],
                out_specs=[whole] * (groups - 1) + [half] * 2 if every else [whole],
            ),
            cost_estimate=pl.CostEstimate(flops=0, bytes_accessed=8 * rows * order, transcendentals=0),
            compiler_params=pltpu.CompilerParams(dimension_semantics=("arbitrary",)),
            name="columns",
        )(numbers, *[matrix] * fold)

    def pick(matrices):
        spec = lambda j: pl.BlockSpec((rows, meet // 2), lambda s, w: (0, jnp.where(w[0] == j, s, 0)))
        return pl.pallas_call(
            pick_kernel,
            out_shape=jax.ShapeDtypeStruct((rows, meet), F32),
            grid_spec=pltpu.PrefetchScalarGridSpec(
                num_scalar_prefetch=1,
                grid=(2,),
                in_specs=[spec(j) for j in range(groups - 1)] + [all_of((rows, meet // 2))] * 2,
                out_specs=pl.BlockSpec((rows, meet // 2), lambda s, w: (0, s)),
            ),
            cost_estimate=pl.CostEstimate(flops=0, bytes_accessed=16 * rows * meet, transcendentals=0),
            compiler_params=pltpu.CompilerParams(dimension_semantics=("arbitrary",)),
            name="pick",
        )(group.astype(jnp.int32).reshape(1), *matrices)

    def gather_near(value):
        pieces = [value] + [lax.ppermute(value, "row", pairs(devices, 2 * k)) for k in range(1, chips)]
        return jnp.concatenate(pieces, axis=0)

    def gather_far(mine):
        return jnp.concatenate([mine, other_core(mine)], axis=0)

    def own_part(value):
        return lax.dynamic_slice(value, (group * part, 0), (part, value.shape[1]))

    def sum_parts(value):
        result = own_part(value)
        for mask in range(1, groups):
            sent = lax.dynamic_slice(value, ((group ^ mask) * part, 0), (part, width))
            result = result + lax.ppermute(sent, "lag", pairs(groups, mask))
        return result

    def whole_rows(value):
        pieces = [value] + [lax.ppermute(value, "lag", pairs(groups, mask)) for mask in range(1, groups)]
        return jnp.concatenate([lax.select_n(group ^ i, *pieces) for i in range(groups)], axis=1)

    def enter(tail):
        return lax.ppermute(tail, "lag", [(i, i + 1) for i in range(groups - 1)])

    def tails(arrays):
        return {hop: value[lags - (STEPS - 1) :] for hop, value in arrays.items()}

    def multiply(matrix, vector):
        return jnp.dot(matrix, vector, precision=HIGHEST)

    ups, downs = {1: go_up(history, 1)}, {1: go_down(history, 1)}
    tail = history[lags - (STEPS - 1) :]
    entered = [enter(jnp.where(group >= 0, tail, 0.0))]
    own_far = other_core(history)
    *chunks, last_near, last_far = columns(lag_weights, True)
    relayed = lax.ppermute(last_far, "lag", [(0, groups // 2)])
    sent = [lax.ppermute(chunks[j], "lag", [(0, j)]) for j in range(1, groups - 1)]
    (head_columns,) = columns(inverse_head[None], False)
    ups[1], downs[1], entered, own_far, head_columns = tie((ups[1], downs[1], entered, own_far, head_columns))
    totals = []
    for stage in range(1, chips - 1):
        next_up, next_down = go_up(ups[stage], stage + 1), go_down(downs[stage], stage + 1)
        near = choose(stage, ups, downs)
        entered.append(enter(choose(stage, tails(ups), tails(downs))))
        if stage == 1:
            last_near, entered[0] = tie((last_near, entered[0]))
            sent.append(lax.ppermute(last_near, "lag", [(0, groups - 1)]))
            totals = add_chip([], history, own_far, 0)
        if stage == chips - 2:
            relayed, near = tie((relayed, near))
            sent.append(lax.ppermute(relayed, "lag", [(groups // 2, groups - 1)]))
        totals = add_chip(totals, near, other_core(near), stage)
        if stage == chips - 2:
            for early in range(chips - 2):
                entered[early], totals = tie((entered[early], totals))
                totals = [totals[0], *add_entered(totals[1], totals[2], entered[early], early)]
        ups[stage + 1], downs[stage + 1] = next_up, next_down
        ups, downs, totals = tie((ups, downs, totals))
    first, one, two = totals

    near = choose(chips - 1, ups, downs)
    far = other_core(near)
    first = add_first(first, near, far, chips - 1)

    right_side = own_part(excitation[0]) - sum_parts(first)
    right_side, ups, downs, near, far, one, two = tie((right_side, ups, downs, near, far, one, two))
    mine = gather_near(right_side)
    entered.append(enter(choose(chips - 1, tails(ups), tails(downs))))
    one, two = add_rest(one, two, near, far, chips - 1)
    mine, one, two, sent = tie((mine, one, two, sent))
    density = sum_parts(multiply(head_columns, gather_far(mine)))
    first_columns = pick([chunks[0], *sent])
    results = [density]

    density, first_columns, entered, one, two = tie((density, first_columns, entered, one, two))
    mine = gather_near(density)
    for stage in (chips - 2, chips - 1):
        one, two = add_entered(one, two, entered[stage], stage)
    mine, one, two = tie((mine, one, two))
    right_side = own_part(excitation[1]) - sum_parts(one + multiply(first_columns, gather_far(mine)))

    right_side, two, old = tie((right_side, two, mine))
    mine = gather_near(right_side)
    nears = [old] + [lax.ppermute(old, "lag", [(j, 0)]) for j in range(1, groups)]
    mine, two, nears = tie((mine, two, nears))
    spread = gather_far(mine)
    fars = other_core(jnp.stack(nears))
    spread, fars = tie((spread, fars))
    density = sum_parts(multiply(head_columns, spread))
    two = add_second(two, nears, [fars[j] for j in range(groups)])
    results.append(density)

    density, two = tie((density, two))
    mine = gather_near(density)
    right_side = own_part(excitation[2]) - sum_parts(two + multiply(first_columns, gather_far(mine)))

    right_side, results = tie((right_side, results))
    mine = gather_near(right_side)
    early = whole_rows(jnp.stack(results))
    mine, early = tie((mine, early))
    density = sum_parts(multiply(head_columns, gather_far(mine)))
    return jnp.concatenate([early, whole_rows(density[None])], axis=0)


def solution(mesh):
    placed = (P("lag", "row", None), P("row", None), P(None, "row", None), P("lag", "row", None))

    return jax.shard_map(on_device, mesh=mesh, in_specs=placed, out_specs=P(None, "row", None), check_vma=False)
```

```python
import jax
import jax.numpy as jnp
from jax import lax
from jax.experimental import pallas as pl
from jax.experimental.pallas import tpu as pltpu
from jax.sharding import PartitionSpec as P


STEPS = 3
F32 = jnp.float32
BF16 = jnp.bfloat16


def split(value):
    high = value.astype(BF16)
    return high, (value - high.astype(F32)).astype(BF16)


def dot(a, b):
    return jnp.dot(a, b, preferred_element_type=F32)


def product(weight, vectors):
    count, width = len(vectors), vectors[0].shape[1]
    wh, wl = split(weight)
    highs, lows = zip(*(split(v) for v in vectors))
    main = dot(wh, jnp.concatenate(highs + lows, axis=1))
    rest = dot(wl, jnp.concatenate(highs, axis=1) if count > 1 else highs[0])
    return main[:, : count * width] + main[:, count * width :] + rest


def ordered(core, near, far):
    return jnp.concatenate([jnp.where(core == 0, near, far), jnp.where(core == 0, far, near)], axis=0)


def chip_kernel(where, weights, *refs):
    outs, high, low = refs[-STEPS - 2 : -2], *refs[-2:]
    pieces = refs[: len(refs) - STEPS - 2]
    totals = pieces[len(pieces) - STEPS :] if len(pieces) % 2 else []
    number, at = pl.program_id(0), pl.program_id(1)
    lags, rows, width = pieces[0].shape
    core = where[0]

    @pl.when(jnp.logical_and(number == 0, at == 0))
    def _():
        for n, out in enumerate(outs):
            out[...] = totals[n][...] if totals else jnp.zeros_like(out)

    for i in range(len(pieces) // 2 - (1 if totals else 0)):

        @pl.when(jnp.logical_and(number == i, at == 0))
        def _():
            for k in range(lags):
                columns = slice((lags - 1 - k) * width, (lags - k) * width)
                for piece, side in ((pieces[2 * i], core), (pieces[2 * i + 1], 1 - core)):
                    here = pl.ds(pl.multiple_of(side * rows, rows), rows)
                    high[here, columns], low[here, columns] = split(piece[k])

    for k in range(STEPS):

        @pl.when(at == k if k + 1 < STEPS else at >= k)
        def _():
            size = (k + 1) * width
            columns = pl.ds(pl.multiple_of((lags - 1 - at) * width, width), size)
            wh, wl = split(weights[0])
            h = high[:, columns]
            main = dot(wh, jnp.concatenate([h, low[:, columns]], axis=1))
            result = main[:, :size] + main[:, size:] + dot(wl, h)
            for n in range(k + 1):
                outs[n][...] += result[:, n * width : (n + 1) * width]


def first_kernel(where, weights, near, far, total, out, tail):
    @pl.when(pl.program_id(0) == 0)
    def _():
        out[...] = total[...]

    tail[...] = near[...]
    out[...] += product(weights[0], [ordered(where[0], near[0], far[0])])


def rest_kernel(where, weights, near, near_before, far, far_before, one, two, one_out, two_out):
    at = pl.program_id(0)
    width = near.shape[-1]
    now = ordered(where[0], near[0], far[0])

    @pl.when(at == 0)
    def _():
        one_out[...] = one[...] + product(weights[0], [now])
        two_out[...] = two[...]

    @pl.when(at > 0)
    def _():
        result = product(weights[0], [now, ordered(where[0], near_before[0], far_before[0])])
        one_out[...] += result[:, :width]
        two_out[...] += result[:, width:]


def entered_kernel(where, weights, *refs):
    pieces, (one, two, one_out, two_out, high, low) = refs[:-6], refs[-6:]
    number, at = pl.program_id(0), pl.program_id(1)
    before, rows, width = pieces[0].shape

    @pl.when(jnp.logical_and(number == 0, at == 0))
    def _():
        one_out[...] = one[...]
        two_out[...] = two[...]

    for i in range(len(pieces) // 2):

        @pl.when(jnp.logical_and(number == i, at == 0))
        def _():
            for k in range(before):
                columns = slice((before - 1 - k) * width, (before - k) * width)
                for piece, side in ((pieces[2 * i], where[0]), (pieces[2 * i + 1], 1 - where[0])):
                    here = pl.ds(pl.multiple_of(side * rows, rows), rows)
                    high[here, columns], low[here, columns] = split(piece[k])

    for k in range(before):

        @pl.when(jnp.logical_and(where[1] > 0, at == k))
        def _():
            size = (before - k) * width
            wh, wl = split(weights[0])
            h = high[:, :size]
            main = dot(wh, jnp.concatenate([h, low[:, :size]], axis=1))
            result = main[:, :size] + main[:, size:] + dot(wl, h)
            if k == 0:
                one_out[...] += result[:, :width]
            two_out[...] += result[:, size - width :]


def multiply_kernel(where, matrix, near, far, total, out):
    vector = jnp.concatenate([near[...], far[...]], axis=0)
    out[...] = total[...] + product(matrix[...], [vector])


def second_kernel(where, weights, *refs):
    nears, fars, total, out = refs[: len(refs) // 2 - 1], refs[len(refs) // 2 - 1 : -2], refs[-2], refs[-1]

    @pl.when(pl.program_id(0) == 0)
    def _():
        out[...] = total[...]

    @pl.when(where[1] == 0)
    def _():
        near, far = (jnp.concatenate([p[...] for p in parts], axis=0) for parts in (nears, fars))
        out[...] += product(weights[0], [ordered(where[0], near, far)])


def columns_kernel(where, *refs):
    fold, groups = where.shape[1] - 1, where.shape[2]
    sources, outs = refs[:fold], refs[fold:]
    part = sources[0].shape[2] // groups
    take = lambda j: jnp.concatenate([s[0, :, j * part : (j + 1) * part] for s in sources], axis=1)
    if len(outs) == 1:
        for j in range(groups):

            @pl.when(where[0, fold, 0] == j)
            def _():
                outs[0][...] = take(j)

        return
    for j in range(groups - 1):
        outs[j][...] = take(j)
    for side, out in enumerate(outs[groups - 1 :]):

        @pl.when(pl.program_id(0) == side)
        def _():
            out[...] = take(groups - 1)


def pick_kernel(which, *refs):
    sources, out = refs[:-1], refs[-1]
    groups = len(sources) - 1
    for j, source in enumerate(sources):
        chosen = which[0] == min(j, groups - 1)
        if j >= groups - 1:
            chosen = jnp.logical_and(chosen, pl.program_id(0) == j - groups + 1)

        @pl.when(chosen)
        def _():
            out[...] = source[...]


def call(kernel, where, grid, operands, specs, count, shape, cost, aliases={}, scratch=()):
    return pl.pallas_call(
        kernel,
        out_shape=[jax.ShapeDtypeStruct(shape, F32)] * count,
        grid_spec=pltpu.PrefetchScalarGridSpec(
            num_scalar_prefetch=1, grid=grid, in_specs=specs, out_specs=[all_of(shape)] * count, scratch_shapes=scratch
        ),
        input_output_aliases=aliases,
        cost_estimate=pl.CostEstimate(flops=cost[0], bytes_accessed=cost[1], transcendentals=0),
        compiler_params=pltpu.CompilerParams(dimension_semantics=("arbitrary",) * len(grid)),
    )(where, *operands)


def all_of(shape):
    return pl.BlockSpec(shape, lambda *_: (0,) * len(shape))


def on_device(lag_weights, inverse_head, excitation, history):
    groups, devices = lax.axis_size("lag"), lax.axis_size("row")
    group, at = lax.axis_index("lag"), lax.axis_index("row")
    chips = devices // 2
    chip, core = at // 2, at % 2
    lags, rows, order = lag_weights.shape
    width = history.shape[-1]
    part = rows // groups
    tile = rows * 2 * rows
    square = (rows, width)
    tie = lax.optimization_barrier

    def pairs(axis_size, mask):
        return [(i, i ^ mask) for i in range(axis_size)]

    def other_core(value):
        return lax.ppermute(value, "row", pairs(devices, 1))

    def along(value, step, sources):
        return lax.ppermute(value, "row", [(2 * i + c, 2 * (i + step) + c) for i in sources for c in (0, 1)])

    def go_up(value, hop):
        return along(value, 1, range(hop - 1, chips - 1))

    def go_down(value, hop):
        return along(value, -1, range(1, chips - hop + 1))

    def taken(z, stage):
        both = min(z, chips - 1 - z)
        if stage <= 2 * both:
            return (stage + 1) // 2, stage % 2 == 1
        return stage - both, z >= stage - both

    def by_chip(values):
        result = jnp.int32(values[0])
        for z in range(1, chips):
            result = jnp.where(chip == z, values[z], result)
        return result

    def source_of(stage):
        return by_chip([z + (-h if u else h) for z in range(chips) for h, u in [taken(z, stage)]])

    def choose(stage, ups, downs):
        found = sorted({taken(z, stage) for z in range(chips)})
        arrays = [(ups if u else downs)[h] for h, u in found]
        return lax.select_n(by_chip([found.index(taken(z, stage)) for z in range(chips)]), *arrays) if len(found) > 1 else arrays[0]

    stages = [chip] + [source_of(stage) for stage in range(1, chips)]
    xored = [chip ^ k for k in range(chips)]
    where = jnp.stack([core, group, *stages, *xored]).astype(jnp.int32)

    def weight_spec(stage, first=0):
        return pl.BlockSpec((1, rows, 2 * rows), lambda k, w: (k + first, 0, w[2 + stage]))

    def lag_spec(shift):
        return pl.BlockSpec((1, rows, width), lambda k, w: (jnp.maximum(k + shift, 0), 0, 0))

    def add_chip(totals, pieces, stage):
        count = len(pieces) // 2
        return call(
            chip_kernel, where, (count, lags), (lag_weights, *pieces, *totals),
            [pl.BlockSpec((1, rows, 2 * rows), lambda i, k, w: (k, 0, w[2 + stage + i]))]
            + [all_of(v.shape) for v in (*pieces, *totals)], STEPS, square,
            (18 * count * lags * tile * width, 4 * count * lags * tile), {2 + len(pieces) + n: n for n in range(len(totals))},
            [pltpu.VMEM((2 * rows, lags * width), BF16)] * 2,
        )

    def add_first(total, near, far, stage):
        before = STEPS - 1
        return pl.pallas_call(
            first_kernel,
            out_shape=[jax.ShapeDtypeStruct(square, F32), jax.ShapeDtypeStruct((before, *square), F32)],
            grid_spec=pltpu.PrefetchScalarGridSpec(
                num_scalar_prefetch=1,
                grid=(lags,),
                in_specs=[weight_spec(stage), lag_spec(0), lag_spec(0), all_of(square)],
                out_specs=[all_of(square), pl.BlockSpec((1, *square), lambda k, w: (jnp.maximum(k + before - lags, 0), 0, 0))],
            ),
            input_output_aliases={4: 0},
            cost_estimate=pl.CostEstimate(flops=6 * lags * tile * width, bytes_accessed=4 * lags * tile, transcendentals=0),
            compiler_params=pltpu.CompilerParams(dimension_semantics=("arbitrary",)),
            name="first",
        )(where, lag_weights, near, far, total)

    def add_rest(one, two, near, far, stage):
        return call(
            rest_kernel, where, (lags - 1,), (lag_weights, near, near, far, far, one, two),
            [weight_spec(stage, 1), lag_spec(0), lag_spec(-1), lag_spec(0), lag_spec(-1), all_of(square), all_of(square)],
            2, square, (12 * lags * tile * width, 4 * lags * tile), {6: 0, 7: 1},
        )

    def add_entered(one, two, nears, stage):
        pieces = [v for near in nears for v in (near, other_core(near))]
        spec = pl.BlockSpec((1, rows, 2 * rows), lambda i, k, w: (jnp.where(w[1] > 0, k, 0), 0, jnp.where(w[1] > 0, w[2 + stage + i], 0)))
        return call(
            entered_kernel, where, (len(nears), STEPS - 1), (lag_weights, *pieces, one, two),
            [spec] + [all_of(v.shape) for v in (*pieces, one, two)],
            2, square, (18 * len(nears) * tile * width, 8 * len(nears) * tile), {2 + len(pieces): 0, 3 + len(pieces): 1},
            [pltpu.VMEM((2 * rows, (STEPS - 1) * width), BF16)] * 2,
        )

    def add_second(total, nears, fars):
        block = pl.BlockSpec((part, width), lambda k, w: (k, 0))
        return call(
            second_kernel, where, (chips,), (lag_weights, *nears, *fars, total),
            [pl.BlockSpec((1, rows, 2 * rows), lambda k, w: (1, 0, jnp.where(w[1] == 0, w[2 + chips + k], 0)))]
            + [block] * 2 * groups + [all_of(square)],
            1, square, (6 * rows * order * width, 4 * rows * order), {2 + 2 * groups: 0},
        )[0]

    slots = jnp.stack([(chip ^ k) * 2 + (core ^ h) for h in (0, 1) for k in range(chips)]).astype(jnp.int32)
    meet = devices * part

    def columns(matrix, every):
        fold = devices // 2
        numbers = jnp.tile(slots.reshape(2, fold, 1), (1, 1, groups))
        numbers = jnp.concatenate([numbers, jnp.full((2, 1, groups), group, jnp.int32)], axis=1)
        whole = pl.BlockSpec((rows, meet // 2), lambda s, w: (0, s))
        half = pl.BlockSpec((rows, meet // 2), lambda s, w: (0, 0))
        shape = lambda size: jax.ShapeDtypeStruct((rows, size), F32)
        return pl.pallas_call(
            columns_kernel,
            out_shape=[shape(meet)] * (groups - 1) + [shape(meet // 2)] * 2 if every else [shape(meet)],
            grid_spec=pltpu.PrefetchScalarGridSpec(
                num_scalar_prefetch=1,
                grid=(2,),
                in_specs=[pl.BlockSpec((1, rows, rows), lambda s, w, i=i: (0, 0, w[s, i, 0])) for i in range(fold)],
                out_specs=[whole] * (groups - 1) + [half] * 2 if every else [whole],
            ),
            cost_estimate=pl.CostEstimate(flops=0, bytes_accessed=8 * rows * order, transcendentals=0),
            compiler_params=pltpu.CompilerParams(dimension_semantics=("arbitrary",)),
            name="columns",
        )(numbers, *[matrix] * fold)

    def pick(matrices):
        spec = lambda j: pl.BlockSpec((rows, meet // 2), lambda s, w: (0, jnp.where(w[0] == j, s, 0)))
        return pl.pallas_call(
            pick_kernel,
            out_shape=jax.ShapeDtypeStruct((rows, meet), F32),
            grid_spec=pltpu.PrefetchScalarGridSpec(
                num_scalar_prefetch=1,
                grid=(2,),
                in_specs=[spec(j) for j in range(groups - 1)] + [all_of((rows, meet // 2))] * 2,
                out_specs=pl.BlockSpec((rows, meet // 2), lambda s, w: (0, s)),
            ),
            cost_estimate=pl.CostEstimate(flops=0, bytes_accessed=16 * rows * meet, transcendentals=0),
            compiler_params=pltpu.CompilerParams(dimension_semantics=("arbitrary",)),
            name="pick",
        )(group.astype(jnp.int32).reshape(1), *matrices)

    def gather_near(value):
        pieces = [value] + [lax.ppermute(value, "row", pairs(devices, 2 * k)) for k in range(1, chips)]
        return jnp.concatenate(pieces, axis=0)

    def own_part(value):
        return lax.dynamic_slice(value, (group * part, 0), (part, value.shape[1]))

    def sum_parts(value):
        result = own_part(value)
        for mask in range(1, groups):
            sent = lax.dynamic_slice(value, ((group ^ mask) * part, 0), (part, width))
            result = result + lax.ppermute(sent, "lag", pairs(groups, mask))
        return result

    def whole_rows(value):
        pieces = [value] + [lax.ppermute(value, "lag", pairs(groups, mask)) for mask in range(1, groups)]
        return jnp.concatenate([lax.select_n(group ^ i, *pieces) for i in range(groups)], axis=1)

    def enter(tail):
        return lax.ppermute(tail, "lag", [(i, i + 1) for i in range(groups - 1)])

    def tails(arrays):
        return {hop: value[lags - (STEPS - 1) :] for hop, value in arrays.items()}

    def multiply(matrix, mine, total):
        operands = (matrix, mine, other_core(mine), total)
        return call(
            multiply_kernel, where, (1,), operands, [all_of(v.shape) for v in operands],
            1, square, (6 * rows * meet * width, 4 * rows * meet),
        )[0]

    ups, downs = {1: go_up(history, 1)}, {1: go_down(history, 1)}
    tail = history[lags - (STEPS - 1) :]
    entered = [enter(jnp.where(group >= 0, tail, 0.0))]
    own_far = other_core(history)
    *chunks, last_near, last_far = columns(lag_weights, True)
    relayed = lax.ppermute(last_far, "lag", [(0, groups // 2)])
    sent = [lax.ppermute(chunks[j], "lag", [(0, j)]) for j in range(1, groups - 1)]
    (head_columns,) = columns(inverse_head[None], False)
    ups[1], downs[1], entered, own_far, head_columns = tie((ups[1], downs[1], entered, own_far, head_columns))
    totals = []
    for stage in range(1, chips - 1):
        next_up, next_down = go_up(ups[stage], stage + 1), go_down(downs[stage], stage + 1)
        near = choose(stage, ups, downs)
        entered.append(enter(choose(stage, tails(ups), tails(downs))))
        if stage == 1:
            last_near, entered[0] = tie((last_near, entered[0]))
            sent.append(lax.ppermute(last_near, "lag", [(0, groups - 1)]))
        if stage == chips - 2:
            relayed, near = tie((relayed, near))
            sent.append(lax.ppermute(relayed, "lag", [(groups // 2, groups - 1)]))
        pieces = [near, other_core(near)]
        totals = add_chip([], [history, own_far, *pieces], 0) if stage == 1 else add_chip(totals, pieces, stage)
        if stage == chips - 2:
            totals = [totals[0], *add_entered(totals[1], totals[2], entered[:1], 0)]
        ups[stage + 1], downs[stage + 1] = next_up, next_down
        ups, downs, totals = tie((ups, downs, totals))
    first, one, two = totals

    near = choose(chips - 1, ups, downs)
    far = other_core(near)
    first, tail = add_first(first, near, far, chips - 1)
    nothing = jnp.zeros(square, F32)

    right_side = own_part(excitation[0]) - sum_parts(first)
    right_side, tail, near, far, one, two = tie((right_side, tail, near, far, one, two))
    mine = gather_near(right_side)
    entered.append(enter(tail))
    one, two = add_rest(one, two, near, far, chips - 1)
    mine, one, two, sent = tie((mine, one, two, sent))
    density = sum_parts(multiply(head_columns, mine, nothing))
    first_columns = pick([chunks[0], *sent])
    results = [density]

    density, first_columns, entered, one, two = tie((density, first_columns, entered, one, two))
    mine = gather_near(density)
    one, two = add_entered(one, two, entered[1:], 1)
    mine, one, two = tie((mine, one, two))
    right_side = own_part(excitation[1]) - sum_parts(multiply(first_columns, mine, one))

    right_side, two, old = tie((right_side, two, mine))
    mine = gather_near(right_side)
    nears = [old] + [lax.ppermute(old, "lag", [(j, 0)]) for j in range(1, groups)]
    mine, two, nears = tie((mine, two, nears))
    density = sum_parts(multiply(head_columns, mine, nothing))
    fars = other_core(jnp.stack(nears))
    results.append(density)

    density, two, nears, fars = tie((density, two, nears, fars))
    mine = gather_near(density)
    two = add_second(two, nears, [fars[j] for j in range(groups)])
    mine, two = tie((mine, two))
    right_side = own_part(excitation[2]) - sum_parts(multiply(first_columns, mine, two))

    right_side, results = tie((right_side, results))
    mine = gather_near(right_side)
    early = whole_rows(jnp.stack(results))
    mine, early = tie((mine, early))
    density = sum_parts(multiply(head_columns, mine, nothing))
    return jnp.concatenate([early, whole_rows(density[None])], axis=0)


def solution(mesh):
    placed = (P("lag", "row", None), P("row", None), P(None, "row", None), P("lag", "row", None))

    return jax.shard_map(on_device, mesh=mesh, in_specs=placed, out_specs=P(None, "row", None), check_vma=False)
```

```python
import jax
import jax.numpy as jnp
from jax import lax
from jax.experimental import pallas as pl
from jax.experimental.pallas import tpu as pltpu
from jax.sharding import PartitionSpec as P


STEPS = 3
F32 = jnp.float32
BF16 = jnp.bfloat16


def split(value):
    high = value.astype(BF16)
    return high, (value - high.astype(F32)).astype(BF16)


def dot(a, b):
    return jnp.dot(a, b, preferred_element_type=F32)


def product(weight, vectors):
    count, width = len(vectors), vectors[0].shape[1]
    wh, wl = split(weight)
    highs, lows = zip(*(split(v) for v in vectors))
    main = dot(wh, jnp.concatenate(highs + lows, axis=1))
    rest = dot(wl, jnp.concatenate(highs, axis=1) if count > 1 else highs[0])
    return main[:, : count * width] + main[:, count * width :] + rest


def ordered(core, near, far):
    return jnp.concatenate([jnp.where(core == 0, near, far), jnp.where(core == 0, far, near)], axis=0)


def chip_kernel(where, weights, *refs):
    outs, tail, high, low = refs[-STEPS - 3 : -3], *refs[-3:]
    pieces = refs[: len(refs) - STEPS - 3]
    totals = pieces[len(pieces) - STEPS :] if len(pieces) % 2 else []
    number, at = pl.program_id(0), pl.program_id(1)
    lags, rows, width = pieces[0].shape
    core = where[0]

    @pl.when(jnp.logical_and(number == 0, at == 0))
    def _():
        for n, out in enumerate(outs):
            out[...] = totals[n][...] if totals else jnp.zeros_like(out)

    count = len(pieces) // 2 - (1 if totals else 0)

    @pl.when(jnp.logical_and(number == count - 1, at == 0))
    def _():
        tail[...] = pieces[2 * count - 2][lags - tail.shape[0] :]

    for i in range(count):

        @pl.when(jnp.logical_and(number == i, at == 0))
        def _():
            for k in range(lags):
                columns = slice((lags - 1 - k) * width, (lags - k) * width)
                for piece, side in ((pieces[2 * i], core), (pieces[2 * i + 1], 1 - core)):
                    here = pl.ds(pl.multiple_of(side * rows, rows), rows)
                    high[here, columns], low[here, columns] = split(piece[k])

    for k in range(STEPS):

        @pl.when(at == k if k + 1 < STEPS else at >= k)
        def _():
            size = (k + 1) * width
            columns = pl.ds(pl.multiple_of((lags - 1 - at) * width, width), size)
            wh, wl = split(weights[0])
            h = high[:, columns]
            main = dot(wh, jnp.concatenate([h, low[:, columns]], axis=1))
            result = main[:, :size] + main[:, size:] + dot(wl, h)
            for n in range(k + 1):
                outs[n][...] += result[:, n * width : (n + 1) * width]


def first_kernel(where, weights, near, far, total, out, tail):
    @pl.when(pl.program_id(0) == 0)
    def _():
        out[...] = total[...]

    tail[...] = near[...]
    out[...] += product(weights[0], [ordered(where[0], near[0], far[0])])


def rest_kernel(where, weights, near, near_before, far, far_before, one, two, one_out, two_out):
    at = pl.program_id(0)
    width = near.shape[-1]
    now = ordered(where[0], near[0], far[0])

    @pl.when(at == 0)
    def _():
        one_out[...] = one[...] + product(weights[0], [now])
        two_out[...] = two[...]

    @pl.when(at > 0)
    def _():
        result = product(weights[0], [now, ordered(where[0], near_before[0], far_before[0])])
        one_out[...] += result[:, :width]
        two_out[...] += result[:, width:]


def entered_kernel(where, weights, *refs):
    pieces, (one, two, one_out, two_out, high, low) = refs[:-6], refs[-6:]
    number, at = pl.program_id(0), pl.program_id(1)
    before, rows, width = pieces[0].shape

    @pl.when(jnp.logical_and(number == 0, at == 0))
    def _():
        one_out[...] = one[...]
        two_out[...] = two[...]

    for i in range(len(pieces) // 2):

        @pl.when(jnp.logical_and(number == i, at == 0))
        def _():
            for k in range(before):
                columns = slice((before - 1 - k) * width, (before - k) * width)
                for piece, side in ((pieces[2 * i], where[0]), (pieces[2 * i + 1], 1 - where[0])):
                    here = pl.ds(pl.multiple_of(side * rows, rows), rows)
                    high[here, columns], low[here, columns] = split(piece[k])

    for k in range(before):

        @pl.when(jnp.logical_and(where[1] > 0, at == k))
        def _():
            size = (before - k) * width
            wh, wl = split(weights[0])
            h = high[:, :size]
            main = dot(wh, jnp.concatenate([h, low[:, :size]], axis=1))
            result = main[:, :size] + main[:, size:] + dot(wl, h)
            if k == 0:
                one_out[...] += result[:, :width]
            two_out[...] += result[:, size - width :]


def second_kernel(where, weights, *refs):
    nears, fars, total, out = refs[: len(refs) // 2 - 1], refs[len(refs) // 2 - 1 : -2], refs[-2], refs[-1]

    @pl.when(pl.program_id(0) == 0)
    def _():
        out[...] = total[...]

    @pl.when(where[1] == 0)
    def _():
        near, far = (jnp.concatenate([p[...] for p in parts], axis=0) for parts in (nears, fars))
        out[...] += product(weights[0], [ordered(where[0], near, far)])


def columns_kernel(where, *refs):
    fold, groups = where.shape[1] - 1, where.shape[2]
    sources, outs = refs[:fold], refs[fold:]
    part = sources[0].shape[2] // groups
    take = lambda j: jnp.concatenate([s[0, :, j * part : (j + 1) * part] for s in sources], axis=1)
    if len(outs) == 1:
        for j in range(groups):

            @pl.when(where[0, fold, 0] == j)
            def _():
                outs[0][...] = take(j)

        return
    for j in range(groups - 1):
        outs[j][...] = take(j)
    for side, out in enumerate(outs[groups - 1 :]):

        @pl.when(pl.program_id(0) == side)
        def _():
            out[...] = take(groups - 1)


def pick_kernel(which, *refs):
    sources, out = refs[:-1], refs[-1]
    groups = len(sources) - 1
    for j, source in enumerate(sources):
        chosen = which[0] == min(j, groups - 1)
        if j >= groups - 1:
            chosen = jnp.logical_and(chosen, pl.program_id(0) == j - groups + 1)

        @pl.when(chosen)
        def _():
            out[...] = source[...]


def call(kernel, where, grid, operands, specs, count, shape, cost, aliases={}, scratch=()):
    return pl.pallas_call(
        kernel,
        out_shape=[jax.ShapeDtypeStruct(shape, F32)] * count,
        grid_spec=pltpu.PrefetchScalarGridSpec(
            num_scalar_prefetch=1, grid=grid, in_specs=specs, out_specs=[all_of(shape)] * count, scratch_shapes=scratch
        ),
        input_output_aliases=aliases,
        cost_estimate=pl.CostEstimate(flops=cost[0], bytes_accessed=cost[1], transcendentals=0),
        compiler_params=pltpu.CompilerParams(dimension_semantics=("arbitrary",) * len(grid)),
    )(where, *operands)


def all_of(shape):
    return pl.BlockSpec(shape, lambda *_: (0,) * len(shape))


def on_device(lag_weights, inverse_head, excitation, history):
    groups, devices = lax.axis_size("lag"), lax.axis_size("row")
    group, at = lax.axis_index("lag"), lax.axis_index("row")
    chips = devices // 2
    chip, core = at // 2, at % 2
    lags, rows, order = lag_weights.shape
    width = history.shape[-1]
    part = rows // groups
    tile = rows * 2 * rows
    square = (rows, width)
    tie = lax.optimization_barrier

    def pairs(axis_size, mask):
        return [(i, i ^ mask) for i in range(axis_size)]

    def other_core(value):
        return lax.ppermute(value, "row", pairs(devices, 1))

    def along(value, step, sources):
        return lax.ppermute(value, "row", [(2 * i + c, 2 * (i + step) + c) for i in sources for c in (0, 1)])

    def go_up(value, hop):
        return along(value, 1, range(hop - 1, chips - 1))

    def go_down(value, hop):
        return along(value, -1, range(1, chips - hop + 1))

    def taken(z, stage):
        both = min(z, chips - 1 - z)
        if stage <= 2 * both:
            return (stage + 1) // 2, stage % 2 == 1
        return stage - both, z >= stage - both

    def by_chip(values):
        result = jnp.int32(values[0])
        for z in range(1, chips):
            result = jnp.where(chip == z, values[z], result)
        return result

    def source_of(stage):
        return by_chip([z + (-h if u else h) for z in range(chips) for h, u in [taken(z, stage)]])

    def choose(stage, ups, downs):
        found = sorted({taken(z, stage) for z in range(chips)})
        arrays = [(ups if u else downs)[h] for h, u in found]
        return lax.select_n(by_chip([found.index(taken(z, stage)) for z in range(chips)]), *arrays) if len(found) > 1 else arrays[0]

    stages = [chip] + [source_of(stage) for stage in range(1, chips)]
    xored = [chip ^ k for k in range(chips)]
    where = jnp.stack([core, group, *stages, *xored]).astype(jnp.int32)

    def weight_spec(stage, first=0):
        return pl.BlockSpec((1, rows, 2 * rows), lambda k, w: (k + first, 0, w[2 + stage]))

    def lag_spec(shift):
        return pl.BlockSpec((1, rows, width), lambda k, w: (jnp.maximum(k + shift, 0), 0, 0))

    def add_chip(totals, pieces, stage):
        count = len(pieces) // 2
        before = (STEPS - 1, *square)
        *totals, tail = pl.pallas_call(
            chip_kernel,
            out_shape=[jax.ShapeDtypeStruct(square, F32)] * STEPS + [jax.ShapeDtypeStruct(before, F32)],
            grid_spec=pltpu.PrefetchScalarGridSpec(
                num_scalar_prefetch=1,
                grid=(count, lags),
                in_specs=[pl.BlockSpec((1, rows, 2 * rows), lambda i, k, w: (k, 0, w[2 + stage + i]))]
                + [all_of(v.shape) for v in (*pieces, *totals)],
                out_specs=[all_of(square)] * STEPS + [all_of(before)],
                scratch_shapes=[pltpu.VMEM((2 * rows, lags * width), BF16)] * 2,
            ),
            input_output_aliases={2 + len(pieces) + n: n for n in range(len(totals))},
            cost_estimate=pl.CostEstimate(flops=18 * count * lags * tile * width, bytes_accessed=4 * count * lags * tile, transcendentals=0),
            compiler_params=pltpu.CompilerParams(dimension_semantics=("arbitrary", "arbitrary")),
            name="chip",
        )(where, lag_weights, *pieces, *totals)
        return totals, tail

    def add_first(total, near, far, stage):
        before = STEPS - 1
        return pl.pallas_call(
            first_kernel,
            out_shape=[jax.ShapeDtypeStruct(square, F32), jax.ShapeDtypeStruct((before, *square), F32)],
            grid_spec=pltpu.PrefetchScalarGridSpec(
                num_scalar_prefetch=1,
                grid=(lags,),
                in_specs=[weight_spec(stage), lag_spec(0), lag_spec(0), all_of(square)],
                out_specs=[all_of(square), pl.BlockSpec((1, *square), lambda k, w: (jnp.maximum(k + before - lags, 0), 0, 0))],
            ),
            input_output_aliases={4: 0},
            cost_estimate=pl.CostEstimate(flops=6 * lags * tile * width, bytes_accessed=4 * lags * tile, transcendentals=0),
            compiler_params=pltpu.CompilerParams(dimension_semantics=("arbitrary",)),
            name="first",
        )(where, lag_weights, near, far, total)

    def add_rest(one, two, near, far, stage):
        return call(
            rest_kernel, where, (lags - 1,), (lag_weights, near, near, far, far, one, two),
            [weight_spec(stage, 1), lag_spec(0), lag_spec(-1), lag_spec(0), lag_spec(-1), all_of(square), all_of(square)],
            2, square, (12 * lags * tile * width, 4 * lags * tile), {6: 0, 7: 1},
        )

    def add_entered(one, two, nears, stage):
        pieces = [v for near in nears for v in (near, other_core(near))]
        spec = pl.BlockSpec((1, rows, 2 * rows), lambda i, k, w: (jnp.where(w[1] > 0, k, 0), 0, jnp.where(w[1] > 0, w[2 + stage + i], 0)))
        return call(
            entered_kernel, where, (len(nears), STEPS - 1), (lag_weights, *pieces, one, two),
            [spec] + [all_of(v.shape) for v in (*pieces, one, two)],
            2, square, (18 * len(nears) * tile * width, 8 * len(nears) * tile), {2 + len(pieces): 0, 3 + len(pieces): 1},
            [pltpu.VMEM((2 * rows, (STEPS - 1) * width), BF16)] * 2,
        )

    def add_second(total, nears, fars):
        block = pl.BlockSpec((part, width), lambda k, w: (k, 0))
        return call(
            second_kernel, where, (chips,), (lag_weights, *nears, *fars, total),
            [pl.BlockSpec((1, rows, 2 * rows), lambda k, w: (1, 0, jnp.where(w[1] == 0, w[2 + chips + k], 0)))]
            + [block] * 2 * groups + [all_of(square)],
            1, square, (6 * rows * order * width, 4 * rows * order), {2 + 2 * groups: 0},
        )[0]

    slots = jnp.stack([(chip ^ k) * 2 + (core ^ h) for h in (0, 1) for k in range(chips)]).astype(jnp.int32)
    meet = devices * part

    def columns(matrix, every):
        fold = devices // 2
        numbers = jnp.tile(slots.reshape(2, fold, 1), (1, 1, groups))
        numbers = jnp.concatenate([numbers, jnp.full((2, 1, groups), group, jnp.int32)], axis=1)
        whole = pl.BlockSpec((rows, meet // 2), lambda s, w: (0, s))
        half = pl.BlockSpec((rows, meet // 2), lambda s, w: (0, 0))
        shape = lambda size: jax.ShapeDtypeStruct((rows, size), F32)
        return pl.pallas_call(
            columns_kernel,
            out_shape=[shape(meet)] * (groups - 1) + [shape(meet // 2)] * 2 if every else [shape(meet)],
            grid_spec=pltpu.PrefetchScalarGridSpec(
                num_scalar_prefetch=1,
                grid=(2,),
                in_specs=[pl.BlockSpec((1, rows, rows), lambda s, w, i=i: (0, 0, w[s, i, 0])) for i in range(fold)],
                out_specs=[whole] * (groups - 1) + [half] * 2 if every else [whole],
            ),
            cost_estimate=pl.CostEstimate(flops=0, bytes_accessed=8 * rows * order, transcendentals=0),
            compiler_params=pltpu.CompilerParams(dimension_semantics=("arbitrary",)),
            name="columns",
        )(numbers, *[matrix] * fold)

    def pick(matrices):
        spec = lambda j: pl.BlockSpec((rows, meet // 2), lambda s, w: (0, jnp.where(w[0] == j, s, 0)))
        return pl.pallas_call(
            pick_kernel,
            out_shape=jax.ShapeDtypeStruct((rows, meet), F32),
            grid_spec=pltpu.PrefetchScalarGridSpec(
                num_scalar_prefetch=1,
                grid=(2,),
                in_specs=[spec(j) for j in range(groups - 1)] + [all_of((rows, meet // 2))] * 2,
                out_specs=pl.BlockSpec((rows, meet // 2), lambda s, w: (0, s)),
            ),
            cost_estimate=pl.CostEstimate(flops=0, bytes_accessed=16 * rows * meet, transcendentals=0),
            compiler_params=pltpu.CompilerParams(dimension_semantics=("arbitrary",)),
            name="pick",
        )(group.astype(jnp.int32).reshape(1), *matrices)

    def gather_near(value):
        pieces = [value] + [lax.ppermute(value, "row", pairs(devices, 2 * k)) for k in range(1, chips)]
        return jnp.concatenate(pieces, axis=0)

    def own_part(value):
        return lax.dynamic_slice(value, (group * part, 0), (part, value.shape[1]))

    def sum_parts(value):
        result = own_part(value)
        for mask in range(1, groups):
            sent = lax.dynamic_slice(value, ((group ^ mask) * part, 0), (part, width))
            result = result + lax.ppermute(sent, "lag", pairs(groups, mask))
        return result

    def whole_rows(value):
        pieces = [value] + [lax.ppermute(value, "lag", pairs(groups, mask)) for mask in range(1, groups)]
        return jnp.concatenate([lax.select_n(group ^ i, *pieces) for i in range(groups)], axis=1)

    def enter(tail):
        return lax.ppermute(tail, "lag", [(i, i + 1) for i in range(groups - 1)])

    def multiply(matrix, mine):
        vector = jnp.concatenate([mine, other_core(mine)], axis=0)
        return jnp.dot(matrix, vector, precision=lax.Precision.HIGH)

    ups, downs = {1: go_up(history, 1)}, {1: go_down(history, 1)}
    tail = history[lags - (STEPS - 1) :]
    entered = [enter(jnp.where(group >= 0, tail, 0.0))]
    own_far = other_core(history)
    *chunks, last_near, last_far = columns(lag_weights, True)
    relayed = lax.ppermute(last_far, "lag", [(0, groups // 2)])
    sent = [lax.ppermute(chunks[j], "lag", [(0, j)]) for j in range(1, groups - 1)]
    (head_columns,) = columns(inverse_head[None], False)
    ups[1], downs[1], entered, own_far, head_columns = tie((ups[1], downs[1], entered, own_far, head_columns))
    totals, waiting = [], []
    for stage in range(1, chips - 1):
        next_up, next_down = go_up(ups[stage], stage + 1), go_down(downs[stage], stage + 1)
        near = choose(stage, ups, downs)
        if stage == chips - 2:
            relayed, near = tie((relayed, near))
            sent.append(lax.ppermute(relayed, "lag", [(groups // 2, groups - 1)]))
        pieces = [near, other_core(near)]
        if stage == 1:
            pieces = [history, own_far, *pieces]
        totals, tail = add_chip(totals, pieces, stage if stage > 1 else 0)
        if stage < chips - 2:
            entered.append(enter(tail))
            if stage == 1:
                last_near, tail = tie((last_near, tail))
                late = lax.ppermute(last_near, "lag", [(0, groups - 1)])
                sent.append(late)
        else:
            waiting.append(tail)
            totals = [totals[0], *add_entered(totals[1], totals[2], entered[:1], 0)]
        ups[stage + 1], downs[stage + 1] = next_up, next_down
        ups, downs, totals = tie((ups, downs, totals))
    first, one, two = totals

    near = choose(chips - 1, ups, downs)
    far = other_core(near)
    first, tail = add_first(first, near, far, chips - 1)

    right_side = own_part(excitation[0]) - sum_parts(first)
    right_side, waiting, tail, near, far, one, two = tie((right_side, waiting, tail, near, far, one, two))
    mine = gather_near(right_side)
    entered += [enter(value) for value in (*waiting, tail)]
    one, two = add_rest(one, two, near, far, chips - 1)
    mine, one, two, sent = tie((mine, one, two, sent))
    density = sum_parts(multiply(head_columns, mine))
    first_columns = pick([chunks[0], *sent])
    results = [density]

    density, first_columns, entered, one, two = tie((density, first_columns, entered, one, two))
    mine = gather_near(density)
    one, two = add_entered(one, two, entered[1:], 1)
    mine, one, two = tie((mine, one, two))
    right_side = own_part(excitation[1]) - sum_parts(one + multiply(first_columns, mine))

    right_side, two, old = tie((right_side, two, mine))
    mine = gather_near(right_side)
    nears = [old] + [lax.ppermute(old, "lag", [(j, 0)]) for j in range(1, groups)]
    mine, two, nears = tie((mine, two, nears))
    density = sum_parts(multiply(head_columns, mine))
    fars = other_core(jnp.stack(nears))
    results.append(density)

    density, two, nears, fars = tie((density, two, nears, fars))
    mine = gather_near(density)
    two = add_second(two, nears, [fars[j] for j in range(groups)])
    mine, two = tie((mine, two))
    right_side = own_part(excitation[2]) - sum_parts(two + multiply(first_columns, mine))

    right_side, results = tie((right_side, results))
    mine = gather_near(right_side)
    early = whole_rows(jnp.stack(results))
    mine, early = tie((mine, early))
    density = sum_parts(multiply(head_columns, mine))
    return jnp.concatenate([early, whole_rows(density[None])], axis=0)


def solution(mesh):
    placed = (P("lag", "row", None), P("row", None), P(None, "row", None), P("lag", "row", None))

    return jax.shard_map(on_device, mesh=mesh, in_specs=placed, out_specs=P(None, "row", None), check_vma=False)
```

```python
import jax
import jax.numpy as jnp
from jax import lax
from jax.experimental import pallas as pl
from jax.experimental.pallas import tpu as pltpu
from jax.sharding import PartitionSpec as P


STEPS = 3
F32 = jnp.float32
BF16 = jnp.bfloat16


def split(value):
    high = value.astype(BF16)
    return high, (value - high.astype(F32)).astype(BF16)


def dot(a, b):
    return jnp.dot(a, b, preferred_element_type=F32)


def product(weight, vectors):
    count, width = len(vectors), vectors[0].shape[1]
    wh, wl = split(weight)
    highs, lows = zip(*(split(v) for v in vectors))
    main = dot(wh, jnp.concatenate(highs + lows, axis=1))
    rest = dot(wl, jnp.concatenate(highs, axis=1) if count > 1 else highs[0])
    return main[:, : count * width] + main[:, count * width :] + rest


def ordered(core, near, far):
    return jnp.concatenate([jnp.where(core == 0, near, far), jnp.where(core == 0, far, near)], axis=0)


def chip_kernel(where, weights, *refs):
    outs, tail, high, low = refs[-STEPS - 3 : -3], *refs[-3:]
    pieces = refs[: len(refs) - STEPS - 3]
    totals = pieces[len(pieces) - STEPS :] if len(pieces) % 2 else []
    number, at = pl.program_id(0), pl.program_id(1)
    lags, rows, width = pieces[0].shape
    core = where[0]

    @pl.when(jnp.logical_and(number == 0, at == 0))
    def _():
        for n, out in enumerate(outs):
            out[...] = totals[n][...] if totals else jnp.zeros_like(out)

    count = len(pieces) // 2 - (1 if totals else 0)

    @pl.when(jnp.logical_and(number == count - 1, at == 0))
    def _():
        tail[...] = pieces[2 * count - 2][lags - tail.shape[0] :]

    for i in range(count):

        @pl.when(jnp.logical_and(number == i, at == 0))
        def _():
            for k in range(lags):
                columns = slice((lags - 1 - k) * width, (lags - k) * width)
                for piece, side in ((pieces[2 * i], core), (pieces[2 * i + 1], 1 - core)):
                    here = pl.ds(pl.multiple_of(side * rows, rows), rows)
                    high[here, columns], low[here, columns] = split(piece[k])

    for k in range(STEPS):

        @pl.when(at == k if k + 1 < STEPS else at >= k)
        def _():
            size = (k + 1) * width
            columns = pl.ds(pl.multiple_of((lags - 1 - at) * width, width), size)
            wh, wl = split(weights[0])
            h = high[:, columns]
            main = dot(wh, jnp.concatenate([h, low[:, columns]], axis=1))
            result = main[:, :size] + main[:, size:] + dot(wl, h)
            for n in range(k + 1):
                outs[n][...] += result[:, n * width : (n + 1) * width]


def first_kernel(where, weights, near, far, total, out, tail):
    @pl.when(pl.program_id(0) == 0)
    def _():
        out[...] = total[...]

    tail[...] = near[...]
    out[...] += product(weights[0], [ordered(where[0], near[0], far[0])])


def rest_kernel(where, weights, near, near_before, far, far_before, one, two, one_out, two_out):
    at = pl.program_id(0)
    width = near.shape[-1]
    now = ordered(where[0], near[0], far[0])

    @pl.when(at == 0)
    def _():
        one_out[...] = one[...] + product(weights[0], [now])
        two_out[...] = two[...]

    @pl.when(at > 0)
    def _():
        result = product(weights[0], [now, ordered(where[0], near_before[0], far_before[0])])
        one_out[...] += result[:, :width]
        two_out[...] += result[:, width:]


def entered_kernel(where, weights, *refs):
    pieces, (one, two, one_out, two_out) = refs[:-4], refs[-4:]
    number = pl.program_id(0)
    width = pieces[0].shape[2]

    @pl.when(number == 0)
    def _():
        one_out[...] = one[...]
        two_out[...] = two[...]

    for i in range(len(pieces) // 2):

        @pl.when(jnp.logical_and(where[1] > 0, number == i))
        def _():
            near, far = pieces[2 * i : 2 * i + 2]
            result = product(weights[0], [ordered(where[0], near[k], far[k]) for k in (1, 0)])
            one_out[...] += result[:, :width]
            two_out[...] += result[:, width:]


def second_kernel(where, weights, *refs):
    (fars, total, out, vector), operands = refs[-4:], refs[:-4]
    groups = fars.shape[0]
    chips = (len(operands) - groups) // 2
    nears, pieces = operands[:groups], operands[groups:]
    rows, number = vector.shape[0] // 2, pl.program_id(0)
    part = rows // groups

    @pl.when(number == 0)
    def _():
        out[...] = total[...]

    @pl.when(where[1] == 0)
    def _():
        here = pl.ds(pl.multiple_of(number * part, part), part)
        near = jnp.concatenate([p[here, :] for p in nears], axis=0)
        far = jnp.concatenate([fars[j, here, :] for j in range(groups)], axis=0)
        vector[...] = ordered(where[0], near, far)

    for i in range(chips):

        @pl.when(jnp.logical_and(where[1] > 0, number == i))
        def _():
            vector[...] = ordered(where[0], pieces[2 * i][0], pieces[2 * i + 1][0])

    out[...] += product(weights[0], [vector[...]])


def columns_kernel(where, *refs):
    fold, groups = where.shape[1] - 1, where.shape[2]
    sources, outs = refs[:fold], refs[fold:]
    part = sources[0].shape[2] // groups
    take = lambda j: jnp.concatenate([s[0, :, j * part : (j + 1) * part] for s in sources], axis=1)
    if len(outs) == 1:
        for j in range(groups):

            @pl.when(where[0, fold, 0] == j)
            def _():
                outs[0][...] = take(j)

        return
    for j in range(groups - 1):
        outs[j][...] = take(j)
    for side, out in enumerate(outs[groups - 1 :]):

        @pl.when(pl.program_id(0) == side)
        def _():
            out[...] = take(groups - 1)


def pick_kernel(which, *refs):
    sources, out = refs[:-1], refs[-1]
    groups = len(sources) - 1
    for j, source in enumerate(sources):
        chosen = which[0] == min(j, groups - 1)
        if j >= groups - 1:
            chosen = jnp.logical_and(chosen, pl.program_id(0) == j - groups + 1)

        @pl.when(chosen)
        def _():
            out[...] = source[...]


def call(kernel, where, grid, operands, specs, count, shape, cost, aliases={}, scratch=()):
    return pl.pallas_call(
        kernel,
        out_shape=[jax.ShapeDtypeStruct(shape, F32)] * count,
        grid_spec=pltpu.PrefetchScalarGridSpec(
            num_scalar_prefetch=1, grid=grid, in_specs=specs, out_specs=[all_of(shape)] * count, scratch_shapes=scratch
        ),
        input_output_aliases=aliases,
        cost_estimate=pl.CostEstimate(flops=cost[0], bytes_accessed=cost[1], transcendentals=0),
        compiler_params=pltpu.CompilerParams(dimension_semantics=("arbitrary",) * len(grid)),
    )(where, *operands)


def all_of(shape):
    return pl.BlockSpec(shape, lambda *_: (0,) * len(shape))


def on_device(lag_weights, inverse_head, excitation, history):
    groups, devices = lax.axis_size("lag"), lax.axis_size("row")
    group, at = lax.axis_index("lag"), lax.axis_index("row")
    chips = devices // 2
    chip, core = at // 2, at % 2
    lags, rows, order = lag_weights.shape
    width = history.shape[-1]
    part = rows // groups
    tile = rows * 2 * rows
    square = (rows, width)
    tie = lax.optimization_barrier

    def pairs(axis_size, mask):
        return [(i, i ^ mask) for i in range(axis_size)]

    def other_core(value):
        return lax.ppermute(value, "row", pairs(devices, 1))

    def along(value, step, sources):
        return lax.ppermute(value, "row", [(2 * i + c, 2 * (i + step) + c) for i in sources for c in (0, 1)])

    def go_up(value, hop):
        return along(value, 1, range(hop - 1, chips - 1))

    def go_down(value, hop):
        return along(value, -1, range(1, chips - hop + 1))

    def taken(z, stage):
        both = min(z, chips - 1 - z)
        if stage <= 2 * both:
            return (stage + 1) // 2, stage % 2 == 1
        return stage - both, z >= stage - both

    def by_chip(values):
        result = jnp.int32(values[0])
        for z in range(1, chips):
            result = jnp.where(chip == z, values[z], result)
        return result

    def source_of(stage):
        return by_chip([z + (-h if u else h) for z in range(chips) for h, u in [taken(z, stage)]])

    def choose(stage, ups, downs):
        found = sorted({taken(z, stage) for z in range(chips)})
        arrays = [(ups if u else downs)[h] for h, u in found]
        return lax.select_n(by_chip([found.index(taken(z, stage)) for z in range(chips)]), *arrays) if len(found) > 1 else arrays[0]

    stages = [chip] + [source_of(stage) for stage in range(1, chips)]
    xored = [chip ^ k for k in range(chips)]
    where = jnp.stack([core, group, *stages, *xored]).astype(jnp.int32)

    def weight_spec(stage, first=0):
        return pl.BlockSpec((1, rows, 2 * rows), lambda k, w: (k + first, 0, w[2 + stage]))

    def lag_spec(shift):
        return pl.BlockSpec((1, rows, width), lambda k, w: (jnp.maximum(k + shift, 0), 0, 0))

    def add_chip(totals, pieces, stage):
        count = len(pieces) // 2
        before = (STEPS - 1, *square)
        *totals, tail = pl.pallas_call(
            chip_kernel,
            out_shape=[jax.ShapeDtypeStruct(square, F32)] * STEPS + [jax.ShapeDtypeStruct(before, F32)],
            grid_spec=pltpu.PrefetchScalarGridSpec(
                num_scalar_prefetch=1,
                grid=(count, lags),
                in_specs=[pl.BlockSpec((1, rows, 2 * rows), lambda i, k, w: (k, 0, w[2 + stage + i]))]
                + [all_of(v.shape) for v in (*pieces, *totals)],
                out_specs=[all_of(square)] * STEPS + [all_of(before)],
                scratch_shapes=[pltpu.VMEM((2 * rows, lags * width), BF16)] * 2,
            ),
            input_output_aliases={2 + len(pieces) + n: n for n in range(len(totals))},
            cost_estimate=pl.CostEstimate(flops=18 * count * lags * tile * width, bytes_accessed=4 * count * lags * tile, transcendentals=0),
            compiler_params=pltpu.CompilerParams(dimension_semantics=("arbitrary", "arbitrary")),
            name="chip",
        )(where, lag_weights, *pieces, *totals)
        return totals, tail

    def add_first(total, near, far, stage):
        before = STEPS - 1
        return pl.pallas_call(
            first_kernel,
            out_shape=[jax.ShapeDtypeStruct(square, F32), jax.ShapeDtypeStruct((before, *square), F32)],
            grid_spec=pltpu.PrefetchScalarGridSpec(
                num_scalar_prefetch=1,
                grid=(lags,),
                in_specs=[weight_spec(stage), lag_spec(0), lag_spec(0), all_of(square)],
                out_specs=[all_of(square), pl.BlockSpec((1, *square), lambda k, w: (jnp.maximum(k + before - lags, 0), 0, 0))],
            ),
            input_output_aliases={4: 0},
            cost_estimate=pl.CostEstimate(flops=6 * lags * tile * width, bytes_accessed=4 * lags * tile, transcendentals=0),
            compiler_params=pltpu.CompilerParams(dimension_semantics=("arbitrary",)),
            name="first",
        )(where, lag_weights, near, far, total)

    def add_rest(one, two, near, far, stage):
        return call(
            rest_kernel, where, (lags - 1,), (lag_weights, near, near, far, far, one, two),
            [weight_spec(stage, 1), lag_spec(0), lag_spec(-1), lag_spec(0), lag_spec(-1), all_of(square), all_of(square)],
            2, square, (12 * lags * tile * width, 4 * lags * tile), {6: 0, 7: 1},
        )

    def add_entered(one, two, pieces, stage):
        count = len(pieces) // 2
        spec = pl.BlockSpec((1, rows, 2 * rows), lambda i, w: (0, 0, jnp.where(w[1] > 0, w[2 + stage + i], 0)))
        return call(
            entered_kernel, where, (count,), (lag_weights, *pieces, one, two),
            [spec] + [all_of(v.shape) for v in (*pieces, one, two)],
            2, square, (12 * count * tile * width, 4 * count * tile), {2 + len(pieces): 0, 3 + len(pieces): 1},
        )

    def add_second(total, nears, pieces, fars):
        spec = pl.BlockSpec((1, rows, 2 * rows), lambda i, w: (1, 0, w[2 + i + jnp.where(w[1] == 0, chips, 0)]))
        last = pl.BlockSpec((1, rows, width), lambda i, w: (STEPS - 2, 0, 0))
        return call(
            second_kernel, where, (chips,), (lag_weights, *nears, *pieces, fars, total),
            [spec] + [all_of(v.shape) for v in nears] + [last] * len(pieces) + [all_of(fars.shape), all_of(square)],
            1, square, (6 * rows * order * width, 4 * rows * order), {3 + len(nears) + len(pieces): 0},
            [pltpu.VMEM((2 * rows, width), F32)],
        )[0]

    slots = jnp.stack([(chip ^ k) * 2 + (core ^ h) for h in (0, 1) for k in range(chips)]).astype(jnp.int32)
    meet = devices * part

    def columns(matrix, every):
        fold = devices // 2
        numbers = jnp.tile(slots.reshape(2, fold, 1), (1, 1, groups))
        numbers = jnp.concatenate([numbers, jnp.full((2, 1, groups), group, jnp.int32)], axis=1)
        whole = pl.BlockSpec((rows, meet // 2), lambda s, w: (0, s))
        half = pl.BlockSpec((rows, meet // 2), lambda s, w: (0, 0))
        shape = lambda size: jax.ShapeDtypeStruct((rows, size), F32)
        return pl.pallas_call(
            columns_kernel,
            out_shape=[shape(meet)] * (groups - 1) + [shape(meet // 2)] * 2 if every else [shape(meet)],
            grid_spec=pltpu.PrefetchScalarGridSpec(
                num_scalar_prefetch=1,
                grid=(2,),
                in_specs=[pl.BlockSpec((1, rows, rows), lambda s, w, i=i: (0, 0, w[s, i, 0])) for i in range(fold)],
                out_specs=[whole] * (groups - 1) + [half] * 2 if every else [whole],
            ),
            cost_estimate=pl.CostEstimate(flops=0, bytes_accessed=8 * rows * order, transcendentals=0),
            compiler_params=pltpu.CompilerParams(dimension_semantics=("arbitrary",)),
            name="columns",
        )(numbers, *[matrix] * fold)

    def pick(matrices):
        spec = lambda j: pl.BlockSpec((rows, meet // 2), lambda s, w: (0, jnp.where(w[0] == j, s, 0)))
        return pl.pallas_call(
            pick_kernel,
            out_shape=jax.ShapeDtypeStruct((rows, meet), F32),
            grid_spec=pltpu.PrefetchScalarGridSpec(
                num_scalar_prefetch=1,
                grid=(2,),
                in_specs=[spec(j) for j in range(groups - 1)] + [all_of((rows, meet // 2))] * 2,
                out_specs=pl.BlockSpec((rows, meet // 2), lambda s, w: (0, s)),
            ),
            cost_estimate=pl.CostEstimate(flops=0, bytes_accessed=16 * rows * meet, transcendentals=0),
            compiler_params=pltpu.CompilerParams(dimension_semantics=("arbitrary",)),
            name="pick",
        )(group.astype(jnp.int32).reshape(1), *matrices)

    def gather_near(value):
        pieces = [value] + [lax.ppermute(value, "row", pairs(devices, 2 * k)) for k in range(1, chips)]
        return jnp.concatenate(pieces, axis=0)

    def own_part(value):
        return lax.dynamic_slice(value, (group * part, 0), (part, value.shape[1]))

    def sum_parts(value):
        result = own_part(value)
        for mask in range(1, groups):
            sent = lax.dynamic_slice(value, ((group ^ mask) * part, 0), (part, width))
            result = result + lax.ppermute(sent, "lag", pairs(groups, mask))
        return result

    def whole_rows(value):
        pieces = [value] + [lax.ppermute(value, "lag", pairs(groups, mask)) for mask in range(1, groups)]
        return jnp.concatenate([lax.select_n(group ^ i, *pieces) for i in range(groups)], axis=1)

    def enter(tail):
        return lax.ppermute(tail, "lag", [(i, i + 1) for i in range(groups - 1)])

    def multiply(matrix, mine):
        vector = jnp.concatenate([mine, other_core(mine)], axis=0)
        return jnp.dot(matrix, vector, precision=lax.Precision.HIGH)

    ups, downs = {1: go_up(history, 1)}, {1: go_down(history, 1)}
    tail = history[lags - (STEPS - 1) :]
    entered = [enter(jnp.where(group >= 0, tail, 0.0))]
    own_far = other_core(history)
    *chunks, last_near, last_far = columns(lag_weights, True)
    relayed = lax.ppermute(last_far, "lag", [(0, groups // 2)])
    sent = [lax.ppermute(chunks[j], "lag", [(0, j)]) for j in range(1, groups - 1)]
    (head_columns,) = columns(inverse_head[None], False)
    ups[1], downs[1], entered, own_far, head_columns = tie((ups[1], downs[1], entered, own_far, head_columns))
    totals = []
    for stage in range(1, chips - 1):
        next_up, next_down = go_up(ups[stage], stage + 1), go_down(downs[stage], stage + 1)
        near = choose(stage, ups, downs)
        if stage == chips - 2:
            relayed, near = tie((relayed, near))
            sent.append(lax.ppermute(relayed, "lag", [(groups // 2, groups - 1)]))
        pieces = [near, other_core(near)]
        if stage == 1:
            pieces = [history, own_far, *pieces]
        totals, tail = add_chip(totals, pieces, stage if stage > 1 else 0)
        entered.append(enter(tail))
        if stage == 1:
            last_near, tail = tie((last_near, tail))
            sent.append(lax.ppermute(last_near, "lag", [(0, groups - 1)]))
        if stage == chips - 2:
            both = [entered[0], other_core(entered[0])]
            totals = [totals[0], *add_entered(totals[1], totals[2], both, 0)]
        ups[stage + 1], downs[stage + 1] = next_up, next_down
        ups, downs, totals = tie((ups, downs, totals))
    first, one, two = totals

    near = choose(chips - 1, ups, downs)
    far = other_core(near)
    first, tail = add_first(first, near, far, chips - 1)

    right_side = own_part(excitation[0]) - sum_parts(first)
    right_side, tail, near, far, one, two = tie((right_side, tail, near, far, one, two))
    mine = gather_near(right_side)
    entered.append(enter(tail))
    one, two = add_rest(one, two, near, far, chips - 1)
    mine, one, two, sent = tie((mine, one, two, sent))
    density = sum_parts(multiply(head_columns, mine))
    first_columns = pick([chunks[0], *sent])
    results = [density]

    density, first_columns, entered, one, two = tie((density, first_columns, entered, one, two))
    mine = gather_near(density)
    both += [v for piece in entered[1:] for v in (piece, other_core(piece))]
    one, two = add_entered(one, two, both[2:], 1)
    mine, one, two, both = tie((mine, one, two, both))
    right_side = own_part(excitation[1]) - sum_parts(one + multiply(first_columns, mine))

    right_side, two, old, both = tie((right_side, two, mine, both))
    mine = gather_near(right_side)
    nears = [old] + [lax.ppermute(old, "lag", [(j, 0)]) for j in range(1, groups)]
    mine, two = tie((mine, two))
    density = sum_parts(multiply(head_columns, mine))
    fars = other_core(jnp.stack(nears))
    results.append(density)

    density, two, nears, fars = tie((density, two, nears, fars))
    mine = gather_near(density)
    two = add_second(two, nears, both, fars)
    mine, two = tie((mine, two))
    right_side = own_part(excitation[2]) - sum_parts(two + multiply(first_columns, mine))

    right_side, results = tie((right_side, results))
    mine = gather_near(right_side)
    early = whole_rows(jnp.stack(results))
    mine, early = tie((mine, early))
    density = sum_parts(multiply(head_columns, mine))
    return jnp.concatenate([early, whole_rows(density[None])], axis=0)


def solution(mesh):
    placed = (P("lag", "row", None), P("row", None), P(None, "row", None), P("lag", "row", None))

    return jax.shard_map(on_device, mesh=mesh, in_specs=placed, out_specs=P(None, "row", None), check_vma=False)
```

```python
import jax
import jax.numpy as jnp
from jax import lax
from jax.experimental import pallas as pl
from jax.experimental.pallas import tpu as pltpu
from jax.sharding import PartitionSpec as P


STEPS = 3
F32 = jnp.float32
BF16 = jnp.bfloat16


def split(value):
    high = value.astype(BF16)
    return high, (value - high.astype(F32)).astype(BF16)


def dot(a, b):
    return jnp.dot(a, b, preferred_element_type=F32)


def product(weight, vectors):
    count, width = len(vectors), vectors[0].shape[1]
    wh, wl = split(weight)
    highs, lows = zip(*(split(v) for v in vectors))
    main = dot(wh, jnp.concatenate(highs + lows, axis=1))
    rest = dot(wl, jnp.concatenate(highs, axis=1) if count > 1 else highs[0])
    return main[:, : count * width] + main[:, count * width :] + rest


def ordered(core, near, far):
    return jnp.concatenate([jnp.where(core == 0, near, far), jnp.where(core == 0, far, near)], axis=0)


def chip_kernel(where, weights, *refs):
    outs, nearest, farther, high, low = refs[-STEPS - 4 : -4], *refs[-4:]
    pieces = refs[: len(refs) - STEPS - 4]
    totals = pieces[len(pieces) - STEPS :] if len(pieces) % 2 else []
    number, at = pl.program_id(0), pl.program_id(1)
    lags, rows, width = pieces[0].shape
    core = where[0]

    @pl.when(jnp.logical_and(number == 0, at == 0))
    def _():
        for n, out in enumerate(outs):
            out[...] = totals[n][...] if totals else jnp.zeros_like(out)

    count = len(pieces) // 2 - (1 if totals else 0)

    @pl.when(jnp.logical_and(number == count - 1, at == 0))
    def _():
        nearest[0] = pieces[2 * count - 2][lags - 1]
        farther[0] = pieces[2 * count - 2][lags - 2]

    for i in range(count):

        @pl.when(jnp.logical_and(number == i, at == 0))
        def _():
            for k in range(lags):
                columns = slice((lags - 1 - k) * width, (lags - k) * width)
                for piece, side in ((pieces[2 * i], core), (pieces[2 * i + 1], 1 - core)):
                    here = pl.ds(pl.multiple_of(side * rows, rows), rows)
                    high[here, columns], low[here, columns] = split(piece[k])

    for k in range(STEPS):

        @pl.when(at == k if k + 1 < STEPS else at >= k)
        def _():
            size = (k + 1) * width
            columns = pl.ds(pl.multiple_of((lags - 1 - at) * width, width), size)
            wh, wl = split(weights[0])
            h = high[:, columns]
            main = dot(wh, jnp.concatenate([h, low[:, columns]], axis=1))
            result = main[:, :size] + main[:, size:] + dot(wl, h)
            for n in range(k + 1):
                outs[n][...] += result[:, n * width : (n + 1) * width]


def first_kernel(where, weights, near, far, total, out, nearest, farther):
    at, lags = pl.program_id(0), pl.num_programs(0)

    @pl.when(at == lags - 2)
    def _():
        farther[...] = near[...]

    @pl.when(at == lags - 1)
    def _():
        nearest[...] = near[...]

    @pl.when(pl.program_id(0) == 0)
    def _():
        out[...] = total[...]

    out[...] += product(weights[0], [ordered(where[0], near[0], far[0])])


def rest_kernel(where, weights, near, near_before, far, far_before, one, two, one_out, two_out):
    at = pl.program_id(0)
    width = near.shape[-1]
    now = ordered(where[0], near[0], far[0])

    @pl.when(at == 0)
    def _():
        one_out[...] = one[...] + product(weights[0], [now])
        two_out[...] = two[...]

    @pl.when(at > 0)
    def _():
        result = product(weights[0], [now, ordered(where[0], near_before[0], far_before[0])])
        one_out[...] += result[:, :width]
        two_out[...] += result[:, width:]


def entered_kernel(where, weights, *refs):
    pieces, (total, out) = refs[:-2], refs[-2:]
    number = pl.program_id(0)

    @pl.when(number == 0)
    def _():
        out[...] = total[...]

    for i in range(len(pieces) // 2):

        @pl.when(jnp.logical_and(where[1] > 0, number == i))
        def _():
            out[...] += product(weights[0], [ordered(where[0], pieces[2 * i][0], pieces[2 * i + 1][0])])


def second_kernel(where, weights, *refs):
    (fars, total, out, vector), operands = refs[-4:], refs[:-4]
    groups = fars.shape[0]
    chips = (len(operands) - groups) // 2
    nears, pieces = operands[:groups], operands[groups:]
    rows, number = vector.shape[0] // 2, pl.program_id(0)
    part = rows // groups

    @pl.when(number == 0)
    def _():
        out[...] = total[...]

    @pl.when(where[1] == 0)
    def _():
        here = pl.ds(pl.multiple_of(number * part, part), part)
        near = jnp.concatenate([p[here, :] for p in nears], axis=0)
        far = jnp.concatenate([fars[j, here, :] for j in range(groups)], axis=0)
        vector[...] = ordered(where[0], near, far)

    for i in range(chips):

        @pl.when(jnp.logical_and(where[1] > 0, number == i))
        def _():
            vector[...] = ordered(where[0], pieces[2 * i][0], pieces[2 * i + 1][0])

    out[...] += product(weights[0], [vector[...]])


def columns_kernel(where, *refs):
    fold, groups = where.shape[1] - 1, where.shape[2]
    sources, outs = refs[:fold], refs[fold:]
    part = sources[0].shape[2] // groups
    take = lambda j: jnp.concatenate([s[0, :, j * part : (j + 1) * part] for s in sources], axis=1)
    if len(outs) == 1:
        for j in range(groups):

            @pl.when(where[0, fold, 0] == j)
            def _():
                outs[0][...] = take(j)

        return
    for j in range(groups - 1):
        outs[j][...] = take(j)
    for side, out in enumerate(outs[groups - 1 :]):

        @pl.when(pl.program_id(0) == side)
        def _():
            out[...] = take(groups - 1)


def pick_kernel(which, *refs):
    sources, out = refs[:-1], refs[-1]
    groups = len(sources) - 1
    for j, source in enumerate(sources):
        chosen = which[0] == min(j, groups - 1)
        if j >= groups - 1:
            chosen = jnp.logical_and(chosen, pl.program_id(0) == j - groups + 1)

        @pl.when(chosen)
        def _():
            out[...] = source[...]


def call(kernel, where, grid, operands, specs, count, shape, cost, aliases={}, scratch=()):
    return pl.pallas_call(
        kernel,
        out_shape=[jax.ShapeDtypeStruct(shape, F32)] * count,
        grid_spec=pltpu.PrefetchScalarGridSpec(
            num_scalar_prefetch=1, grid=grid, in_specs=specs, out_specs=[all_of(shape)] * count, scratch_shapes=scratch
        ),
        input_output_aliases=aliases,
        cost_estimate=pl.CostEstimate(flops=cost[0], bytes_accessed=cost[1], transcendentals=0),
        compiler_params=pltpu.CompilerParams(dimension_semantics=("arbitrary",) * len(grid)),
    )(where, *operands)


def all_of(shape):
    return pl.BlockSpec(shape, lambda *_: (0,) * len(shape))


def on_device(lag_weights, inverse_head, excitation, history):
    groups, devices = lax.axis_size("lag"), lax.axis_size("row")
    group, at = lax.axis_index("lag"), lax.axis_index("row")
    chips = devices // 2
    chip, core = at // 2, at % 2
    lags, rows, order = lag_weights.shape
    width = history.shape[-1]
    part = rows // groups
    tile = rows * 2 * rows
    square = (rows, width)
    tie = lax.optimization_barrier

    def pairs(axis_size, mask):
        return [(i, i ^ mask) for i in range(axis_size)]

    def other_core(value):
        return lax.ppermute(value, "row", pairs(devices, 1))

    def along(value, step, sources):
        return lax.ppermute(value, "row", [(2 * i + c, 2 * (i + step) + c) for i in sources for c in (0, 1)])

    def go_up(value, hop):
        return along(value, 1, range(hop - 1, chips - 1))

    def go_down(value, hop):
        return along(value, -1, range(1, chips - hop + 1))

    def taken(z, stage):
        both = min(z, chips - 1 - z)
        if stage <= 2 * both:
            return (stage + 1) // 2, stage % 2 == 1
        return stage - both, z >= stage - both

    def by_chip(values):
        result = jnp.int32(values[0])
        for z in range(1, chips):
            result = jnp.where(chip == z, values[z], result)
        return result

    def source_of(stage):
        return by_chip([z + (-h if u else h) for z in range(chips) for h, u in [taken(z, stage)]])

    def choose(stage, ups, downs):
        found = sorted({taken(z, stage) for z in range(chips)})
        arrays = [(ups if u else downs)[h] for h, u in found]
        return lax.select_n(by_chip([found.index(taken(z, stage)) for z in range(chips)]), *arrays) if len(found) > 1 else arrays[0]

    stages = [chip] + [source_of(stage) for stage in range(1, chips)]
    xored = [chip ^ k for k in range(chips)]
    where = jnp.stack([core, group, *stages, *xored]).astype(jnp.int32)

    def weight_spec(stage, first=0):
        return pl.BlockSpec((1, rows, 2 * rows), lambda k, w: (k + first, 0, w[2 + stage]))

    def lag_spec(shift):
        return pl.BlockSpec((1, rows, width), lambda k, w: (jnp.maximum(k + shift, 0), 0, 0))

    def add_chip(totals, pieces, stage):
        count = len(pieces) // 2
        single = (1, *square)
        *totals, nearest, farther = pl.pallas_call(
            chip_kernel,
            out_shape=[jax.ShapeDtypeStruct(square, F32)] * STEPS + [jax.ShapeDtypeStruct(single, F32)] * 2,
            grid_spec=pltpu.PrefetchScalarGridSpec(
                num_scalar_prefetch=1,
                grid=(count, lags),
                in_specs=[pl.BlockSpec((1, rows, 2 * rows), lambda i, k, w: (k, 0, w[2 + stage + i]))]
                + [all_of(v.shape) for v in (*pieces, *totals)],
                out_specs=[all_of(square)] * STEPS + [all_of(single)] * 2,
                scratch_shapes=[pltpu.VMEM((2 * rows, lags * width), BF16)] * 2,
            ),
            input_output_aliases={2 + len(pieces) + n: n for n in range(len(totals))},
            cost_estimate=pl.CostEstimate(flops=18 * count * lags * tile * width, bytes_accessed=4 * count * lags * tile, transcendentals=0),
            compiler_params=pltpu.CompilerParams(dimension_semantics=("arbitrary", "arbitrary")),
            name="chip",
        )(where, lag_weights, *pieces, *totals)
        return totals, nearest, farther

    def add_first(total, near, far, stage):
        single = (1, *square)
        return pl.pallas_call(
            first_kernel,
            out_shape=[jax.ShapeDtypeStruct(square, F32)] + [jax.ShapeDtypeStruct(single, F32)] * 2,
            grid_spec=pltpu.PrefetchScalarGridSpec(
                num_scalar_prefetch=1,
                grid=(lags,),
                in_specs=[weight_spec(stage), lag_spec(0), lag_spec(0), all_of(square)],
                out_specs=[all_of(square)] + [all_of(single)] * 2,
            ),
            input_output_aliases={4: 0},
            cost_estimate=pl.CostEstimate(flops=6 * lags * tile * width, bytes_accessed=4 * lags * tile, transcendentals=0),
            compiler_params=pltpu.CompilerParams(dimension_semantics=("arbitrary",)),
            name="first",
        )(where, lag_weights, near, far, total)

    def add_rest(one, two, near, far, stage):
        return call(
            rest_kernel, where, (lags - 1,), (lag_weights, near, near, far, far, one, two),
            [weight_spec(stage, 1), lag_spec(0), lag_spec(-1), lag_spec(0), lag_spec(-1), all_of(square), all_of(square)],
            2, square, (12 * lags * tile * width, 4 * lags * tile), {6: 0, 7: 1},
        )

    def add_entered(total, pieces, stage):
        count = len(pieces) // 2
        spec = pl.BlockSpec((1, rows, 2 * rows), lambda i, w: (0, 0, jnp.where(w[1] > 0, w[2 + stage + i], 0)))
        return call(
            entered_kernel, where, (count,), (lag_weights, *[v for v, _ in pieces], total),
            [spec] + [pl.BlockSpec((1, rows, width), lambda i, w, at=at: (at, 0, 0)) for _, at in pieces] + [all_of(square)],
            1, square, (6 * count * tile * width, 4 * count * tile), {2 + len(pieces): 0},
        )[0]

    def add_second(total, nears, pieces, fars):
        spec = pl.BlockSpec((1, rows, 2 * rows), lambda i, w: (1, 0, w[2 + i + jnp.where(w[1] == 0, chips, 0)]))
        last = all_of((1, rows, width))
        return call(
            second_kernel, where, (chips,), (lag_weights, *nears, *pieces, fars, total),
            [spec] + [all_of(v.shape) for v in nears] + [last] * len(pieces) + [all_of(fars.shape), all_of(square)],
            1, square, (6 * rows * order * width, 4 * rows * order), {3 + len(nears) + len(pieces): 0},
            [pltpu.VMEM((2 * rows, width), F32)],
        )[0]

    slots = jnp.stack([(chip ^ k) * 2 + (core ^ h) for h in (0, 1) for k in range(chips)]).astype(jnp.int32)
    meet = devices * part

    def columns(matrix, every):
        fold = devices // 2
        numbers = jnp.tile(slots.reshape(2, fold, 1), (1, 1, groups))
        numbers = jnp.concatenate([numbers, jnp.full((2, 1, groups), group, jnp.int32)], axis=1)
        whole = pl.BlockSpec((rows, meet // 2), lambda s, w: (0, s))
        half = pl.BlockSpec((rows, meet // 2), lambda s, w: (0, 0))
        shape = lambda size: jax.ShapeDtypeStruct((rows, size), F32)
        return pl.pallas_call(
            columns_kernel,
            out_shape=[shape(meet)] * (groups - 1) + [shape(meet // 2)] * 2 if every else [shape(meet)],
            grid_spec=pltpu.PrefetchScalarGridSpec(
                num_scalar_prefetch=1,
                grid=(2,),
                in_specs=[pl.BlockSpec((1, rows, rows), lambda s, w, i=i: (0, 0, w[s, i, 0])) for i in range(fold)],
                out_specs=[whole] * (groups - 1) + [half] * 2 if every else [whole],
            ),
            cost_estimate=pl.CostEstimate(flops=0, bytes_accessed=8 * rows * order, transcendentals=0),
            compiler_params=pltpu.CompilerParams(dimension_semantics=("arbitrary",)),
            name="columns",
        )(numbers, *[matrix] * fold)

    def pick(matrices):
        spec = lambda j: pl.BlockSpec((rows, meet // 2), lambda s, w: (0, jnp.where(w[0] == j, s, 0)))
        return pl.pallas_call(
            pick_kernel,
            out_shape=jax.ShapeDtypeStruct((rows, meet), F32),
            grid_spec=pltpu.PrefetchScalarGridSpec(
                num_scalar_prefetch=1,
                grid=(2,),
                in_specs=[spec(j) for j in range(groups - 1)] + [all_of((rows, meet // 2))] * 2,
                out_specs=pl.BlockSpec((rows, meet // 2), lambda s, w: (0, s)),
            ),
            cost_estimate=pl.CostEstimate(flops=0, bytes_accessed=16 * rows * meet, transcendentals=0),
            compiler_params=pltpu.CompilerParams(dimension_semantics=("arbitrary",)),
            name="pick",
        )(group.astype(jnp.int32).reshape(1), *matrices)

    def gather_near(value):
        pieces = [value] + [lax.ppermute(value, "row", pairs(devices, 2 * k)) for k in range(1, chips)]
        return jnp.concatenate(pieces, axis=0)

    def own_part(value):
        return lax.dynamic_slice(value, (group * part, 0), (part, value.shape[1]))

    def sum_parts(value):
        result = own_part(value)
        for mask in range(1, groups):
            sent = lax.dynamic_slice(value, ((group ^ mask) * part, 0), (part, width))
            result = result + lax.ppermute(sent, "lag", pairs(groups, mask))
        return result

    def whole_rows(value):
        pieces = [value] + [lax.ppermute(value, "lag", pairs(groups, mask)) for mask in range(1, groups)]
        return jnp.concatenate([lax.select_n(group ^ i, *pieces) for i in range(groups)], axis=1)

    def enter(tail):
        return lax.ppermute(tail, "lag", [(i, i + 1) for i in range(groups - 1)])

    def multiply(matrix, mine):
        vector = jnp.concatenate([mine, other_core(mine)], axis=0)
        return jnp.dot(matrix, vector, precision=lax.Precision.HIGH)

    ups, downs = {1: go_up(history, 1)}, {1: go_down(history, 1)}
    entered = [enter(jnp.where(group >= 0, history[lags - 1 :], 0.0))]
    farthers = [history[lags - 2 : lags - 1]]
    own_far = other_core(history)
    *chunks, last_near, last_far = columns(lag_weights, True)
    relayed = lax.ppermute(last_far, "lag", [(0, groups // 2)])
    sent = [lax.ppermute(chunks[j], "lag", [(0, j)]) for j in range(1, groups - 1)]
    (head_columns,) = columns(inverse_head[None], False)
    ups[1], downs[1], entered, own_far, head_columns = tie((ups[1], downs[1], entered, own_far, head_columns))
    totals = []
    for stage in range(1, chips - 1):
        next_up, next_down = go_up(ups[stage], stage + 1), go_down(downs[stage], stage + 1)
        near = choose(stage, ups, downs)
        if stage == chips - 2:
            relayed, near = tie((relayed, near))
            sent.append(lax.ppermute(relayed, "lag", [(groups // 2, groups - 1)]))
        pieces = [near, other_core(near)]
        if stage == 1:
            pieces = [history, own_far, *pieces]
        totals, tail, farther = add_chip(totals, pieces, stage if stage > 1 else 0)
        farthers.append(farther)
        entered.append(enter(tail))
        if stage == 1:
            last_near, tail = tie((last_near, tail))
            sent.append(lax.ppermute(last_near, "lag", [(0, groups - 1)]))
        if stage == chips - 2:
            both = [entered[0], other_core(entered[0])]
            totals[1] = add_entered(totals[1], [(v, 0) for v in both], 0)
        ups[stage + 1], downs[stage + 1] = next_up, next_down
        ups, downs, totals = tie((ups, downs, totals))
    first, one, two = totals

    near = choose(chips - 1, ups, downs)
    far = other_core(near)
    first, tail, farther = add_first(first, near, far, chips - 1)

    right_side = own_part(excitation[0]) - sum_parts(first)
    farthers.append(farther)
    right_side, tail, farthers, near, far, one, two = tie((right_side, tail, farthers, near, far, one, two))
    mine = gather_near(right_side)
    entered.append(enter(tail))
    packs = [enter(jnp.concatenate(farthers[: chips // 2], axis=0))]
    one, two = add_rest(one, two, near, far, chips - 1)
    mine, one, two, sent = tie((mine, one, two, sent))
    density = sum_parts(multiply(head_columns, mine))
    first_columns = pick([chunks[0], *sent])
    results = [density]

    density, first_columns, entered, farthers, one, two = tie((density, first_columns, entered, farthers, one, two))
    mine = gather_near(density)
    packs.append(enter(jnp.concatenate(farthers[chips // 2 :], axis=0)))
    both += [v for piece in entered[1:] for v in (piece, other_core(piece))]
    one = add_entered(one, [(v, 0) for v in both[2:]], 1)
    mine, one, two, both = tie((mine, one, two, both))
    right_side = own_part(excitation[1]) - sum_parts(one + multiply(first_columns, mine))

    right_side, two, old, both, packs = tie((right_side, two, mine, both, packs))
    mine = gather_near(right_side)
    nears = [old] + [lax.ppermute(old, "lag", [(j, 0)]) for j in range(1, groups)]
    pack_fars = [other_core(pack) for pack in packs]
    last = [(pack, far, i) for pack, far in zip(packs, pack_fars) for i in range(chips // 2)]
    two = add_entered(two, [v for pack, far, i in last for v in ((pack, i), (far, i))], 0)
    mine, two = tie((mine, two))
    carried = multiply(head_columns, mine)
    density = sum_parts(carried)
    fars = other_core(jnp.stack(nears))
    results.append(density)

    density, two = tie((density, two))
    mine = gather_near(density)
    two = add_second(two, nears, both, fars)
    mine, two = tie((mine, two))
    right_side = own_part(excitation[2]) - sum_parts(two + multiply(first_columns, mine))

    right_side, results = tie((right_side, results))
    mine = gather_near(right_side)
    early = whole_rows(jnp.stack(results))
    mine, early = tie((mine, early))
    density = sum_parts(multiply(head_columns, mine))
    return jnp.concatenate([early, whole_rows(density[None])], axis=0)


def solution(mesh):
    placed = (P("lag", "row", None), P("row", None), P(None, "row", None), P("lag", "row", None))

    return jax.shard_map(on_device, mesh=mesh, in_specs=placed, out_specs=P(None, "row", None), check_vma=False)
```

```python
import jax
import jax.numpy as jnp
from jax import lax
from jax.experimental import pallas as pl
from jax.experimental.pallas import tpu as pltpu
from jax.sharding import PartitionSpec as P


STEPS = 3
F32 = jnp.float32
BF16 = jnp.bfloat16


def split(value):
    high = value.astype(BF16)
    return high, (value - high.astype(F32)).astype(BF16)


def dot(a, b):
    return jnp.dot(a, b, preferred_element_type=F32)


def product(weight, vectors):
    count, width = len(vectors), vectors[0].shape[1]
    wh, wl = split(weight)
    highs, lows = zip(*(split(v) for v in vectors))
    main = dot(wh, jnp.concatenate(highs + lows, axis=1))
    rest = dot(wl, jnp.concatenate(highs, axis=1) if count > 1 else highs[0])
    return main[:, : count * width] + main[:, count * width :] + rest


def ordered(core, near, far):
    return jnp.concatenate([jnp.where(core == 0, near, far), jnp.where(core == 0, far, near)], axis=0)


def chip_kernel(where, weights, *refs):
    outs, tail, high, low = refs[-STEPS - 3 : -3], *refs[-3:]
    pieces = refs[: len(refs) - STEPS - 3]
    totals = pieces[len(pieces) - STEPS :] if len(pieces) % 2 else []
    number, at = pl.program_id(0), pl.program_id(1)
    lags, rows, width = pieces[0].shape
    core = where[0]

    @pl.when(jnp.logical_and(number == 0, at == 0))
    def _():
        for n, out in enumerate(outs):
            out[...] = totals[n][...] if totals else jnp.zeros_like(out)

    count = len(pieces) // 2 - (1 if totals else 0)

    @pl.when(jnp.logical_and(number == count - 1, at == 0))
    def _():
        tail[...] = pieces[2 * count - 2][lags - tail.shape[0] :]

    for i in range(count):

        @pl.when(jnp.logical_and(number == i, at == 0))
        def _():
            for k in range(lags):
                columns = slice((lags - 1 - k) * width, (lags - k) * width)
                for piece, side in ((pieces[2 * i], core), (pieces[2 * i + 1], 1 - core)):
                    here = pl.ds(pl.multiple_of(side * rows, rows), rows)
                    high[here, columns], low[here, columns] = split(piece[k])

    for k in range(STEPS):

        @pl.when(at == k if k + 1 < STEPS else at >= k)
        def _():
            size = (k + 1) * width
            columns = pl.ds(pl.multiple_of((lags - 1 - at) * width, width), size)
            wh, wl = split(weights[0])
            h = high[:, columns]
            main = dot(wh, jnp.concatenate([h, low[:, columns]], axis=1))
            result = main[:, :size] + main[:, size:] + dot(wl, h)
            for n in range(k + 1):
                outs[n][...] += result[:, n * width : (n + 1) * width]


def first_kernel(where, weights, near, far, total, out, tail):
    @pl.when(pl.program_id(0) == 0)
    def _():
        out[...] = total[...]

    tail[...] = near[...]
    out[...] += product(weights[0], [ordered(where[0], near[0], far[0])])


def rest_kernel(where, weights, near, near_before, far, far_before, one, two, one_out, two_out):
    at = pl.program_id(0)
    width = near.shape[-1]
    now = ordered(where[0], near[0], far[0])

    @pl.when(at == 0)
    def _():
        one_out[...] = one[...] + product(weights[0], [now])
        two_out[...] = two[...]

    @pl.when(at > 0)
    def _():
        result = product(weights[0], [now, ordered(where[0], near_before[0], far_before[0])])
        one_out[...] += result[:, :width]
        two_out[...] += result[:, width:]


def entered_kernel(where, weights, *refs):
    pieces, (one, two, one_out, two_out) = refs[:-4], refs[-4:]
    number = pl.program_id(0)
    width = pieces[0].shape[2]

    @pl.when(number == 0)
    def _():
        one_out[...] = one[...]
        two_out[...] = two[...]

    for i in range(len(pieces) // 2):

        @pl.when(jnp.logical_and(where[1] > 0, number == i))
        def _():
            near, far = pieces[2 * i : 2 * i + 2]
            result = product(weights[0], [ordered(where[0], near[k], far[k]) for k in (1, 0)])
            one_out[...] += result[:, :width]
            two_out[...] += result[:, width:]


def second_kernel(where, weights, *refs):
    (fars, total, out, vector), operands = refs[-4:], refs[:-4]
    groups = fars.shape[0]
    chips = (len(operands) - groups) // 2
    nears, pieces = operands[:groups], operands[groups:]
    rows, number = vector.shape[0] // 2, pl.program_id(0)
    part = rows // groups

    @pl.when(number == 0)
    def _():
        out[...] = total[...]

    @pl.when(where[1] == 0)
    def _():
        here = pl.ds(pl.multiple_of(number * part, part), part)
        near = jnp.concatenate([p[here, :] for p in nears], axis=0)
        far = jnp.concatenate([fars[j, here, :] for j in range(groups)], axis=0)
        vector[...] = ordered(where[0], near, far)

    for i in range(chips):

        @pl.when(jnp.logical_and(where[1] > 0, number == i))
        def _():
            vector[...] = ordered(where[0], pieces[2 * i][0], pieces[2 * i + 1][0])

    out[...] += product(weights[0], [vector[...]])


def columns_kernel(where, *refs):
    fold, groups = where.shape[1] - 1, where.shape[2]
    sources, outs = refs[:fold], refs[fold:]
    part = sources[0].shape[2] // groups
    take = lambda j: jnp.concatenate([s[0, :, j * part : (j + 1) * part] for s in sources], axis=1)
    if len(outs) == 1:
        for j in range(groups):

            @pl.when(where[0, fold, 0] == j)
            def _():
                outs[0][...] = take(j)

        return
    for j in range(groups - 1):
        outs[j][...] = take(j)
    for side, out in enumerate(outs[groups - 1 :]):

        @pl.when(pl.program_id(0) == side)
        def _():
            out[...] = take(groups - 1)


def pick_kernel(which, *refs):
    sources, out = refs[:-1], refs[-1]
    groups = len(sources) - 1
    for j, source in enumerate(sources):
        chosen = which[0] == min(j, groups - 1)
        if j >= groups - 1:
            chosen = jnp.logical_and(chosen, pl.program_id(0) == j - groups + 1)

        @pl.when(chosen)
        def _():
            out[...] = source[...]


def call(kernel, where, grid, operands, specs, count, shape, cost, aliases={}, scratch=()):
    return pl.pallas_call(
        kernel,
        out_shape=[jax.ShapeDtypeStruct(shape, F32)] * count,
        grid_spec=pltpu.PrefetchScalarGridSpec(
            num_scalar_prefetch=1, grid=grid, in_specs=specs, out_specs=[all_of(shape)] * count, scratch_shapes=scratch
        ),
        input_output_aliases=aliases,
        cost_estimate=pl.CostEstimate(flops=cost[0], bytes_accessed=cost[1], transcendentals=0),
        compiler_params=pltpu.CompilerParams(dimension_semantics=("arbitrary",) * len(grid)),
    )(where, *operands)


def all_of(shape):
    return pl.BlockSpec(shape, lambda *_: (0,) * len(shape))


def on_device(lag_weights, inverse_head, excitation, history):
    groups, devices = lax.axis_size("lag"), lax.axis_size("row")
    group, at = lax.axis_index("lag"), lax.axis_index("row")
    chips = devices // 2
    chip, core = at // 2, at % 2
    lags, rows, order = lag_weights.shape
    width = history.shape[-1]
    part = rows // groups
    tile = rows * 2 * rows
    square = (rows, width)
    tie = lax.optimization_barrier

    def pairs(axis_size, mask):
        return [(i, i ^ mask) for i in range(axis_size)]

    def other_core(value):
        return lax.ppermute(value, "row", pairs(devices, 1))

    def along(value, step, sources):
        return lax.ppermute(value, "row", [(2 * i + c, 2 * (i + step) + c) for i in sources for c in (0, 1)])

    def go_up(value, hop):
        return along(value, 1, range(hop - 1, chips - 1))

    def go_down(value, hop):
        return along(value, -1, range(1, chips - hop + 1))

    def taken(z, stage):
        both = min(z, chips - 1 - z)
        if stage <= 2 * both:
            return (stage + 1) // 2, stage % 2 == 1
        return stage - both, z >= stage - both

    def by_chip(values):
        result = jnp.int32(values[0])
        for z in range(1, chips):
            result = jnp.where(chip == z, values[z], result)
        return result

    def source_of(stage):
        return by_chip([z + (-h if u else h) for z in range(chips) for h, u in [taken(z, stage)]])

    def choose(stage, ups, downs):
        found = sorted({taken(z, stage) for z in range(chips)})
        arrays = [(ups if u else downs)[h] for h, u in found]
        return lax.select_n(by_chip([found.index(taken(z, stage)) for z in range(chips)]), *arrays) if len(found) > 1 else arrays[0]

    stages = [chip] + [source_of(stage) for stage in range(1, chips)]
    xored = [chip ^ k for k in range(chips)]
    where = jnp.stack([core, group, *stages, *xored]).astype(jnp.int32)

    def weight_spec(stage, first=0):
        return pl.BlockSpec((1, rows, 2 * rows), lambda k, w: (k + first, 0, w[2 + stage]))

    def lag_spec(shift):
        return pl.BlockSpec((1, rows, width), lambda k, w: (jnp.maximum(k + shift, 0), 0, 0))

    def add_chip(totals, pieces, stage):
        count = len(pieces) // 2
        before = (STEPS - 1, *square)
        *totals, tail = pl.pallas_call(
            chip_kernel,
            out_shape=[jax.ShapeDtypeStruct(square, F32)] * STEPS + [jax.ShapeDtypeStruct(before, F32)],
            grid_spec=pltpu.PrefetchScalarGridSpec(
                num_scalar_prefetch=1,
                grid=(count, lags),
                in_specs=[pl.BlockSpec((1, rows, 2 * rows), lambda i, k, w: (k, 0, w[2 + stage + i]))]
                + [all_of(v.shape) for v in (*pieces, *totals)],
                out_specs=[all_of(square)] * STEPS + [all_of(before)],
                scratch_shapes=[pltpu.VMEM((2 * rows, lags * width), BF16)] * 2,
            ),
            input_output_aliases={2 + len(pieces) + n: n for n in range(len(totals))},
            cost_estimate=pl.CostEstimate(flops=18 * count * lags * tile * width, bytes_accessed=4 * count * lags * tile, transcendentals=0),
            compiler_params=pltpu.CompilerParams(dimension_semantics=("arbitrary", "arbitrary")),
            name="chip",
        )(where, lag_weights, *pieces, *totals)
        return totals, tail

    def add_first(total, near, far, stage):
        before = STEPS - 1
        return pl.pallas_call(
            first_kernel,
            out_shape=[jax.ShapeDtypeStruct(square, F32), jax.ShapeDtypeStruct((before, *square), F32)],
            grid_spec=pltpu.PrefetchScalarGridSpec(
                num_scalar_prefetch=1,
                grid=(lags,),
                in_specs=[weight_spec(stage), lag_spec(0), lag_spec(0), all_of(square)],
                out_specs=[all_of(square), pl.BlockSpec((1, *square), lambda k, w: (jnp.maximum(k + before - lags, 0), 0, 0))],
            ),
            input_output_aliases={4: 0},
            cost_estimate=pl.CostEstimate(flops=6 * lags * tile * width, bytes_accessed=4 * lags * tile, transcendentals=0),
            compiler_params=pltpu.CompilerParams(dimension_semantics=("arbitrary",)),
            name="first",
        )(where, lag_weights, near, far, total)

    def add_rest(one, two, near, far, stage):
        return call(
            rest_kernel, where, (lags - 1,), (lag_weights, near, near, far, far, one, two),
            [weight_spec(stage, 1), lag_spec(0), lag_spec(-1), lag_spec(0), lag_spec(-1), all_of(square), all_of(square)],
            2, square, (12 * lags * tile * width, 4 * lags * tile), {6: 0, 7: 1},
        )

    def add_entered(one, two, pieces, stage):
        count = len(pieces) // 2
        spec = pl.BlockSpec((1, rows, 2 * rows), lambda i, w: (0, 0, jnp.where(w[1] > 0, w[2 + stage + i], 0)))
        return call(
            entered_kernel, where, (count,), (lag_weights, *pieces, one, two),
            [spec] + [all_of(v.shape) for v in (*pieces, one, two)],
            2, square, (12 * count * tile * width, 4 * count * tile), {2 + len(pieces): 0, 3 + len(pieces): 1},
        )

    def add_second(total, nears, pieces, fars):
        spec = pl.BlockSpec((1, rows, 2 * rows), lambda i, w: (1, 0, w[2 + i + jnp.where(w[1] == 0, chips, 0)]))
        last = pl.BlockSpec((1, rows, width), lambda i, w: (STEPS - 2, 0, 0))
        return call(
            second_kernel, where, (chips,), (lag_weights, *nears, *pieces, fars, total),
            [spec] + [all_of(v.shape) for v in nears] + [last] * len(pieces) + [all_of(fars.shape), all_of(square)],
            1, square, (6 * rows * order * width, 4 * rows * order), {3 + len(nears) + len(pieces): 0},
            [pltpu.VMEM((2 * rows, width), F32)],
        )[0]

    slots = jnp.stack([(chip ^ k) * 2 + (core ^ h) for h in (0, 1) for k in range(chips)]).astype(jnp.int32)
    meet = devices * part

    def columns(matrix, every):
        fold = devices // 2
        numbers = jnp.tile(slots.reshape(2, fold, 1), (1, 1, groups))
        numbers = jnp.concatenate([numbers, jnp.full((2, 1, groups), group, jnp.int32)], axis=1)
        whole = pl.BlockSpec((rows, meet // 2), lambda s, w: (0, s))
        half = pl.BlockSpec((rows, meet // 2), lambda s, w: (0, 0))
        shape = lambda size: jax.ShapeDtypeStruct((rows, size), F32)
        return pl.pallas_call(
            columns_kernel,
            out_shape=[shape(meet)] * (groups - 1) + [shape(meet // 2)] * 2 if every else [shape(meet)],
            grid_spec=pltpu.PrefetchScalarGridSpec(
                num_scalar_prefetch=1,
                grid=(2,),
                in_specs=[pl.BlockSpec((1, rows, rows), lambda s, w, i=i: (0, 0, w[s, i, 0])) for i in range(fold)],
                out_specs=[whole] * (groups - 1) + [half] * 2 if every else [whole],
            ),
            cost_estimate=pl.CostEstimate(flops=0, bytes_accessed=8 * rows * order, transcendentals=0),
            compiler_params=pltpu.CompilerParams(dimension_semantics=("arbitrary",)),
            name="columns",
        )(numbers, *[matrix] * fold)

    def pick(matrices):
        spec = lambda j: pl.BlockSpec((rows, meet // 2), lambda s, w: (0, jnp.where(w[0] == j, s, 0)))
        return pl.pallas_call(
            pick_kernel,
            out_shape=jax.ShapeDtypeStruct((rows, meet), F32),
            grid_spec=pltpu.PrefetchScalarGridSpec(
                num_scalar_prefetch=1,
                grid=(2,),
                in_specs=[spec(j) for j in range(groups - 1)] + [all_of((rows, meet // 2))] * 2,
                out_specs=pl.BlockSpec((rows, meet // 2), lambda s, w: (0, s)),
            ),
            cost_estimate=pl.CostEstimate(flops=0, bytes_accessed=16 * rows * meet, transcendentals=0),
            compiler_params=pltpu.CompilerParams(dimension_semantics=("arbitrary",)),
            name="pick",
        )(group.astype(jnp.int32).reshape(1), *matrices)

    def gather_near(value):
        pieces = [value] + [lax.ppermute(value, "row", pairs(devices, 2 * k)) for k in range(1, chips)]
        return jnp.concatenate(pieces, axis=0)

    def own_part(value):
        return lax.dynamic_slice(value, (group * part, 0), (part, value.shape[1]))

    def sum_parts(value):
        result = own_part(value)
        for mask in range(1, groups):
            sent = lax.dynamic_slice(value, ((group ^ mask) * part, 0), (part, width))
            result = result + lax.ppermute(sent, "lag", pairs(groups, mask))
        return result

    def whole_rows(value):
        pieces = [value] + [lax.ppermute(value, "lag", pairs(groups, mask)) for mask in range(1, groups)]
        return jnp.concatenate([lax.select_n(group ^ i, *pieces) for i in range(groups)], axis=1)

    def enter(tail):
        return lax.ppermute(tail, "lag", [(i, i + 1) for i in range(groups - 1)])

    def multiply(matrix, mine):
        vector = jnp.concatenate([mine, other_core(mine)], axis=0)
        return jnp.dot(matrix, vector, precision=lax.Precision.HIGH)

    ups, downs = {1: go_up(history, 1)}, {1: go_down(history, 1)}
    tail = history[lags - (STEPS - 1) :]
    entered = [enter(jnp.where(group >= 0, tail, 0.0))]
    own_far = other_core(history)
    *chunks, last_near, last_far = columns(lag_weights, True)
    relayed = lax.ppermute(last_far, "lag", [(0, groups // 2)])
    sent = [lax.ppermute(chunks[j], "lag", [(0, j)]) for j in range(1, groups - 1)]
    (head_columns,) = columns(inverse_head[None], False)
    ups[1], downs[1], entered, own_far, head_columns = tie((ups[1], downs[1], entered, own_far, head_columns))
    totals = []
    for stage in range(1, chips - 1):
        next_up, next_down = go_up(ups[stage], stage + 1), go_down(downs[stage], stage + 1)
        near = choose(stage, ups, downs)
        if stage == chips - 2:
            relayed, near = tie((relayed, near))
            sent.append(lax.ppermute(relayed, "lag", [(groups // 2, groups - 1)]))
        pieces = [near, other_core(near)]
        if stage == 1:
            pieces = [history, own_far, *pieces]
        totals, tail = add_chip(totals, pieces, stage if stage > 1 else 0)
        if stage == chips - 2:
            waiting = tail
        else:
            entered.append(enter(tail))
        if stage == 1:
            last_near, tail = tie((last_near, tail))
            sent.append(lax.ppermute(last_near, "lag", [(0, groups - 1)]))
        if stage == chips - 2:
            both = [entered[0], other_core(entered[0])]
            totals = [totals[0], *add_entered(totals[1], totals[2], both, 0)]
        ups[stage + 1], downs[stage + 1] = next_up, next_down
        ups, downs, totals = tie((ups, downs, totals))
    first, one, two = totals

    near = choose(chips - 1, ups, downs)
    far = other_core(near)
    first, tail = add_first(first, near, far, chips - 1)

    right_side = own_part(excitation[0]) - sum_parts(first)
    right_side, waiting, tail, near, far, one, two = tie((right_side, waiting, tail, near, far, one, two))
    mine = gather_near(right_side)
    entered += [enter(waiting), enter(tail)]
    one, two = add_rest(one, two, near, far, chips - 1)
    mine, one, two, sent = tie((mine, one, two, sent))
    density = sum_parts(multiply(head_columns, mine))
    first_columns = pick([chunks[0], *sent])
    results = [density]

    density, first_columns, entered, one, two = tie((density, first_columns, entered, one, two))
    mine = gather_near(density)
    both += [v for piece in entered[1:] for v in (piece, other_core(piece))]
    one, two = add_entered(one, two, both[2:], 1)
    mine, one, two, both = tie((mine, one, two, both))
    right_side = own_part(excitation[1]) - sum_parts(one + multiply(first_columns, mine))

    right_side, two, old, both = tie((right_side, two, mine, both))
    mine = gather_near(right_side)
    nears = [old] + [lax.ppermute(old, "lag", [(j, 0)]) for j in range(1, groups)]
    mine, two = tie((mine, two))
    carried = multiply(head_columns, mine)
    density = sum_parts(carried)
    fars = other_core(jnp.stack(nears))
    results.append(density)

    density, two = tie((density, two))
    mine = gather_near(density)
    two = add_second(two, nears, both, fars)
    mine, two = tie((mine, two))
    right_side = own_part(excitation[2]) - sum_parts(two + multiply(first_columns, mine))

    right_side, results = tie((right_side, results))
    mine = gather_near(right_side)
    early = whole_rows(jnp.stack(results))
    mine, early = tie((mine, early))
    density = sum_parts(multiply(head_columns, mine))
    return jnp.concatenate([early, whole_rows(density[None])], axis=0)


def solution(mesh):
    placed = (P("lag", "row", None), P("row", None), P(None, "row", None), P("lag", "row", None))

    return jax.shard_map(on_device, mesh=mesh, in_specs=placed, out_specs=P(None, "row", None), check_vma=False)
```

```python
import jax
import jax.numpy as jnp
from jax import lax
from jax.experimental import pallas as pl
from jax.experimental.pallas import tpu as pltpu
from jax.sharding import PartitionSpec as P


STEPS = 3
F32 = jnp.float32
BF16 = jnp.bfloat16


def split(value):
    high = value.astype(BF16)
    return high, (value - high.astype(F32)).astype(BF16)


def dot(a, b):
    return jnp.dot(a, b, preferred_element_type=F32)


def product(weight, vectors):
    count, width = len(vectors), vectors[0].shape[1]
    wh, wl = split(weight)
    highs, lows = zip(*(split(v) for v in vectors))
    main = dot(wh, jnp.concatenate(highs + lows, axis=1))
    rest = dot(wl, jnp.concatenate(highs, axis=1) if count > 1 else highs[0])
    return main[:, : count * width] + main[:, count * width :] + rest


def ordered(core, near, far):
    return jnp.concatenate([jnp.where(core == 0, near, far), jnp.where(core == 0, far, near)], axis=0)


def chip_kernel(where, weights, *refs):
    outs, tail, high, low = refs[-STEPS - 3 : -3], *refs[-3:]
    pieces = refs[: len(refs) - STEPS - 3]
    totals = pieces[len(pieces) - STEPS :] if len(pieces) % 2 else []
    number, at = pl.program_id(0), pl.program_id(1)
    lags, rows, width = pieces[0].shape
    core = where[0]

    @pl.when(jnp.logical_and(number == 0, at == 0))
    def _():
        for n, out in enumerate(outs):
            out[...] = totals[n][...] if totals else jnp.zeros_like(out)

    count = len(pieces) // 2 - (1 if totals else 0)

    @pl.when(jnp.logical_and(number == count - 1, at == 0))
    def _():
        tail[...] = pieces[2 * count - 2][lags - tail.shape[0] :]

    for i in range(count):

        @pl.when(jnp.logical_and(number == i, at == 0))
        def _():
            for k in range(lags):
                columns = slice((lags - 1 - k) * width, (lags - k) * width)
                for piece, side in ((pieces[2 * i], core), (pieces[2 * i + 1], 1 - core)):
                    here = pl.ds(pl.multiple_of(side * rows, rows), rows)
                    high[here, columns], low[here, columns] = split(piece[k])

    for k in range(STEPS):

        @pl.when(at == k if k + 1 < STEPS else at >= k)
        def _():
            size = (k + 1) * width
            columns = pl.ds(pl.multiple_of((lags - 1 - at) * width, width), size)
            wh, wl = split(weights[0])
            h = high[:, columns]
            main = dot(wh, jnp.concatenate([h, low[:, columns]], axis=1))
            result = main[:, :size] + main[:, size:] + dot(wl, h)
            for n in range(k + 1):
                outs[n][...] += result[:, n * width : (n + 1) * width]


def first_kernel(where, weights, near, far, total, out, tail):
    @pl.when(pl.program_id(0) == 0)
    def _():
        out[...] = total[...]

    tail[...] = near[...]
    out[...] += product(weights[0], [ordered(where[0], near[0], far[0])])


def rest_kernel(where, weights, near, near_before, far, far_before, one, two, one_out, two_out):
    at = pl.program_id(0)
    width = near.shape[-1]
    now = ordered(where[0], near[0], far[0])

    @pl.when(at == 0)
    def _():
        one_out[...] = one[...] + product(weights[0], [now])
        two_out[...] = two[...]

    @pl.when(at > 0)
    def _():
        result = product(weights[0], [now, ordered(where[0], near_before[0], far_before[0])])
        one_out[...] += result[:, :width]
        two_out[...] += result[:, width:]


def entered_kernel(where, weights, *refs):
    pieces, (one, two, one_out, two_out) = refs[:-4], refs[-4:]
    number = pl.program_id(0)
    width = pieces[0].shape[2]

    @pl.when(number == 0)
    def _():
        one_out[...] = one[...]
        two_out[...] = two[...]

    for i in range(len(pieces) // 2):

        @pl.when(jnp.logical_and(where[1] > 0, number == i))
        def _():
            near, far = pieces[2 * i : 2 * i + 2]
            result = product(weights[0], [ordered(where[0], near[k], far[k]) for k in (1, 0)])
            one_out[...] += result[:, :width]
            two_out[...] += result[:, width:]


def second_kernel(where, weights, *refs):
    (fars, total, out, vector), operands = refs[-4:], refs[:-4]
    groups = fars.shape[0]
    chips = (len(operands) - groups) // 2
    nears, pieces = operands[:groups], operands[groups:]
    rows, number = vector.shape[0] // 2, pl.program_id(0)
    part = rows // groups

    @pl.when(number == 0)
    def _():
        out[...] = total[...]

    @pl.when(where[1] == 0)
    def _():
        here = pl.ds(pl.multiple_of(number * part, part), part)
        near = jnp.concatenate([p[here, :] for p in nears], axis=0)
        far = jnp.concatenate([fars[j, here, :] for j in range(groups)], axis=0)
        vector[...] = ordered(where[0], near, far)

    for i in range(chips):

        @pl.when(jnp.logical_and(where[1] > 0, number == i))
        def _():
            vector[...] = ordered(where[0], pieces[2 * i][0], pieces[2 * i + 1][0])

    out[...] += product(weights[0], [vector[...]])


def part_kernel(which, source, out):
    out[...] = source[0]


def columns_kernel(where, *refs):
    fold, groups = where.shape[1] - 1, where.shape[2]
    sources, outs = refs[:fold], refs[fold:]
    part = sources[0].shape[2] // groups
    take = lambda j: jnp.concatenate([s[0, :, j * part : (j + 1) * part] for s in sources], axis=1)
    if len(outs) == 1:
        for j in range(groups):

            @pl.when(where[0, fold, 0] == j)
            def _():
                outs[0][...] = take(j)

        return
    for j in range(groups - 1):
        outs[j][...] = take(j)
    for side, out in enumerate(outs[groups - 1 :]):

        @pl.when(pl.program_id(0) == side)
        def _():
            out[...] = take(groups - 1)


def pick_kernel(which, *refs):
    sources, out = refs[:-1], refs[-1]
    groups = len(sources) - 1
    for j, source in enumerate(sources):
        chosen = which[0] == min(j, groups - 1)
        if j >= groups - 1:
            chosen = jnp.logical_and(chosen, pl.program_id(0) == j - groups + 1)

        @pl.when(chosen)
        def _():
            out[...] = source[...]


def call(kernel, where, grid, operands, specs, count, shape, cost, aliases={}, scratch=()):
    return pl.pallas_call(
        kernel,
        out_shape=[jax.ShapeDtypeStruct(shape, F32)] * count,
        grid_spec=pltpu.PrefetchScalarGridSpec(
            num_scalar_prefetch=1, grid=grid, in_specs=specs, out_specs=[all_of(shape)] * count, scratch_shapes=scratch
        ),
        input_output_aliases=aliases,
        cost_estimate=pl.CostEstimate(flops=cost[0], bytes_accessed=cost[1], transcendentals=0),
        compiler_params=pltpu.CompilerParams(dimension_semantics=("arbitrary",) * len(grid)),
    )(where, *operands)


def all_of(shape):
    return pl.BlockSpec(shape, lambda *_: (0,) * len(shape))


def on_device(lag_weights, inverse_head, excitation, history):
    groups, devices = lax.axis_size("lag"), lax.axis_size("row")
    group, at = lax.axis_index("lag"), lax.axis_index("row")
    chips = devices // 2
    chip, core = at // 2, at % 2
    lags, rows, order = lag_weights.shape
    width = history.shape[-1]
    part = rows // groups
    tile = rows * 2 * rows
    square = (rows, width)
    tie = lax.optimization_barrier

    def pairs(axis_size, mask):
        return [(i, i ^ mask) for i in range(axis_size)]

    def other_core(value):
        return lax.ppermute(value, "row", pairs(devices, 1))

    def along(value, step, sources):
        return lax.ppermute(value, "row", [(2 * i + c, 2 * (i + step) + c) for i in sources for c in (0, 1)])

    def go_up(value, hop):
        return along(value, 1, range(hop - 1, chips - 1))

    def go_down(value, hop):
        return along(value, -1, range(1, chips - hop + 1))

    def taken(z, stage):
        both = min(z, chips - 1 - z)
        if stage <= 2 * both:
            return (stage + 1) // 2, stage % 2 == 1
        return stage - both, z >= stage - both

    def by_chip(values):
        result = jnp.int32(values[0])
        for z in range(1, chips):
            result = jnp.where(chip == z, values[z], result)
        return result

    def source_of(stage):
        return by_chip([z + (-h if u else h) for z in range(chips) for h, u in [taken(z, stage)]])

    def choose(stage, ups, downs):
        found = sorted({taken(z, stage) for z in range(chips)})
        arrays = [(ups if u else downs)[h] for h, u in found]
        return lax.select_n(by_chip([found.index(taken(z, stage)) for z in range(chips)]), *arrays) if len(found) > 1 else arrays[0]

    stages = [chip] + [source_of(stage) for stage in range(1, chips)]
    xored = [chip ^ k for k in range(chips)]
    where = jnp.stack([core, group, *stages, *xored]).astype(jnp.int32)

    def weight_spec(stage, first=0):
        return pl.BlockSpec((1, rows, 2 * rows), lambda k, w: (k + first, 0, w[2 + stage]))

    def lag_spec(shift):
        return pl.BlockSpec((1, rows, width), lambda k, w: (jnp.maximum(k + shift, 0), 0, 0))

    def add_chip(totals, pieces, stage):
        count = len(pieces) // 2
        before = (STEPS - 1, *square)
        *totals, tail = pl.pallas_call(
            chip_kernel,
            out_shape=[jax.ShapeDtypeStruct(square, F32)] * STEPS + [jax.ShapeDtypeStruct(before, F32)],
            grid_spec=pltpu.PrefetchScalarGridSpec(
                num_scalar_prefetch=1,
                grid=(count, lags),
                in_specs=[pl.BlockSpec((1, rows, 2 * rows), lambda i, k, w: (k, 0, w[2 + stage + i]))]
                + [all_of(v.shape) for v in (*pieces, *totals)],
                out_specs=[all_of(square)] * STEPS + [all_of(before)],
                scratch_shapes=[pltpu.VMEM((2 * rows, lags * width), BF16)] * 2,
            ),
            input_output_aliases={2 + len(pieces) + n: n for n in range(len(totals))},
            cost_estimate=pl.CostEstimate(flops=18 * count * lags * tile * width, bytes_accessed=4 * count * lags * tile, transcendentals=0),
            compiler_params=pltpu.CompilerParams(dimension_semantics=("arbitrary", "arbitrary")),
            name="chip",
        )(where, lag_weights, *pieces, *totals)
        return totals, tail

    def add_first(total, near, far, stage):
        before = STEPS - 1
        return pl.pallas_call(
            first_kernel,
            out_shape=[jax.ShapeDtypeStruct(square, F32), jax.ShapeDtypeStruct((before, *square), F32)],
            grid_spec=pltpu.PrefetchScalarGridSpec(
                num_scalar_prefetch=1,
                grid=(lags,),
                in_specs=[weight_spec(stage), lag_spec(0), lag_spec(0), all_of(square)],
                out_specs=[all_of(square), pl.BlockSpec((1, *square), lambda k, w: (jnp.maximum(k + before - lags, 0), 0, 0))],
            ),
            input_output_aliases={4: 0},
            cost_estimate=pl.CostEstimate(flops=6 * lags * tile * width, bytes_accessed=4 * lags * tile, transcendentals=0),
            compiler_params=pltpu.CompilerParams(dimension_semantics=("arbitrary",)),
            name="first",
        )(where, lag_weights, near, far, total)

    def add_rest(one, two, near, far, stage):
        return call(
            rest_kernel, where, (lags - 1,), (lag_weights, near, near, far, far, one, two),
            [weight_spec(stage, 1), lag_spec(0), lag_spec(-1), lag_spec(0), lag_spec(-1), all_of(square), all_of(square)],
            2, square, (12 * lags * tile * width, 4 * lags * tile), {6: 0, 7: 1},
        )

    def add_entered(one, two, pieces, stage):
        count = len(pieces) // 2
        spec = pl.BlockSpec((1, rows, 2 * rows), lambda i, w: (0, 0, jnp.where(w[1] > 0, w[2 + stage + i], 0)))
        return call(
            entered_kernel, where, (count,), (lag_weights, *pieces, one, two),
            [spec] + [all_of(v.shape) for v in (*pieces, one, two)],
            2, square, (12 * count * tile * width, 4 * count * tile), {2 + len(pieces): 0, 3 + len(pieces): 1},
        )

    def add_second(total, nears, pieces, fars):
        spec = pl.BlockSpec((1, rows, 2 * rows), lambda i, w: (1, 0, w[2 + i + jnp.where(w[1] == 0, chips, 0)]))
        last = pl.BlockSpec((1, rows, width), lambda i, w: (STEPS - 2, 0, 0))
        return call(
            second_kernel, where, (chips,), (lag_weights, *nears, *pieces, fars, total),
            [spec] + [all_of(v.shape) for v in nears] + [last] * len(pieces) + [all_of(fars.shape), all_of(square)],
            1, square, (6 * rows * order * width, 4 * rows * order), {3 + len(nears) + len(pieces): 0},
            [pltpu.VMEM((2 * rows, width), F32)],
        )[0]

    slots = jnp.stack([(chip ^ k) * 2 + (core ^ h) for h in (0, 1) for k in range(chips)]).astype(jnp.int32)
    meet = devices * part

    def columns(matrix, every):
        fold = devices // 2
        numbers = jnp.tile(slots.reshape(2, fold, 1), (1, 1, groups))
        numbers = jnp.concatenate([numbers, jnp.full((2, 1, groups), group, jnp.int32)], axis=1)
        whole = pl.BlockSpec((rows, meet // 2), lambda s, w: (0, s))
        half = pl.BlockSpec((rows, meet // 2), lambda s, w: (0, 0))
        shape = lambda size: jax.ShapeDtypeStruct((rows, size), F32)
        return pl.pallas_call(
            columns_kernel,
            out_shape=[shape(meet)] * (groups - 1) + [shape(meet // 2)] * 2 if every else [shape(meet)],
            grid_spec=pltpu.PrefetchScalarGridSpec(
                num_scalar_prefetch=1,
                grid=(2,),
                in_specs=[pl.BlockSpec((1, rows, rows), lambda s, w, i=i: (0, 0, w[s, i, 0])) for i in range(fold)],
                out_specs=[whole] * (groups - 1) + [half] * 2 if every else [whole],
            ),
            cost_estimate=pl.CostEstimate(flops=0, bytes_accessed=8 * rows * order, transcendentals=0),
            compiler_params=pltpu.CompilerParams(dimension_semantics=("arbitrary",)),
            name="columns",
        )(numbers, *[matrix] * fold)

    def pick(matrices):
        spec = lambda j: pl.BlockSpec((rows, meet // 2), lambda s, w: (0, jnp.where(w[0] == j, s, 0)))
        return pl.pallas_call(
            pick_kernel,
            out_shape=jax.ShapeDtypeStruct((rows, meet), F32),
            grid_spec=pltpu.PrefetchScalarGridSpec(
                num_scalar_prefetch=1,
                grid=(2,),
                in_specs=[spec(j) for j in range(groups - 1)] + [all_of((rows, meet // 2))] * 2,
                out_specs=pl.BlockSpec((rows, meet // 2), lambda s, w: (0, s)),
            ),
            cost_estimate=pl.CostEstimate(flops=0, bytes_accessed=16 * rows * meet, transcendentals=0),
            compiler_params=pltpu.CompilerParams(dimension_semantics=("arbitrary",)),
            name="pick",
        )(group.astype(jnp.int32).reshape(1), *matrices)

    def gather_near(value):
        pieces = [value] + [lax.ppermute(value, "row", pairs(devices, 2 * k)) for k in range(1, chips)]
        return jnp.concatenate(pieces, axis=0)

    def own_part(value):
        return lax.dynamic_slice(value, (group * part, 0), (part, value.shape[1]))

    def sum_parts(value):
        result = own_part(value)
        for mask in range(1, groups):
            sent = lax.dynamic_slice(value, ((group ^ mask) * part, 0), (part, width))
            result = result + lax.ppermute(sent, "lag", pairs(groups, mask))
        return result

    def whole_rows(value):
        pieces = [value] + [lax.ppermute(value, "lag", pairs(groups, mask)) for mask in range(1, groups)]
        return jnp.concatenate([lax.select_n(group ^ i, *pieces) for i in range(groups)], axis=1)

    def enter(tail):
        return lax.ppermute(tail, "lag", [(i, i + 1) for i in range(groups - 1)])

    def multiply(matrix, mine):
        vector = jnp.concatenate([mine, other_core(mine)], axis=0)
        return jnp.dot(matrix, vector, precision=lax.Precision.HIGH)

    ups, downs = {1: go_up(history, 1)}, {1: go_down(history, 1)}
    tail = history[lags - (STEPS - 1) :]
    entered = [enter(jnp.where(group >= 0, tail, 0.0))]
    own_far = other_core(history)
    *chunks, last_near, last_far = columns(lag_weights, True)
    relayed = lax.ppermute(last_far, "lag", [(0, groups // 2)])
    sent = [lax.ppermute(chunks[j], "lag", [(0, j)]) for j in range(1, groups - 1)]
    (head_columns,) = columns(inverse_head[None], False)
    ups[1], downs[1], entered, own_far, head_columns = tie((ups[1], downs[1], entered, own_far, head_columns))
    totals = []
    for stage in range(1, chips - 1):
        next_up, next_down = go_up(ups[stage], stage + 1), go_down(downs[stage], stage + 1)
        near = choose(stage, ups, downs)
        if stage == chips - 2:
            relayed, near = tie((relayed, near))
            sent.append(lax.ppermute(relayed, "lag", [(groups // 2, groups - 1)]))
        pieces = [near, other_core(near)]
        if stage == 1:
            pieces = [history, own_far, *pieces]
        totals, tail = add_chip(totals, pieces, stage if stage > 1 else 0)
        if stage == chips - 2:
            waiting = tail
        else:
            entered.append(enter(tail))
        if stage == 1:
            last_near, tail = tie((last_near, tail))
            sent.append(lax.ppermute(last_near, "lag", [(0, groups - 1)]))
        if stage == chips - 2:
            both = [entered[0], other_core(entered[0])]
            totals = [totals[0], *add_entered(totals[1], totals[2], both, 0)]
        ups[stage + 1], downs[stage + 1] = next_up, next_down
        ups, downs, totals = tie((ups, downs, totals))
    first, one, two = totals

    near = choose(chips - 1, ups, downs)
    far = other_core(near)
    first, tail = add_first(first, near, far, chips - 1)

    right_side = own_part(excitation[0]) - sum_parts(first)
    right_side, waiting, tail, near, far, one, two = tie((right_side, waiting, tail, near, far, one, two))
    mine = gather_near(right_side)
    entered += [enter(waiting), enter(tail)]
    one, two = add_rest(one, two, near, far, chips - 1)
    mine, one, two, sent = tie((mine, one, two, sent))
    density = sum_parts(multiply(head_columns, mine))
    first_columns = pick([chunks[0], *sent])
    results = [density]

    density, first_columns, entered, one, two = tie((density, first_columns, entered, one, two))
    mine = gather_near(density)
    both += [v for piece in entered[1:] for v in (piece, other_core(piece))]
    one, two = add_entered(one, two, both[2:], 1)
    mine, one, two, both = tie((mine, one, two, both))
    right_side = own_part(excitation[1]) - sum_parts(one + multiply(first_columns, mine))

    right_side, two, old, both = tie((right_side, two, mine, both))
    mine = gather_near(right_side)
    nears = [old] + [lax.ppermute(old, "lag", [(j, 0)]) for j in range(1, groups)]
    field = call(
        part_kernel, group.astype(jnp.int32).reshape(1), (1,), (excitation,),
        [pl.BlockSpec((1, part, width), lambda i, w: (STEPS - 1, w[0], 0))], 1, (part, width), (0, 8 * part * width),
    )[0]
    mine, two, field = tie((mine, two, field))
    carried = multiply(head_columns, mine)
    density = sum_parts(carried)
    fars = other_core(jnp.stack(nears))
    results.append(density)

    density, two = tie((density, two))
    mine = gather_near(density)
    two = add_second(two, nears, both, fars)
    mine, two = tie((mine, two))
    right_side = field - sum_parts(two + multiply(first_columns, mine))

    right_side, results = tie((right_side, results))
    mine = gather_near(right_side)
    early = whole_rows(jnp.stack(results))
    mine, early = tie((mine, early))
    density = sum_parts(multiply(head_columns, mine))
    return jnp.concatenate([early, whole_rows(density[None])], axis=0)


def solution(mesh):
    placed = (P("lag", "row", None), P("row", None), P(None, "row", None), P("lag", "row", None))

    return jax.shard_map(on_device, mesh=mesh, in_specs=placed, out_specs=P(None, "row", None), check_vma=False)
```

```python
import jax
import jax.numpy as jnp
from jax import lax
from jax.experimental import pallas as pl
from jax.experimental.pallas import tpu as pltpu
from jax.sharding import PartitionSpec as P


STEPS = 3
F32 = jnp.float32
BF16 = jnp.bfloat16


def split(value):
    high = value.astype(BF16)
    return high, (value - high.astype(F32)).astype(BF16)


def dot(a, b):
    return jnp.dot(a, b, preferred_element_type=F32)


def product(weight, vectors):
    count, width = len(vectors), vectors[0].shape[1]
    wh, wl = split(weight)
    highs, lows = zip(*(split(v) for v in vectors))
    main = dot(wh, jnp.concatenate(highs + lows, axis=1))
    rest = dot(wl, jnp.concatenate(highs, axis=1) if count > 1 else highs[0])
    return main[:, : count * width] + main[:, count * width :] + rest


def ordered(core, near, far):
    return jnp.concatenate([jnp.where(core == 0, near, far), jnp.where(core == 0, far, near)], axis=0)


def chip_kernel(where, weights, *refs):
    outs, tail, high, low = refs[-STEPS - 3 : -3], *refs[-3:]
    pieces = refs[: len(refs) - STEPS - 3]
    totals = pieces[len(pieces) - STEPS :] if len(pieces) % 2 else []
    number, at = pl.program_id(0), pl.program_id(1)
    lags, rows, width = pieces[0].shape
    core = where[0]

    @pl.when(jnp.logical_and(number == 0, at == 0))
    def _():
        for n, out in enumerate(outs):
            out[...] = totals[n][...] if totals else jnp.zeros_like(out)

    count = len(pieces) // 2 - (1 if totals else 0)

    @pl.when(jnp.logical_and(number == count - 1, at == 0))
    def _():
        tail[...] = pieces[2 * count - 2][lags - tail.shape[0] :]

    for i in range(count):

        @pl.when(jnp.logical_and(number == i, at == 0))
        def _():
            for k in range(lags):
                columns = slice((lags - 1 - k) * width, (lags - k) * width)
                for piece, side in ((pieces[2 * i], core), (pieces[2 * i + 1], 1 - core)):
                    here = pl.ds(pl.multiple_of(side * rows, rows), rows)
                    high[here, columns], low[here, columns] = split(piece[k])

    for k in range(STEPS):

        @pl.when(at == k if k + 1 < STEPS else at >= k)
        def _():
            size = (k + 1) * width
            columns = pl.ds(pl.multiple_of((lags - 1 - at) * width, width), size)
            wh, wl = split(weights[0])
            h = high[:, columns]
            main = dot(wh, jnp.concatenate([h, low[:, columns]], axis=1))
            result = main[:, :size] + main[:, size:] + dot(wl, h)
            for n in range(k + 1):
                outs[n][...] += result[:, n * width : (n + 1) * width]


def first_kernel(where, weights, near, far, total, out, tail):
    @pl.when(pl.program_id(0) == 0)
    def _():
        out[...] = total[...]

    tail[...] = near[...]
    out[...] += product(weights[0], [ordered(where[0], near[0], far[0])])


def rest_kernel(where, weights, near, near_before, far, far_before, one, two, one_out, two_out):
    at = pl.program_id(0)
    width = near.shape[-1]
    now = ordered(where[0], near[0], far[0])

    @pl.when(at == 0)
    def _():
        one_out[...] = one[...] + product(weights[0], [now])
        two_out[...] = two[...]

    @pl.when(at > 0)
    def _():
        result = product(weights[0], [now, ordered(where[0], near_before[0], far_before[0])])
        one_out[...] += result[:, :width]
        two_out[...] += result[:, width:]


def entered_kernel(where, weights, *refs):
    pieces, (one, two, one_out, two_out) = refs[:-4], refs[-4:]
    number = pl.program_id(0)
    width = pieces[0].shape[2]

    @pl.when(number == 0)
    def _():
        one_out[...] = one[...]
        two_out[...] = two[...]

    for i in range(len(pieces) // 2):

        @pl.when(jnp.logical_and(where[1] > 0, number == i))
        def _():
            near, far = pieces[2 * i : 2 * i + 2]
            result = product(weights[0], [ordered(where[0], near[k], far[k]) for k in (1, 0)])
            one_out[...] += result[:, :width]
            two_out[...] += result[:, width:]


def second_kernel(where, weights, *refs):
    (fars, total, out, vector), operands = refs[-4:], refs[:-4]
    groups = fars.shape[0]
    chips = (len(operands) - groups) // 2
    nears, pieces = operands[:groups], operands[groups:]
    rows, number = vector.shape[0] // 2, pl.program_id(0)
    part = rows // groups

    @pl.when(number == 0)
    def _():
        out[...] = total[...]

    @pl.when(where[1] == 0)
    def _():
        here = pl.ds(pl.multiple_of(number * part, part), part)
        near = jnp.concatenate([p[here, :] for p in nears], axis=0)
        far = jnp.concatenate([fars[j, here, :] for j in range(groups)], axis=0)
        vector[...] = ordered(where[0], near, far)

    for i in range(chips):

        @pl.when(jnp.logical_and(where[1] > 0, number == i))
        def _():
            vector[...] = ordered(where[0], pieces[2 * i][0], pieces[2 * i + 1][0])

    out[...] += product(weights[0], [vector[...]])


def part_kernel(which, source, out):
    out[...] = source[0]


def columns_kernel(where, *refs):
    fold, groups = where.shape[1] - 1, where.shape[2]
    sources, outs = refs[:fold], refs[fold:]
    part = sources[0].shape[2] // groups
    take = lambda j: jnp.concatenate([s[0, :, j * part : (j + 1) * part] for s in sources], axis=1)
    if len(outs) == 1:
        for j in range(groups):

            @pl.when(where[0, fold, 0] == j)
            def _():
                outs[0][...] = take(j)

        return
    for j in range(groups - 1):
        outs[j][...] = take(j)
    for side, out in enumerate(outs[groups - 1 :]):

        @pl.when(pl.program_id(0) == side)
        def _():
            out[...] = take(groups - 1)


def pick_kernel(which, *refs):
    sources, out = refs[:-1], refs[-1]
    groups = len(sources) - 1
    for j, source in enumerate(sources):
        chosen = which[0] == min(j, groups - 1)
        if j >= groups - 1:
            chosen = jnp.logical_and(chosen, pl.program_id(0) == j - groups + 1)

        @pl.when(chosen)
        def _():
            out[...] = source[...]


def call(kernel, where, grid, operands, specs, count, shape, cost, aliases={}, scratch=()):
    return pl.pallas_call(
        kernel,
        out_shape=[jax.ShapeDtypeStruct(shape, F32)] * count,
        grid_spec=pltpu.PrefetchScalarGridSpec(
            num_scalar_prefetch=1, grid=grid, in_specs=specs, out_specs=[all_of(shape)] * count, scratch_shapes=scratch
        ),
        input_output_aliases=aliases,
        cost_estimate=pl.CostEstimate(flops=cost[0], bytes_accessed=cost[1], transcendentals=0),
        compiler_params=pltpu.CompilerParams(dimension_semantics=("arbitrary",) * len(grid)),
    )(where, *operands)


def all_of(shape):
    return pl.BlockSpec(shape, lambda *_: (0,) * len(shape))


def on_device(lag_weights, inverse_head, excitation, history):
    groups, devices = lax.axis_size("lag"), lax.axis_size("row")
    group, at = lax.axis_index("lag"), lax.axis_index("row")
    chips = devices // 2
    chip, core = at // 2, at % 2
    lags, rows, order = lag_weights.shape
    width = history.shape[-1]
    part = rows // groups
    tile = rows * 2 * rows
    square = (rows, width)
    tie = lax.optimization_barrier

    def pairs(axis_size, mask):
        return [(i, i ^ mask) for i in range(axis_size)]

    def other_core(value):
        return lax.ppermute(value, "row", pairs(devices, 1))

    def along(value, step, sources):
        return lax.ppermute(value, "row", [(2 * i + c, 2 * (i + step) + c) for i in sources for c in (0, 1)])

    def go_up(value, hop):
        return along(value, 1, range(hop - 1, chips - 1))

    def go_down(value, hop):
        return along(value, -1, range(1, chips - hop + 1))

    def taken(z, stage):
        both = min(z, chips - 1 - z)
        if stage <= 2 * both:
            return (stage + 1) // 2, stage % 2 == 1
        return stage - both, z >= stage - both

    def by_chip(values):
        result = jnp.int32(values[0])
        for z in range(1, chips):
            result = jnp.where(chip == z, values[z], result)
        return result

    def source_of(stage):
        return by_chip([z + (-h if u else h) for z in range(chips) for h, u in [taken(z, stage)]])

    def choose(stage, ups, downs):
        found = sorted({taken(z, stage) for z in range(chips)})
        arrays = [(ups if u else downs)[h] for h, u in found]
        return lax.select_n(by_chip([found.index(taken(z, stage)) for z in range(chips)]), *arrays) if len(found) > 1 else arrays[0]

    stages = [chip] + [source_of(stage) for stage in range(1, chips)]
    xored = [chip ^ k for k in range(chips)]
    where = jnp.stack([core, group, *stages, *xored]).astype(jnp.int32)

    def weight_spec(stage, first=0):
        return pl.BlockSpec((1, rows, 2 * rows), lambda k, w: (k + first, 0, w[2 + stage]))

    def lag_spec(shift):
        return pl.BlockSpec((1, rows, width), lambda k, w: (jnp.maximum(k + shift, 0), 0, 0))

    def add_chip(totals, pieces, stage):
        count = len(pieces) // 2
        before = (STEPS - 1, *square)
        *totals, tail = pl.pallas_call(
            chip_kernel,
            out_shape=[jax.ShapeDtypeStruct(square, F32)] * STEPS + [jax.ShapeDtypeStruct(before, F32)],
            grid_spec=pltpu.PrefetchScalarGridSpec(
                num_scalar_prefetch=1,
                grid=(count, lags),
                in_specs=[pl.BlockSpec((1, rows, 2 * rows), lambda i, k, w: (k, 0, w[2 + stage + i]))]
                + [all_of(v.shape) for v in (*pieces, *totals)],
                out_specs=[all_of(square)] * STEPS + [all_of(before)],
                scratch_shapes=[pltpu.VMEM((2 * rows, lags * width), BF16)] * 2,
            ),
            input_output_aliases={2 + len(pieces) + n: n for n in range(len(totals))},
            cost_estimate=pl.CostEstimate(flops=18 * count * lags * tile * width, bytes_accessed=4 * count * lags * tile, transcendentals=0),
            compiler_params=pltpu.CompilerParams(dimension_semantics=("arbitrary", "arbitrary")),
            name="chip",
        )(where, lag_weights, *pieces, *totals)
        return totals, tail

    def add_first(total, near, far, stage):
        before = STEPS - 1
        return pl.pallas_call(
            first_kernel,
            out_shape=[jax.ShapeDtypeStruct(square, F32), jax.ShapeDtypeStruct((before, *square), F32)],
            grid_spec=pltpu.PrefetchScalarGridSpec(
                num_scalar_prefetch=1,
                grid=(lags,),
                in_specs=[weight_spec(stage), lag_spec(0), lag_spec(0), all_of(square)],
                out_specs=[all_of(square), pl.BlockSpec((1, *square), lambda k, w: (jnp.maximum(k + before - lags, 0), 0, 0))],
            ),
            input_output_aliases={4: 0},
            cost_estimate=pl.CostEstimate(flops=6 * lags * tile * width, bytes_accessed=4 * lags * tile, transcendentals=0),
            compiler_params=pltpu.CompilerParams(dimension_semantics=("arbitrary",)),
            name="first",
        )(where, lag_weights, near, far, total)

    def add_rest(one, two, near, far, stage):
        return call(
            rest_kernel, where, (lags - 1,), (lag_weights, near, near, far, far, one, two),
            [weight_spec(stage, 1), lag_spec(0), lag_spec(-1), lag_spec(0), lag_spec(-1), all_of(square), all_of(square)],
            2, square, (12 * lags * tile * width, 4 * lags * tile), {6: 0, 7: 1},
        )

    def add_entered(one, two, pieces, stage):
        count = len(pieces) // 2
        spec = pl.BlockSpec((1, rows, 2 * rows), lambda i, w: (0, 0, jnp.where(w[1] > 0, w[2 + stage + i], 0)))
        return call(
            entered_kernel, where, (count,), (lag_weights, *pieces, one, two),
            [spec] + [all_of(v.shape) for v in (*pieces, one, two)],
            2, square, (12 * count * tile * width, 4 * count * tile), {2 + len(pieces): 0, 3 + len(pieces): 1},
        )

    def add_second(total, nears, pieces, fars):
        spec = pl.BlockSpec((1, rows, 2 * rows), lambda i, w: (1, 0, w[2 + i + jnp.where(w[1] == 0, chips, 0)]))
        last = pl.BlockSpec((1, rows, width), lambda i, w: (STEPS - 2, 0, 0))
        return call(
            second_kernel, where, (chips,), (lag_weights, *nears, *pieces, fars, total),
            [spec] + [all_of(v.shape) for v in nears] + [last] * len(pieces) + [all_of(fars.shape), all_of(square)],
            1, square, (6 * rows * order * width, 4 * rows * order), {3 + len(nears) + len(pieces): 0},
            [pltpu.VMEM((2 * rows, width), F32)],
        )[0]

    slots = jnp.stack([(chip ^ k) * 2 + (core ^ h) for h in (0, 1) for k in range(chips)]).astype(jnp.int32)
    meet = devices * part

    def columns(matrix, every):
        fold = devices // 2
        numbers = jnp.tile(slots.reshape(2, fold, 1), (1, 1, groups))
        numbers = jnp.concatenate([numbers, jnp.full((2, 1, groups), group, jnp.int32)], axis=1)
        whole = pl.BlockSpec((rows, meet // 2), lambda s, w: (0, s))
        half = pl.BlockSpec((rows, meet // 2), lambda s, w: (0, 0))
        shape = lambda size: jax.ShapeDtypeStruct((rows, size), F32)
        return pl.pallas_call(
            columns_kernel,
            out_shape=[shape(meet)] * (groups - 1) + [shape(meet // 2)] * 2 if every else [shape(meet)],
            grid_spec=pltpu.PrefetchScalarGridSpec(
                num_scalar_prefetch=1,
                grid=(2,),
                in_specs=[pl.BlockSpec((1, rows, rows), lambda s, w, i=i: (0, 0, w[s, i, 0])) for i in range(fold)],
                out_specs=[whole] * (groups - 1) + [half] * 2 if every else [whole],
            ),
            cost_estimate=pl.CostEstimate(flops=0, bytes_accessed=8 * rows * order, transcendentals=0),
            compiler_params=pltpu.CompilerParams(dimension_semantics=("arbitrary",)),
            name="columns",
        )(numbers, *[matrix] * fold)

    def pick(matrices):
        spec = lambda j: pl.BlockSpec((rows, meet // 2), lambda s, w: (0, jnp.where(w[0] == j, s, 0)))
        return pl.pallas_call(
            pick_kernel,
            out_shape=jax.ShapeDtypeStruct((rows, meet), F32),
            grid_spec=pltpu.PrefetchScalarGridSpec(
                num_scalar_prefetch=1,
                grid=(2,),
                in_specs=[spec(j) for j in range(groups - 1)] + [all_of((rows, meet // 2))] * 2,
                out_specs=pl.BlockSpec((rows, meet // 2), lambda s, w: (0, s)),
            ),
            cost_estimate=pl.CostEstimate(flops=0, bytes_accessed=16 * rows * meet, transcendentals=0),
            compiler_params=pltpu.CompilerParams(dimension_semantics=("arbitrary",)),
            name="pick",
        )(group.astype(jnp.int32).reshape(1), *matrices)

    def gather_near(value):
        pieces = [value] + [lax.ppermute(value, "row", pairs(devices, 2 * k)) for k in range(1, chips)]
        return jnp.concatenate(pieces, axis=0)

    def own_part(value):
        return lax.dynamic_slice(value, (group * part, 0), (part, value.shape[1]))

    def sum_parts(value):
        result = own_part(value)
        for mask in range(1, groups):
            sent = lax.dynamic_slice(value, ((group ^ mask) * part, 0), (part, width))
            result = result + lax.ppermute(sent, "lag", pairs(groups, mask))
        return result

    def whole_rows(value):
        pieces = [value] + [lax.ppermute(value, "lag", pairs(groups, mask)) for mask in range(1, groups)]
        return jnp.concatenate([lax.select_n(group ^ i, *pieces) for i in range(groups)], axis=1)

    def enter(tail):
        return lax.ppermute(tail, "lag", [(i, i + 1) for i in range(groups - 1)])

    def field_part(step):
        return call(
            part_kernel, group.astype(jnp.int32).reshape(1), (1,), (excitation,),
            [pl.BlockSpec((1, part, width), lambda i, w: (step, w[0], 0))], 1, (part, width), (0, 8 * part * width),
        )[0]

    def multiply(matrix, mine):
        vector = jnp.concatenate([mine, other_core(mine)], axis=0)
        return jnp.dot(matrix, vector, precision=lax.Precision.HIGH)

    ups, downs = {1: go_up(history, 1)}, {1: go_down(history, 1)}
    tail = history[lags - (STEPS - 1) :]
    entered = [enter(jnp.where(group >= 0, tail, 0.0))]
    own_far = other_core(history)
    *chunks, last_near, last_far = columns(lag_weights, True)
    relayed = lax.ppermute(last_far, "lag", [(0, groups // 2)])
    sent = [lax.ppermute(chunks[j], "lag", [(0, j)]) for j in range(1, groups - 1)]
    (head_columns,) = columns(inverse_head[None], False)
    ups[1], downs[1], entered, own_far, head_columns = tie((ups[1], downs[1], entered, own_far, head_columns))
    totals = []
    for stage in range(1, chips - 1):
        next_up, next_down = go_up(ups[stage], stage + 1), go_down(downs[stage], stage + 1)
        near = choose(stage, ups, downs)
        if stage == chips - 2:
            relayed, near = tie((relayed, near))
            sent.append(lax.ppermute(relayed, "lag", [(groups // 2, groups - 1)]))
        pieces = [near, other_core(near)]
        if stage == 1:
            pieces = [history, own_far, *pieces]
        totals, tail = add_chip(totals, pieces, stage if stage > 1 else 0)
        if stage == chips - 2:
            waiting = tail
        else:
            entered.append(enter(tail))
        if stage == 1:
            last_near, tail = tie((last_near, tail))
            sent.append(lax.ppermute(last_near, "lag", [(0, groups - 1)]))
        if stage == chips - 2:
            both = [entered[0], other_core(entered[0])]
            totals = [totals[0], *add_entered(totals[1], totals[2], both, 0)]
        ups[stage + 1], downs[stage + 1] = next_up, next_down
        ups, downs, totals = tie((ups, downs, totals))
    first, one, two = totals

    near = choose(chips - 1, ups, downs)
    far = other_core(near)
    first, tail = add_first(first, near, far, chips - 1)

    entered.append(enter(waiting))
    field = field_part(0)
    right_side = field - sum_parts(first)
    right_side, tail, near, far, one, two = tie((right_side, tail, near, far, one, two))
    mine = gather_near(right_side)
    entered.append(enter(tail))
    one, two = add_rest(one, two, near, far, chips - 1)
    mine, one, two, sent = tie((mine, one, two, sent))
    density = sum_parts(multiply(head_columns, mine))
    first_columns = pick([chunks[0], *sent])
    results = [density]

    density, first_columns, entered, one, two = tie((density, first_columns, entered, one, two))
    mine = gather_near(density)
    both += [v for piece in entered[1:] for v in (piece, other_core(piece))]
    one, two = add_entered(one, two, both[2:], 1)
    mine, one, two, both = tie((mine, one, two, both))
    right_side = own_part(excitation[1]) - sum_parts(one + multiply(first_columns, mine))

    right_side, two, old, both = tie((right_side, two, mine, both))
    mine = gather_near(right_side)
    nears = [old] + [lax.ppermute(old, "lag", [(j, 0)]) for j in range(1, groups)]
    field = field_part(2)
    mine, two, field = tie((mine, two, field))
    carried = multiply(head_columns, mine)
    density = sum_parts(carried)
    fars = other_core(jnp.stack(nears))
    results.append(density)

    density, two = tie((density, two))
    mine = gather_near(density)
    two = add_second(two, nears, both, fars)
    mine, two = tie((mine, two))
    right_side = field - sum_parts(two + multiply(first_columns, mine))

    right_side, results = tie((right_side, results))
    mine = gather_near(right_side)
    early = whole_rows(jnp.stack(results))
    mine, early = tie((mine, early))
    density = sum_parts(multiply(head_columns, mine))
    return jnp.concatenate([early, whole_rows(density[None])], axis=0)


def solution(mesh):
    placed = (P("lag", "row", None), P("row", None), P(None, "row", None), P("lag", "row", None))

    return jax.shard_map(on_device, mesh=mesh, in_specs=placed, out_specs=P(None, "row", None), check_vma=False)
```

```python
import jax
import jax.numpy as jnp
from jax import lax
from jax.experimental import pallas as pl
from jax.experimental.pallas import tpu as pltpu
from jax.sharding import PartitionSpec as P


STEPS = 3
F32 = jnp.float32
BF16 = jnp.bfloat16


def split(value):
    high = value.astype(BF16)
    return high, (value - high.astype(F32)).astype(BF16)


def dot(a, b):
    return jnp.dot(a, b, preferred_element_type=F32)


def product(weight, vectors):
    count, width = len(vectors), vectors[0].shape[1]
    wh, wl = split(weight)
    highs, lows = zip(*(split(v) for v in vectors))
    main = dot(wh, jnp.concatenate(highs + lows, axis=1))
    rest = dot(wl, jnp.concatenate(highs, axis=1) if count > 1 else highs[0])
    return main[:, : count * width] + main[:, count * width :] + rest


def ordered(core, near, far):
    return jnp.concatenate([jnp.where(core == 0, near, far), jnp.where(core == 0, far, near)], axis=0)


def chip_kernel(where, weights, *refs):
    outs, tail, high, low = refs[-STEPS - 3 : -3], *refs[-3:]
    pieces = refs[: len(refs) - STEPS - 3]
    totals = pieces[len(pieces) - STEPS :] if len(pieces) % 2 else []
    number, at = pl.program_id(0), pl.program_id(1)
    lags, rows, width = pieces[0].shape
    core = where[0]

    @pl.when(jnp.logical_and(number == 0, at == 0))
    def _():
        for n, out in enumerate(outs):
            out[...] = totals[n][...] if totals else jnp.zeros_like(out)

    count = len(pieces) // 2 - (1 if totals else 0)

    @pl.when(jnp.logical_and(number == count - 1, at == 0))
    def _():
        tail[...] = pieces[2 * count - 2][lags - tail.shape[0] :]

    for i in range(count):

        @pl.when(jnp.logical_and(number == i, at == 0))
        def _():
            for k in range(lags):
                columns = slice((lags - 1 - k) * width, (lags - k) * width)
                for piece, side in ((pieces[2 * i], core), (pieces[2 * i + 1], 1 - core)):
                    here = pl.ds(pl.multiple_of(side * rows, rows), rows)
                    high[here, columns], low[here, columns] = split(piece[k])

    for k in range(STEPS):

        @pl.when(at == k if k + 1 < STEPS else at >= k)
        def _():
            size = (k + 1) * width
            columns = pl.ds(pl.multiple_of((lags - 1 - at) * width, width), size)
            wh, wl = split(weights[0])
            h = high[:, columns]
            main = dot(wh, jnp.concatenate([h, low[:, columns]], axis=1))
            result = main[:, :size] + main[:, size:] + dot(wl, h)
            for n in range(k + 1):
                outs[n][...] += result[:, n * width : (n + 1) * width]


def first_kernel(where, weights, near, far, total, out, tail):
    @pl.when(pl.program_id(0) == 0)
    def _():
        out[...] = total[...]

    tail[...] = near[...]
    out[...] += product(weights[0], [ordered(where[0], near[0], far[0])])


def rest_kernel(where, weights, near, near_before, far, far_before, one, two, one_out, two_out):
    at = pl.program_id(0)
    width = near.shape[-1]
    now = ordered(where[0], near[0], far[0])

    @pl.when(at == 0)
    def _():
        one_out[...] = one[...] + product(weights[0], [now])
        two_out[...] = two[...]

    @pl.when(at > 0)
    def _():
        result = product(weights[0], [now, ordered(where[0], near_before[0], far_before[0])])
        one_out[...] += result[:, :width]
        two_out[...] += result[:, width:]


def entered_kernel(where, weights, *refs):
    pieces, (one, two, one_out, two_out) = refs[:-4], refs[-4:]
    number = pl.program_id(0)
    width = pieces[0].shape[2]

    @pl.when(number == 0)
    def _():
        one_out[...] = one[...]
        two_out[...] = two[...]

    for i in range(len(pieces) // 2):

        @pl.when(jnp.logical_and(where[1] > 0, number == i))
        def _():
            near, far = pieces[2 * i : 2 * i + 2]
            result = product(weights[0], [ordered(where[0], near[k], far[k]) for k in (1, 0)])
            one_out[...] += result[:, :width]
            two_out[...] += result[:, width:]


def second_kernel(where, weights, *refs):
    (fars, total, out, vector), operands = refs[-4:], refs[:-4]
    groups = fars.shape[0]
    chips = (len(operands) - groups) // 2
    nears, pieces = operands[:groups], operands[groups:]
    rows, number = vector.shape[0] // 2, pl.program_id(0)
    part = rows // groups

    @pl.when(number == 0)
    def _():
        out[...] = total[...]

    @pl.when(where[1] == 0)
    def _():
        here = pl.ds(pl.multiple_of(number * part, part), part)
        near = jnp.concatenate([p[here, :] for p in nears], axis=0)
        far = jnp.concatenate([fars[j, here, :] for j in range(groups)], axis=0)
        vector[...] = ordered(where[0], near, far)

    for i in range(chips):

        @pl.when(jnp.logical_and(where[1] > 0, number == i))
        def _():
            vector[...] = ordered(where[0], pieces[2 * i][0], pieces[2 * i + 1][0])

    out[...] += product(weights[0], [vector[...]])


def part_kernel(which, source, out):
    out[...] = source[0]


def columns_kernel(where, *refs):
    fold, groups = where.shape[1] - 1, where.shape[2]
    sources, outs = refs[:fold], refs[fold:]
    part = sources[0].shape[2] // groups
    take = lambda j: jnp.concatenate([s[0, :, j * part : (j + 1) * part] for s in sources], axis=1)
    if len(outs) == 1 and sources[0].shape[2] * fold == outs[0].shape[1]:
        outs[0][...] = jnp.concatenate([s[0] for s in sources], axis=1)
        return
    if len(outs) == 1:
        for j in range(groups):

            @pl.when(where[0, fold, 0] == j)
            def _():
                outs[0][...] = take(j)

        return
    for j in range(groups - 1):
        outs[j][...] = take(j)
    for side, out in enumerate(outs[groups - 1 :]):

        @pl.when(pl.program_id(0) == side)
        def _():
            out[...] = take(groups - 1)


def pick_kernel(which, *refs):
    sources, out = refs[:-1], refs[-1]
    groups = len(sources) - 1
    for j, source in enumerate(sources):
        chosen = which[0] == min(j, groups - 1)
        if j >= groups - 1:
            chosen = jnp.logical_and(chosen, pl.program_id(0) == j - groups + 1)

        @pl.when(chosen)
        def _():
            out[...] = source[...]


def call(kernel, where, grid, operands, specs, count, shape, cost, aliases={}, scratch=()):
    return pl.pallas_call(
        kernel,
        out_shape=[jax.ShapeDtypeStruct(shape, F32)] * count,
        grid_spec=pltpu.PrefetchScalarGridSpec(
            num_scalar_prefetch=1, grid=grid, in_specs=specs, out_specs=[all_of(shape)] * count, scratch_shapes=scratch
        ),
        input_output_aliases=aliases,
        cost_estimate=pl.CostEstimate(flops=cost[0], bytes_accessed=cost[1], transcendentals=0),
        compiler_params=pltpu.CompilerParams(dimension_semantics=("arbitrary",) * len(grid)),
    )(where, *operands)


def all_of(shape):
    return pl.BlockSpec(shape, lambda *_: (0,) * len(shape))


def on_device(lag_weights, inverse_head, excitation, history):
    groups, devices = lax.axis_size("lag"), lax.axis_size("row")
    group, at = lax.axis_index("lag"), lax.axis_index("row")
    chips = devices // 2
    chip, core = at // 2, at % 2
    lags, rows, order = lag_weights.shape
    width = history.shape[-1]
    part = rows // groups
    tile = rows * 2 * rows
    square = (rows, width)
    tie = lax.optimization_barrier

    def pairs(axis_size, mask):
        return [(i, i ^ mask) for i in range(axis_size)]

    def other_core(value):
        return lax.ppermute(value, "row", pairs(devices, 1))

    def along(value, step, sources):
        return lax.ppermute(value, "row", [(2 * i + c, 2 * (i + step) + c) for i in sources for c in (0, 1)])

    def go_up(value, hop):
        return along(value, 1, range(hop - 1, chips - 1))

    def go_down(value, hop):
        return along(value, -1, range(1, chips - hop + 1))

    def taken(z, stage):
        both = min(z, chips - 1 - z)
        if stage <= 2 * both:
            return (stage + 1) // 2, stage % 2 == 1
        return stage - both, z >= stage - both

    def by_chip(values):
        result = jnp.int32(values[0])
        for z in range(1, chips):
            result = jnp.where(chip == z, values[z], result)
        return result

    def source_of(stage):
        return by_chip([z + (-h if u else h) for z in range(chips) for h, u in [taken(z, stage)]])

    def choose(stage, ups, downs):
        found = sorted({taken(z, stage) for z in range(chips)})
        arrays = [(ups if u else downs)[h] for h, u in found]
        return lax.select_n(by_chip([found.index(taken(z, stage)) for z in range(chips)]), *arrays) if len(found) > 1 else arrays[0]

    stages = [chip] + [source_of(stage) for stage in range(1, chips)]
    xored = [chip ^ k for k in range(chips)]
    where = jnp.stack([core, group, *stages, *xored]).astype(jnp.int32)

    def weight_spec(stage, first=0):
        return pl.BlockSpec((1, rows, 2 * rows), lambda k, w: (k + first, 0, w[2 + stage]))

    def lag_spec(shift):
        return pl.BlockSpec((1, rows, width), lambda k, w: (jnp.maximum(k + shift, 0), 0, 0))

    def add_chip(totals, pieces, stage):
        count = len(pieces) // 2
        before = (STEPS - 1, *square)
        *totals, tail = pl.pallas_call(
            chip_kernel,
            out_shape=[jax.ShapeDtypeStruct(square, F32)] * STEPS + [jax.ShapeDtypeStruct(before, F32)],
            grid_spec=pltpu.PrefetchScalarGridSpec(
                num_scalar_prefetch=1,
                grid=(count, lags),
                in_specs=[pl.BlockSpec((1, rows, 2 * rows), lambda i, k, w: (k, 0, w[2 + stage + i]))]
                + [all_of(v.shape) for v in (*pieces, *totals)],
                out_specs=[all_of(square)] * STEPS + [all_of(before)],
                scratch_shapes=[pltpu.VMEM((2 * rows, lags * width), BF16)] * 2,
            ),
            input_output_aliases={2 + len(pieces) + n: n for n in range(len(totals))},
            cost_estimate=pl.CostEstimate(flops=18 * count * lags * tile * width, bytes_accessed=4 * count * lags * tile, transcendentals=0),
            compiler_params=pltpu.CompilerParams(dimension_semantics=("arbitrary", "arbitrary")),
            name="chip",
        )(where, lag_weights, *pieces, *totals)
        return totals, tail

    def add_first(total, near, far, stage):
        before = STEPS - 1
        return pl.pallas_call(
            first_kernel,
            out_shape=[jax.ShapeDtypeStruct(square, F32), jax.ShapeDtypeStruct((before, *square), F32)],
            grid_spec=pltpu.PrefetchScalarGridSpec(
                num_scalar_prefetch=1,
                grid=(lags,),
                in_specs=[weight_spec(stage), lag_spec(0), lag_spec(0), all_of(square)],
                out_specs=[all_of(square), pl.BlockSpec((1, *square), lambda k, w: (jnp.maximum(k + before - lags, 0), 0, 0))],
            ),
            input_output_aliases={4: 0},
            cost_estimate=pl.CostEstimate(flops=6 * lags * tile * width, bytes_accessed=4 * lags * tile, transcendentals=0),
            compiler_params=pltpu.CompilerParams(dimension_semantics=("arbitrary",)),
            name="first",
        )(where, lag_weights, near, far, total)

    def add_rest(one, two, near, far, stage):
        return call(
            rest_kernel, where, (lags - 1,), (lag_weights, near, near, far, far, one, two),
            [weight_spec(stage, 1), lag_spec(0), lag_spec(-1), lag_spec(0), lag_spec(-1), all_of(square), all_of(square)],
            2, square, (12 * lags * tile * width, 4 * lags * tile), {6: 0, 7: 1},
        )

    def add_entered(one, two, pieces, stage):
        count = len(pieces) // 2
        spec = pl.BlockSpec((1, rows, 2 * rows), lambda i, w: (0, 0, jnp.where(w[1] > 0, w[2 + stage + i], 0)))
        return call(
            entered_kernel, where, (count,), (lag_weights, *pieces, one, two),
            [spec] + [all_of(v.shape) for v in (*pieces, one, two)],
            2, square, (12 * count * tile * width, 4 * count * tile), {2 + len(pieces): 0, 3 + len(pieces): 1},
        )

    def add_second(total, nears, pieces, fars):
        spec = pl.BlockSpec((1, rows, 2 * rows), lambda i, w: (1, 0, w[2 + i + jnp.where(w[1] == 0, chips, 0)]))
        last = pl.BlockSpec((1, rows, width), lambda i, w: (STEPS - 2, 0, 0))
        return call(
            second_kernel, where, (chips,), (lag_weights, *nears, *pieces, fars, total),
            [spec] + [all_of(v.shape) for v in nears] + [last] * len(pieces) + [all_of(fars.shape), all_of(square)],
            1, square, (6 * rows * order * width, 4 * rows * order), {3 + len(nears) + len(pieces): 0},
            [pltpu.VMEM((2 * rows, width), F32)],
        )[0]

    slots = jnp.stack([(chip ^ k) * 2 + (core ^ h) for h in (0, 1) for k in range(chips)]).astype(jnp.int32)
    meet = devices * part

    def columns(matrix, every):
        fold = devices // 2
        numbers = jnp.tile(slots.reshape(2, fold, 1), (1, 1, groups))
        numbers = jnp.concatenate([numbers, jnp.full((2, 1, groups), group, jnp.int32)], axis=1)
        whole = pl.BlockSpec((rows, meet // 2), lambda s, w: (0, s))
        half = pl.BlockSpec((rows, meet // 2), lambda s, w: (0, 0))
        if every or part % 128:
            specs = [pl.BlockSpec((1, rows, rows), lambda s, w, i=i: (0, 0, w[s, i, 0])) for i in range(fold)]
        else:
            specs = [pl.BlockSpec((1, rows, part), lambda s, w, i=i: (0, 0, w[s, i, 0] * groups + w[s, fold, 0])) for i in range(fold)]
        shape = lambda size: jax.ShapeDtypeStruct((rows, size), F32)
        return pl.pallas_call(
            columns_kernel,
            out_shape=[shape(meet)] * (groups - 1) + [shape(meet // 2)] * 2 if every else [shape(meet)],
            grid_spec=pltpu.PrefetchScalarGridSpec(
                num_scalar_prefetch=1,
                grid=(2,),
                in_specs=specs,
                out_specs=[whole] * (groups - 1) + [half] * 2 if every else [whole],
            ),
            cost_estimate=pl.CostEstimate(flops=0, bytes_accessed=8 * rows * order, transcendentals=0),
            compiler_params=pltpu.CompilerParams(dimension_semantics=("arbitrary",)),
            name="columns",
        )(numbers, *[matrix] * fold)

    def pick(matrices):
        spec = lambda j: pl.BlockSpec((rows, meet // 2), lambda s, w: (0, jnp.where(w[0] == j, s, 0)))
        return pl.pallas_call(
            pick_kernel,
            out_shape=pltpu.VMEM((rows, meet), F32),
            grid_spec=pltpu.PrefetchScalarGridSpec(
                num_scalar_prefetch=1,
                grid=(2,),
                in_specs=[spec(j) for j in range(groups - 1)] + [all_of((rows, meet // 2))] * 2,
                out_specs=pl.BlockSpec((rows, meet // 2), lambda s, w: (0, s), memory_space=pltpu.VMEM),
            ),
            cost_estimate=pl.CostEstimate(flops=0, bytes_accessed=16 * rows * meet, transcendentals=0),
            compiler_params=pltpu.CompilerParams(dimension_semantics=("arbitrary",)),
            name="pick",
        )(group.astype(jnp.int32).reshape(1), *matrices)

    def gather_near(value):
        pieces = [value] + [lax.ppermute(value, "row", pairs(devices, 2 * k)) for k in range(1, chips)]
        return jnp.concatenate(pieces, axis=0)

    def own_part(value):
        return lax.dynamic_slice(value, (group * part, 0), (part, value.shape[1]))

    def sum_parts(value):
        result = own_part(value)
        for mask in range(1, groups):
            sent = lax.dynamic_slice(value, ((group ^ mask) * part, 0), (part, width))
            result = result + lax.ppermute(sent, "lag", pairs(groups, mask))
        return result

    def whole_rows(value):
        pieces = [value] + [lax.ppermute(value, "lag", pairs(groups, mask)) for mask in range(1, groups)]
        return jnp.concatenate([lax.select_n(group ^ i, *pieces) for i in range(groups)], axis=1)

    def enter(tail):
        return lax.ppermute(tail, "lag", [(i, i + 1) for i in range(groups - 1)])

    def field_part(step):
        return call(
            part_kernel, group.astype(jnp.int32).reshape(1), (1,), (excitation,),
            [pl.BlockSpec((1, part, width), lambda i, w: (step, w[0], 0))], 1, (part, width), (0, 8 * part * width),
        )[0]

    def multiply(matrix, mine):
        vector = jnp.concatenate([mine, other_core(mine)], axis=0)
        return jnp.dot(matrix, vector, precision=lax.Precision.HIGH)

    ups, downs = {1: go_up(history, 1)}, {1: go_down(history, 1)}
    tail = history[lags - (STEPS - 1) :]
    entered = [enter(jnp.where(group >= 0, tail, 0.0))]
    own_far = other_core(history)
    *chunks, last_near, last_far = columns(lag_weights, True)
    relayed = lax.ppermute(last_far, "lag", [(0, groups // 2)])
    sent = [lax.ppermute(chunks[j], "lag", [(0, j)]) for j in range(1, groups - 1)]
    (head_columns,) = columns(inverse_head[None], False)
    ups[1], downs[1], entered, own_far, head_columns = tie((ups[1], downs[1], entered, own_far, head_columns))
    totals = []
    for stage in range(1, chips - 1):
        next_up, next_down = go_up(ups[stage], stage + 1), go_down(downs[stage], stage + 1)
        near = choose(stage, ups, downs)
        if stage == chips - 2:
            relayed, near = tie((relayed, near))
            sent.append(lax.ppermute(relayed, "lag", [(groups // 2, groups - 1)]))
        pieces = [near, other_core(near)]
        if stage == 1:
            pieces = [history, own_far, *pieces]
        totals, tail = add_chip(totals, pieces, stage if stage > 1 else 0)
        if stage == chips - 2:
            waiting = tail
        else:
            entered.append(enter(tail))
        if stage == 1:
            last_near, tail = tie((last_near, tail))
            sent.append(lax.ppermute(last_near, "lag", [(0, groups - 1)]))
        if stage == chips - 2:
            both = [entered[0], other_core(entered[0])]
            totals = [totals[0], *add_entered(totals[1], totals[2], both, 0)]
        ups[stage + 1], downs[stage + 1] = next_up, next_down
        ups, downs, totals = tie((ups, downs, totals))
    first, one, two = totals

    near = choose(chips - 1, ups, downs)
    far = other_core(near)
    first, tail = add_first(first, near, far, chips - 1)

    entered.append(enter(waiting))
    field = field_part(0)
    right_side = field - sum_parts(first)
    right_side, tail, near, far, one, two = tie((right_side, tail, near, far, one, two))
    mine = gather_near(right_side)
    entered.append(enter(tail))
    one, two = add_rest(one, two, near, far, chips - 1)
    mine, one, two, sent = tie((mine, one, two, sent))
    density = sum_parts(multiply(head_columns, mine))
    first_columns = pick([chunks[0], *sent])
    results = [density]

    density, first_columns, entered, one, two = tie((density, first_columns, entered, one, two))
    mine = gather_near(density)
    both += [v for piece in entered[1:] for v in (piece, other_core(piece))]
    one, two = add_entered(one, two, both[2:], 1)
    mine, one, two, both = tie((mine, one, two, both))
    right_side = own_part(excitation[1]) - sum_parts(one + multiply(first_columns, mine))

    right_side, two, old, both = tie((right_side, two, mine, both))
    mine = gather_near(right_side)
    nears = [old] + [lax.ppermute(old, "lag", [(j, 0)]) for j in range(1, groups)]
    field = field_part(2)
    mine, two, field = tie((mine, two, field))
    carried = multiply(head_columns, mine)
    density = sum_parts(carried)
    fars = other_core(jnp.stack(nears))
    results.append(density)

    density, two = tie((density, two))
    mine = gather_near(density)
    two = add_second(two, nears, both, fars)
    mine, two = tie((mine, two))
    right_side = field - sum_parts(two + multiply(first_columns, mine))

    right_side, results = tie((right_side, results))
    mine = gather_near(right_side)
    early = whole_rows(jnp.stack(results))
    mine, early = tie((mine, early))
    density = sum_parts(multiply(head_columns, mine))
    return jnp.concatenate([early, whole_rows(density[None])], axis=0)


def solution(mesh):
    placed = (P("lag", "row", None), P("row", None), P(None, "row", None), P("lag", "row", None))

    return jax.shard_map(on_device, mesh=mesh, in_specs=placed, out_specs=P(None, "row", None), check_vma=False)
```
